512 devices in a mesh: lat: 32 (over z, x_hi, core), lon: 16 (over y, x_lo).
Axes of the slice: x: 4 (x_hi: 2, x_lo: 2; x = x_hi * 2 + x_lo), y: 8, z: 8, core: 2. Of those that a mesh axis runs over, the one named last changes fastest.
Arguments:
- latent: float32 [256, 448, 640], P('lat', 'lon'), may hold values from -6 to 6
- conv_first: float32 [25, 640], replicated, may hold values from -1.2 to 1.2
- conv_second: float32 [25, 640], replicated, may hold values from -1.2 to 1.2
- filter_gains: float32 [192, 640], P(None, 'lon'), may hold values from -4 to 4
- norm_gain: float32 [640], replicated, may hold values from 0.5 to 1.5
- up_weight: bfloat16 [640, 1280], replicated, may hold values from -0.25 to 0.25
- down_weight: bfloat16 [1280, 640], replicated, may hold values from -0.15625 to 0.15625
Outputs:
- block_out: float32 [256, 448, 640], P('lat', 'lon')
The draws below stay inside these ranges and needn't reach their ends.
All inputs are finite; a program needn't handle non-finite values.
Results may differ from the reference program's by a relative error of at most 0.0012.
Values sent between devices are 32-bit elements; how exact they have to be, the bound alone decides.
No kernel may reach another device: no remote copies, remote signals or barrier semaphores. Data moves between devices by JAX's collectives and lax.ppermute only.
A program may use at most 64 MiB of HBM per device.

```python
import jax
import jax.numpy as jnp
from jax import lax

C = 640
HIDDEN_SIZE = 1280
MODES = 192
NLAT = 256
NLON = 448


def steps_of(key, shape, pieces, low, top_value):
    def one(axis_at, blocks):
        steps = jax.random.uniform(jax.random.fold_in(jax.random.fold_in(key, 6), axis_at), (blocks,), jnp.float32, low / len(pieces), top_value / len(pieces))
        return jnp.repeat(jnp.exp(steps), shape[axis_at] // blocks).reshape((-1,) + (1,) * (len(shape) - axis_at - 1))

    gain = one(*pieces[0])
    for cut in pieces[1:]:
        gain = gain * one(*cut)
    return gain


def bell_draw(stream_key, dims, deviation, bound, pieces=(), kind=jnp.bfloat16):
    gain = steps_of(stream_key, dims, pieces, -0.22, 0.18) if pieces else 1.0
    values = jax.random.normal(stream_key, dims, jnp.float32) * deviation * gain
    return jnp.minimum(jnp.maximum(values, -bound), bound).astype(kind)


def setup_inputs(seed: int = 0) -> dict:
    key_of = jax.random.split(jax.random.key(seed), 8)
    return {
        "latent": bell_draw(key_of[0], (NLAT, NLON, C), 1.0, 6.0, ((0, 32), (1, 16)), jnp.float32),
        "conv_first": bell_draw(key_of[1], (25, C), 0.2, 1.2, (), jnp.float32),
        "conv_second": bell_draw(key_of[2], (25, C), 0.2, 1.2, (), jnp.float32),
        "filter_gains": bell_draw(key_of[3], (MODES, C), 1.0, 4.0, ((1, 16),), jnp.float32),
        "norm_gain": jnp.clip(1.0 + 0.1 * jax.random.normal(key_of[4], (C,), jnp.float32), 0.5, 1.5),
        "up_weight": bell_draw(key_of[5], (C, HIDDEN_SIZE), C ** -0.5, 0.25),
        "down_weight": bell_draw(key_of[6], (HIDDEN_SIZE, C), HIDDEN_SIZE ** -0.5, 0.15625),
    }


highest = lax.Precision.HIGHEST

def stencil_sum(padded, weights, row_count, col_count):
    stencil_total = jnp.zeros((row_count, col_count, padded.shape[2]), padded.dtype)
    for row_shift in range(5):
        for col_shift in range(5):
            stencil_total = stencil_total + weights[row_shift * 5 + col_shift] * padded[row_shift:row_shift + row_count, col_shift:col_shift + col_count, :]
    return stencil_total

def local_stencil(latent, weights):
    wrapped = jnp.concatenate([latent[:, -2:], latent, latent[:, :2]], axis=1)
    padded = jnp.pad(wrapped, ((2, 2), (0, 0), (0, 0)))
    return stencil_sum(padded, weights, latent.shape[0], latent.shape[1])

def colatitude(cell_count, float_type):
    cell_index = jnp.arange(cell_count).astype(jnp.int32).astype(float_type)
    return jnp.pi * (cell_index + 0.5) / cell_count

def legendre_table(orders, degrees, cosine, sine_theta):
    log_seed = 0.5 * (jnp.log((2.0 * orders + 1.0) / (4.0 * jnp.pi)) + jax.scipy.special.gammaln(2.0 * orders + 1.0) - 2.0 * orders * jnp.log(2.0) - 2.0 * jax.scipy.special.gammaln(orders + 1.0))
    diagonal_term = jnp.exp(log_seed[:, None] + orders[:, None] * jnp.log(sine_theta)[None, :])
    blanks = jnp.zeros_like(diagonal_term)
    legendre = jnp.zeros((orders.shape[0], degrees, sine_theta.shape[0]), diagonal_term.dtype)

    def block_step(block_index, state_tuple):
        previous, earlier, legendre = state_tuple
        values = []
        for offset in range(8):
            degree = (block_index * 8 + offset).astype(diagonal_term.dtype)
            square = degree * degree
            upper_ratio = jnp.sqrt(jnp.maximum(4.0 * square - 1.0, 1.0) / jnp.maximum(square - orders * orders, 1.0))
            below_sq = (degree - 1.0) * (degree - 1.0)
            lower_ratio = jnp.sqrt(jnp.maximum(below_sq - orders * orders, 0.0) / jnp.maximum(4.0 * below_sq - 1.0, 1.0))
            recurred = upper_ratio[:, None] * (cosine[None, :] * previous - lower_ratio[:, None] * earlier)
            current = jnp.where((degree < orders)[:, None], blanks, jnp.where((degree == orders)[:, None], diagonal_term, recurred))
            values.append(current)
            earlier = previous
            previous = current
        stacked = jnp.stack(values, axis=1)
        legendre = lax.dynamic_update_slice(legendre, stacked, (jnp.int32(0), (block_index * 8).astype(jnp.int32), jnp.int32(0)))
        return (previous, earlier, legendre)
    return lax.fori_loop(0, degrees // 8, block_step, (blanks, blanks, legendre))[2]

def fourier_tables(lon_count, mode_count, float_type):
    product_index = jnp.arange(lon_count).astype(jnp.int32)[:, None] * jnp.arange(mode_count).astype(jnp.int32)[None, :] % lon_count
    phase_grid = 2.0 * jnp.pi * product_index.astype(float_type) / lon_count
    forward = jnp.stack([jnp.cos(phase_grid), -jnp.sin(phase_grid)], axis=1) / lon_count
    factor = jnp.where(jnp.arange(mode_count).astype(jnp.int32) == 0, 1.0, 2.0).astype(float_type)
    inverse = jnp.stack([jnp.cos(phase_grid).T * factor[:, None], -jnp.sin(phase_grid).T * factor[:, None]], axis=0)
    return (forward, inverse)

def harmonic_filter(latent, filter_gains):
    lat_count, lon_count = (latent.shape[0], latent.shape[1])
    mode_count = filter_gains.shape[0]
    forward, inverse = fourier_tables(lon_count, mode_count, jnp.float32)
    colat_grid = colatitude(lat_count, jnp.float32)
    orders = jnp.arange(mode_count).astype(jnp.int32).astype(jnp.float32)
    legendre = legendre_table(orders, mode_count, jnp.cos(colat_grid), jnp.sin(colat_grid))
    quadrature = 2.0 * jnp.pi * jnp.pi * jnp.sin(colat_grid) / lat_count
    weighted = legendre * quadrature
    coeffs = jnp.einsum('inc,nrk->irkc', latent, forward, precision=highest)
    spectrum = jnp.einsum('kli,irkc->lrkc', weighted, coeffs, precision=highest)
    spectrum = spectrum * filter_gains[:, None, None, :]
    restored = jnp.einsum('kli,lrkc->irkc', legendre, spectrum, precision=highest)
    return jnp.einsum('irkc,rkn->inc', restored, inverse, precision=highest)

def channel_mlp(latent, norm_gain, up_weight, down_weight):
    average = lax.optimization_barrier(jnp.mean(latent, axis=-1, keepdims=True))
    centred = latent - average
    spread = lax.optimization_barrier(jnp.mean(centred * centred, axis=-1, keepdims=True))
    normed = (centred * lax.rsqrt(spread + 1e-05) * norm_gain).astype(jnp.bfloat16)
    hidden = jnp.dot(normed, up_weight, preferred_element_type=jnp.float32)
    active = jax.nn.gelu(hidden, approximate=True).astype(jnp.bfloat16)
    return latent + jnp.dot(active, down_weight, preferred_element_type=jnp.float32)

def reference(latent, conv_first, conv_second, filter_gains, norm_gain, up_weight, down_weight):
    after_first = latent + local_stencil(latent, conv_first)
    after_second = after_first + harmonic_filter(after_first, filter_gains)
    after_third = after_second + local_stencil(after_second, conv_second)
    return channel_mlp(after_third, norm_gain, up_weight, down_weight)
```

```python
import math

import jax
import jax.numpy as jnp
import numpy as np
from jax import lax
from jax.experimental import pallas as pl
from jax.experimental.pallas import tpu as pltpu
from jax.sharding import PartitionSpec as P

ROWS, COLS, CHANNELS, HIDDEN = 8, 28, 640, 1280
LAT, LON, SLICE = 32, 16, 40
NLAT, NLON, MODES = 256, 448, 192
OWN = MODES // LAT
KEPT = OWN + 1
LON_CHUNK = 72
LAT_CHUNK = 35
f32, bf16 = jnp.float32, jnp.bfloat16


def split_np(table):
    high = table.astype(np.float32).astype(jnp.bfloat16)
    low = (table - high.astype(np.float64)).astype(np.float32).astype(jnp.bfloat16)
    return high, low


def order_of(owner, slot):
    return owner * OWN + slot if slot < OWN else MODES + owner


def fourier_np():
    half, sector, step = np.meshgrid(np.arange(2), np.arange(LON), np.arange(16), indexing="ij")
    place = (sector * COLS + half * 14 + step).reshape(-1)
    valid = (step < 14).reshape(-1)
    forward = np.zeros((2, KEPT, LAT, 512))
    inverse = np.zeros((2, 512, 8, LAT))
    for slot in range(KEPT):
        for owner in range(LAT):
            order = order_of(owner, slot)
            angle = 2.0 * np.pi * ((order * place) % NLON) / NLON
            double = 1.0 if order == 0 else 2.0
            real, imag = np.cos(angle), -np.sin(angle)
            if order == 0:
                imag = np.cos(np.pi * (place % 2))
            forward[0, slot, owner] = real / NLON * valid
            forward[1, slot, owner] = imag / NLON * valid
            inverse[0, :, slot, owner] = real * double * valid
            inverse[1, :, slot, owner] = imag * double * valid
    return forward.reshape(2 * KEPT * LAT, 512), inverse.reshape(2, 512, 8 * LAT)


def phase_np():
    table = np.zeros((LAT, 5, 2, 3, 4))
    for owner in range(LAT):
        for slot in range(KEPT):
            order = order_of(owner, slot)
            for b in range(-2, 3):
                angle = 2.0 * np.pi * ((order * b) % NLON) / NLON
                where = (owner, b + 2, slot // 4)
                table[where + (0, slot % 4)] = np.cos(angle)
                table[where + (1, slot % 4)] = np.cos(np.pi * b) if order == 0 else np.cos(angle)
                table[where + (2, slot % 4)] = np.sin(angle)
    return table.reshape(LAT, 5, 24).astype(np.float32)


def latitude_np():
    e, q = np.meshgrid(np.arange(ROWS), np.arange(LAT), indexing="ij")
    theta = np.pi * ((q * ROWS + e).reshape(-1) + 0.5) / NLAT
    weight = 2.0 * np.pi * np.pi * np.sin(theta) / NLAT
    rows = np.stack([np.cos(theta), np.log(np.sin(theta)), weight])
    return np.concatenate([rows, np.zeros((5, NLAT))]).astype(np.float32)


def seed_np():
    seeds = np.zeros((LAT, 8, 128), np.float32)
    for m in range(MODES):
        value = 0.5 * (
            math.log((2 * m + 1) / (4 * math.pi))
            + math.lgamma(2 * m + 1)
            - 2 * m * math.log(2)
            - 2 * math.lgamma(m + 1)
        )
        seeds[m // OWN, m % OWN] = value
    return seeds


def lane_slot(width):
    return lax.broadcasted_iota(jnp.int32, (1, 128), 1) // width


def swap_blocks(values, width):
    values = list(values)
    step = len(values) // 2
    while step:
        shift = step * width
        first = lane_slot(shift) % 2 == 0
        for a in range(len(values)):
            if not a & step:
                low, high = values[a], values[a | step]
                values[a] = jnp.where(first, low, pltpu.roll(high, shift, 1))
                values[a | step] = jnp.where(first, pltpu.roll(low, 128 - shift, 1), high)
        step //= 2
    return values


def split(value):
    high = value.astype(bf16)
    return high, (value - high.astype(f32)).astype(bf16)


def dot(a, b, dims=((1,), (0,))):
    return lax.dot_general(a, b, (dims, ((), ())), preferred_element_type=f32)


def dot3(a, b, dims=((1,), (0,))):
    return dot(a[0], b[0], dims) + (dot(a[1], b[0], dims) + dot(a[0], b[1], dims))


def pack_kernel(x_ref, out_ref):
    first = lane_slot(8) % 2 == 0
    for j in range(5):
        blocks = swap_blocks([x_ref[i, :, 128 * j : 128 * j + 128] for i in range(ROWS)], 16)
        for b in range(8):
            pair, place = divmod(8 * j + b, 5)
            even, odd = 2 * pair * LON_CHUNK, (2 * pair + 1) * LON_CHUNK
            block = blocks[b]
            if place == 2:
                top, bottom = block[:14], block[14:]
                out_ref[even + 56 : even + 70] = jnp.where(first, top, pltpu.roll(bottom, 8, 1))
                out_ref[odd + 56 : odd + 70] = jnp.where(first, pltpu.roll(top, 120, 1), bottom)
                out_ref[even + 70 : even + 72] = jnp.zeros((2, 128), f32)
                out_ref[odd + 70 : odd + 72] = jnp.zeros((2, 128), f32)
            else:
                base = (even, even + 28, None, odd, odd + 28)[place]
                out_ref[base : base + 28] = block


def forward_kernel(in_ref, high_ref, low_ref, out_ref):
    totals = []
    for half in range(2):
        pieces = []
        for start in (14 * half, 28 + 14 * half, 56):
            pieces.append(
                jnp.concatenate(
                    [in_ref[LON_CHUNK * q + start : LON_CHUNK * q + start + 16] for q in range(LON)],
                    axis=0,
                )
            )
        x = split(jnp.concatenate(pieces, axis=1))
        lanes = slice(256 * half, 256 * half + 256)
        totals.append(dot3((high_ref[:, lanes], low_ref[:, lanes]), x))
    both = totals[0][:, :256] + totals[1][:, :256]
    g0, g1 = totals[0][:, 256:], totals[1][:, 256:]
    half_rows = KEPT * LAT
    first = lane_slot(8) % 2 == 0
    last = jnp.where(
        first,
        g0[:half_rows] + pltpu.roll(g1[:half_rows], 120, 1),
        pltpu.roll(g0[half_rows:], 8, 1) + g1[half_rows:],
    )
    for row in range(2 * KEPT):
        part = both[LAT * row : LAT * row + LAT]
        out_ref[pl.ds(row, LAT, stride=LAT_CHUNK), :] = part[:, :128]
        out_ref[pl.ds(14 + row, LAT, stride=LAT_CHUNK), :] = part[:, 128:]
    for row in range(KEPT):
        out_ref[pl.ds(28 + row, LAT, stride=LAT_CHUNK), :] = last[LAT * row : LAT * row + LAT]


def legendre_kernel(owner_ref, angle_ref, seed_ref, high_ref, low_ref, left_ref, right_ref):
    slot = lax.broadcasted_iota(jnp.int32, (8, 256), 0)
    order_at = jnp.where(slot < OWN, owner_ref[0] * OWN + slot, 2 * MODES)
    order = order_at.astype(f32)
    degree = lax.broadcasted_iota(jnp.int32, (8, 256), 1).astype(f32)
    square, below = degree * degree, (degree - 1.0) * (degree - 1.0)
    upper = jnp.sqrt(
        jnp.maximum(4.0 * square - 1.0, 1.0) / jnp.maximum(square - order * order, 1.0)
    )
    lower = jnp.sqrt(
        jnp.maximum(below - order * order, 0.0) / jnp.maximum(4.0 * below - 1.0, 1.0)
    )
    product = upper * lower
    cosine = jnp.broadcast_to(angle_ref[0:1, :], (8, 256))
    diagonal = jnp.exp(seed_ref[:, 0:1] + order * angle_ref[1:2, :])
    previous = jnp.zeros((8, 256), f32)
    earlier = previous
    for l in range(MODES):
        current = jnp.where(
            order_at == l,
            diagonal,
            (upper[:, l : l + 1] * cosine) * previous - product[:, l : l + 1] * earlier,
        )
        left_ref[8 * l : 8 * l + 8] = current[:, :128]
        right_ref[8 * l : 8 * l + 8] = current[:, 128:]
        previous, earlier = current, previous
    for k in range(OWN):
        for part, source in enumerate((left_ref, right_ref)):
            high, low = split(source[pl.ds(k, MODES, stride=8), :])
            high_ref[k, :, 128 * part : 128 * part + 128] = high
            low_ref[k, :, 128 * part : 128 * part + 128] = low


def spectral_kernel(in_ref, high_ref, low_ref, taps_ref, gain_ref, angle_ref, out_ref, u_ref, v_ref, f_ref):
    lane = lax.broadcasted_iota(jnp.int32, (1, 128), 1) % LAT

    def fill_edges(ref):
        for part in range(2):
            for group in range(2):
                for e in (0, 1):
                    block = pltpu.roll(ref[part, group, 2 + e], 127, 1)
                    ref[part, group, 10 + e] = jnp.where(lane == LAT - 1, 0.0, block)
                    block = pltpu.roll(ref[part, group, 8 + e], 1, 1)
                    ref[part, group, e] = jnp.where(lane == 0, 0.0, block)

    def stencil(ref, which, store):
        for group in range(2):
            for tile in range(5):
                rows = slice(8 * tile, 8 * tile + 8)
                taps = []
                for a in range(5):
                    base = (which * 5 + a) * SLICE + 8 * tile
                    taps.append(
                        [
                            taps_ref[base : base + 8, (group * 3 + kind) * 128 : (group * 3 + kind) * 128 + 128]
                            for kind in range(3)
                        ]
                    )
                real = [ref[0, group, e, rows] for e in range(12)]
                imag = [ref[1, group, e, rows] for e in range(12)]
                for e in range(ROWS):
                    total_r, total_i = real[e + 2], imag[e + 2]
                    for a in range(5):
                        r_tap, s_tap, i_tap = taps[a]
                        total_r = total_r + (r_tap * real[e + a] - i_tap * imag[e + a])
                        total_i = total_i + (s_tap * imag[e + a] + i_tap * real[e + a])
                    store(group, rows, e, total_r, total_i)

    def rows_of(start, count):
        pieces = [in_ref[pl.ds(start + n, LAT, stride=LAT_CHUNK), :] for n in range(count)]
        if count < 4:
            pieces.append(jnp.zeros((LAT * (4 - count), 128), f32))
        return jnp.concatenate(pieces, axis=0).T

    for group in range(2):
        count = min(4, KEPT - 4 * group)
        for tile in range(2):
            for part in range(2):
                block = rows_of(14 * tile + KEPT * part + 4 * group, count)
                for e in range(ROWS):
                    u_ref[part, group, 2 + e, 16 * tile : 16 * tile + 16] = block[16 * e : 16 * e + 16]
        block = rows_of(28 + 4 * group, count)
        for e in range(ROWS):
            for part in range(2):
                start = 16 * e + 8 * part
                u_ref[part, group, 2 + e, 32:40] = block[start : start + 8]
    fill_edges(u_ref)

    def keep_first(group, rows, e, total_r, total_i):
        v_ref[0, group, 2 + e, rows] = total_r
        v_ref[1, group, 2 + e, rows] = total_i

    stencil(u_ref, 0, keep_first)

    weight = angle_ref[2:3, :]
    for part in range(2):
        for group in range(2):
            halves = [
                swap_blocks([v_ref[part, group, 2 + 4 * j + e] for e in range(4)], 32) for j in range(2)
            ]
            for n in range(4):
                if 4 * group + n < OWN:
                    f_ref[4 * group + n, SLICE * part : SLICE * part + SLICE] = (
                        jnp.concatenate([halves[0][n], halves[1][n]], axis=1) * weight
                    )
    for k in range(OWN):
        table = (high_ref[k], low_ref[k])
        spectrum = dot3(split(f_ref[k]), table, ((1,), (1,)))
        gain = gain_ref[80:160] if k == 0 else gain_ref[0:80]
        f_ref[k] = dot3(split(spectrum * gain), table)
    for part in range(2):
        for group in range(2):
            rows = slice(SLICE * part, SLICE * part + SLICE)
            for j in range(2):
                values = [
                    f_ref[4 * group + n, rows, 128 * j : 128 * j + 128]
                    if 4 * group + n < OWN
                    else jnp.zeros((SLICE, 128), f32)
                    for n in range(4)
                ]
                for e, value in enumerate(swap_blocks(values, 32)):
                    v_ref[part, group, 2 + 4 * j + e] = v_ref[part, group, 2 + 4 * j + e] + value
    fill_edges(v_ref)

    def keep_second(group, rows, e, total_r, total_i):
        u_ref[0, group, 2 + e, rows] = total_r
        u_ref[1, group, 2 + e, rows] = total_i

    stencil(v_ref, 1, keep_second)

    def give(start, count, pieces):
        block = jnp.concatenate(pieces, axis=0).T
        for n in range(count):
            out_ref[pl.ds(start + n, LAT, stride=LAT_CHUNK), :] = block[LAT * n : LAT * n + LAT]

    for group in range(2):
        count = min(4, KEPT - 4 * group)
        for tile in range(2):
            for part in range(2):
                give(
                    14 * tile + KEPT * part + 4 * group,
                    count,
                    [u_ref[part, group, 2 + e, 16 * tile : 16 * tile + 16] for e in range(ROWS)],
                )
        give(
            28 + 4 * group,
            count,
            [u_ref[part, group, 2 + e, 32:40] for e in range(ROWS) for part in range(2)],
        )


def inverse_kernel(in_ref, high_ref, low_ref, out_ref):
    totals = []
    for part in range(2):
        columns = []
        for start in (KEPT * part, 14 + KEPT * part, 28):
            pieces = [in_ref[pl.ds(start + k, LAT, stride=LAT_CHUNK), :] for k in range(KEPT)]
            columns.append(jnp.concatenate(pieces + [jnp.zeros((LAT, 128), f32)], axis=0))
        x = split(jnp.concatenate(columns, axis=1))
        totals.append(dot3((high_ref[part], low_ref[part]), x))
    both = totals[0][:, :256] + totals[1][:, :256]
    g0, g1 = totals[0][:, 256:], totals[1][:, 256:]
    first = lane_slot(8) % 2 == 0
    last = jnp.where(
        first,
        g0[:256] + pltpu.roll(g1[:256], 120, 1),
        pltpu.roll(g0[256:], 8, 1) + g1[256:],
    )
    for q in range(LON):
        base = LON_CHUNK * q
        for tile in range(2):
            for half in range(2):
                row = 256 * half + 16 * q
                start = base + 28 * tile + 14 * half
                out_ref[start : start + 14] = both[row : row + 14, 128 * tile : 128 * tile + 128]
        out_ref[base + 56 : base + 72] = last[16 * q : 16 * q + 16]


def mlp_kernel(in_ref, gain_ref, up_ref, down_ref, out_ref, x_ref):
    first = lane_slot(8) % 2 == 0
    for j in range(5):
        blocks = []
        for b in range(8):
            pair, place = divmod(8 * j + b, 5)
            even, odd = 2 * pair * LON_CHUNK, (2 * pair + 1) * LON_CHUNK
            if place == 2:
                e, o = in_ref[even + 56 : even + 70], in_ref[odd + 56 : odd + 70]
                top = jnp.where(first, e, pltpu.roll(o, 8, 1))
                bottom = jnp.where(first, pltpu.roll(e, 120, 1), o)
                blocks.append(jnp.concatenate([top, bottom], axis=0))
            else:
                base = (even, even + 28, None, odd, odd + 28)[place]
                blocks.append(in_ref[base : base + 28])
        for i, value in enumerate(swap_blocks(blocks, 16)):
            x_ref[i, 0:28, 128 * j : 128 * j + 128] = value
    x_ref[:, 28:32, :] = jnp.zeros((ROWS, 4, CHANNELS), f32)
    x = x_ref[...].reshape(ROWS * 32, CHANNELS)
    average = jnp.mean(x, axis=-1, keepdims=True)
    centred = x - average
    spread = jnp.mean(centred * centred, axis=-1, keepdims=True)
    normed = (centred * lax.rsqrt(spread + 1e-05) * gain_ref[...]).astype(bf16)
    total = x
    for n in range(5):
        cut = slice(256 * n, 256 * n + 256)
        hidden = dot(normed, up_ref[:, cut])
        active = jax.nn.gelu(hidden, approximate=True).astype(bf16)
        total = total + dot(active, down_ref[cut, :])
    for i in range(ROWS):
        out_ref[i] = total[32 * i : 32 * i + 28]


def vmem(count):
    return [pl.BlockSpec(memory_space=pltpu.VMEM)] * count


def run(kernel, shape, *operands, scratch=(), cost=(0, 0)):
    return pl.pallas_call(
        kernel,
        out_shape=jax.ShapeDtypeStruct(shape, f32),
        in_specs=vmem(len(operands)),
        out_specs=pl.BlockSpec(memory_space=pltpu.VMEM),
        scratch_shapes=list(scratch),
        cost_estimate=pl.CostEstimate(flops=cost[0], bytes_accessed=cost[1], transcendentals=0),
    )(*operands)


def legendre(owner, angles, seeds):
    table = jax.ShapeDtypeStruct((OWN, MODES, NLAT), bf16)
    return pl.pallas_call(
        legendre_kernel,
        out_shape=(table, table),
        in_specs=[pl.BlockSpec(memory_space=pltpu.SMEM)] + vmem(2),
        out_specs=vmem(2),
        scratch_shapes=[pltpu.VMEM((8 * MODES, 128), f32)] * 2,
        cost_estimate=pl.CostEstimate(flops=10**7, bytes_accessed=10**7, transcendentals=0),
    )(owner, angles, seeds)


def own_channels(array, axis, start, odd):
    part = lax.dynamic_slice_in_dim(array, start, SLICE, axis)
    return jnp.where(odd, jnp.roll(part, -8, axis), part)


def exchange(array, axis, count):
    rows = array.shape[0] // count
    shape = (count, rows, 128) if rows % 8 == 0 else (count, 1, rows * 128)
    moved = lax.all_to_all(array.reshape(shape), axis, split_axis=0, concat_axis=0, tiled=True)
    return moved.reshape(array.shape)


def per_device(latent, conv_first, conv_second, filter_gains, norm_gain, up_weight, down_weight):
    band = lax.axis_index("lat")
    sector = lax.axis_index("lon")
    odd = sector % 2 == 1
    forward, inverse = fourier_np()
    forward, inverse = split_np(forward), split_np(inverse)
    angles = jnp.asarray(latitude_np())

    packed = run(pack_kernel, (LON * LON_CHUNK, 128), latent)
    circles = exchange(packed, "lon", LON)

    seeds = lax.dynamic_index_in_dim(jnp.asarray(seed_np()), band, 0, False)
    high, low = legendre(band.astype(jnp.int32).reshape(1), angles, seeds)
    phases = lax.dynamic_index_in_dim(jnp.asarray(phase_np()), band, 0, False)
    spread_np = np.kron(np.eye(24, dtype=np.float32), np.ones((1, LAT), np.float32))
    taps = jnp.stack([conv_first, conv_second]).reshape(2, 5, 5, CHANNELS)
    taps = own_channels(taps, 3, sector * SLICE, odd).transpose(0, 1, 3, 2).reshape(10 * SLICE, 5)
    taps = jnp.dot(taps, phases, precision=lax.Precision.HIGHEST)
    taps = jnp.dot(taps, jnp.asarray(spread_np), precision=lax.Precision.HIGHEST)
    gains = own_channels(filter_gains, 1, 0, odd).T
    gains = jnp.concatenate([gains, gains, gains, jnp.where(band == 0, 0.0, gains)], axis=0)

    coeffs = run(forward_kernel, (LAT * LAT_CHUNK, 128), circles, *map(jnp.asarray, forward))
    orders = exchange(coeffs, "lat", LAT)
    state = pltpu.VMEM((2, 2, 12, SLICE, 128), f32)
    third = run(
        spectral_kernel,
        (LAT * LAT_CHUNK, 128),
        orders,
        high,
        low,
        taps,
        gains,
        angles,
        scratch=[state, state, pltpu.VMEM((OWN, 2 * SLICE, NLAT), f32)],
    )
    returned = exchange(third, "lat", LAT)
    restored = run(inverse_kernel, (LON * LON_CHUNK, 128), returned, *map(jnp.asarray, inverse))
    arrived = exchange(restored, "lon", LON)
    return run(
        mlp_kernel,
        (ROWS, COLS, CHANNELS),
        arrived,
        norm_gain.reshape(1, CHANNELS),
        up_weight,
        down_weight,
        scratch=[pltpu.VMEM((ROWS, 32, CHANNELS), f32)],
    )


def solution(mesh):
    return jax.shard_map(
        per_device,
        mesh=mesh,
        in_specs=(P("lat", "lon", None), P(), P(), P(None, "lon"), P(), P(), P()),
        out_specs=P("lat", "lon", None),
        check_vma=False,
    )
```

```python
import math

import jax
import jax.numpy as jnp
import numpy as np
from jax import lax
from jax.experimental import pallas as pl
from jax.experimental.pallas import tpu as pltpu
from jax.sharding import PartitionSpec as P

ROWS, COLS, CHANNELS, HIDDEN = 8, 28, 640, 1280
LAT, LON, SLICE = 32, 16, 40
NLAT, NLON, MODES = 256, 448, 192
OWN = MODES // LAT
KEPT = OWN + 1
LON_CHUNK = 72
LAT_CHUNK = 35
f32, bf16 = jnp.float32, jnp.bfloat16


def split_np(table):
    high = table.astype(np.float32).astype(jnp.bfloat16)
    low = (table - high.astype(np.float64)).astype(np.float32).astype(jnp.bfloat16)
    return high, low


def order_of(owner, slot):
    return owner * OWN + slot if slot < OWN else MODES + owner


def fourier_np():
    half, sector, step = np.meshgrid(np.arange(2), np.arange(LON), np.arange(16), indexing="ij")
    place = (sector * COLS + half * 14 + step).reshape(-1)
    valid = (step < 14).reshape(-1)
    forward = np.zeros((2, KEPT, LAT, 512))
    inverse = np.zeros((2, 512, 8, LAT))
    for slot in range(KEPT):
        for owner in range(LAT):
            order = order_of(owner, slot)
            angle = 2.0 * np.pi * ((order * place) % NLON) / NLON
            double = 1.0 if order == 0 else 2.0
            real, imag = np.cos(angle), -np.sin(angle)
            if order == 0:
                imag = np.cos(np.pi * (place % 2))
            forward[0, slot, owner] = real / NLON * valid
            forward[1, slot, owner] = imag / NLON * valid
            inverse[0, :, slot, owner] = real * double * valid
            inverse[1, :, slot, owner] = imag * double * valid
    return forward.reshape(2 * KEPT * LAT, 512), inverse.reshape(2, 512, 8 * LAT)


def phase_np():
    table = np.zeros((LAT, 5, 2, 3, 4))
    for owner in range(LAT):
        for slot in range(KEPT):
            order = order_of(owner, slot)
            for b in range(-2, 3):
                angle = 2.0 * np.pi * ((order * b) % NLON) / NLON
                where = (owner, b + 2, slot // 4)
                table[where + (0, slot % 4)] = np.cos(angle)
                table[where + (1, slot % 4)] = np.cos(np.pi * b) if order == 0 else np.cos(angle)
                table[where + (2, slot % 4)] = np.sin(angle)
    return table.reshape(LAT, 5, 24).astype(np.float32)


def latitude_np():
    e, q = np.meshgrid(np.arange(ROWS), np.arange(LAT), indexing="ij")
    theta = np.pi * ((q * ROWS + e).reshape(-1) + 0.5) / NLAT
    weight = 2.0 * np.pi * np.pi * np.sin(theta) / NLAT
    rows = np.stack([np.cos(theta), np.log(np.sin(theta)), weight])
    return np.concatenate([rows, np.zeros((5, NLAT))]).astype(np.float32)


def seed_np():
    seeds = np.zeros((LAT, 8, 128), np.float32)
    for m in range(MODES):
        value = 0.5 * (
            math.log((2 * m + 1) / (4 * math.pi))
            + math.lgamma(2 * m + 1)
            - 2 * m * math.log(2)
            - 2 * math.lgamma(m + 1)
        )
        seeds[m // OWN, m % OWN] = value
    return seeds


def lane_slot(width):
    return lax.broadcasted_iota(jnp.int32, (1, 128), 1) // width


def swap_blocks(values, width):
    values = list(values)
    step = len(values) // 2
    while step:
        shift = step * width
        first = lane_slot(shift) % 2 == 0
        for a in range(len(values)):
            if not a & step:
                low, high = values[a], values[a | step]
                values[a] = jnp.where(first, low, pltpu.roll(high, shift, 1))
                values[a | step] = jnp.where(first, pltpu.roll(low, 128 - shift, 1), high)
        step //= 2
    return values


def split(value):
    high = value.astype(bf16)
    return high, (value - high.astype(f32)).astype(bf16)


def dot(a, b, dims=((1,), (0,))):
    return lax.dot_general(a, b, (dims, ((), ())), preferred_element_type=f32)


def dot3(a, b, dims=((1,), (0,))):
    return dot(a[0], b[0], dims) + (dot(a[1], b[0], dims) + dot(a[0], b[1], dims))


def pack_kernel(x_ref, out_ref):
    first = lane_slot(8) % 2 == 0
    for j in range(5):
        blocks = swap_blocks([x_ref[:, i, 128 * j : 128 * j + 128] for i in range(ROWS)], 16)
        for b in range(8):
            pair, place = divmod(8 * j + b, 5)
            even, odd = 2 * pair * LON_CHUNK, (2 * pair + 1) * LON_CHUNK
            block = blocks[b]
            if place == 2:
                top, bottom = block[:14], block[14:]
                out_ref[even + 56 : even + 70] = jnp.where(first, top, pltpu.roll(bottom, 8, 1))
                out_ref[odd + 56 : odd + 70] = jnp.where(first, pltpu.roll(top, 120, 1), bottom)
                out_ref[even + 70 : even + 72] = jnp.zeros((2, 128), f32)
                out_ref[odd + 70 : odd + 72] = jnp.zeros((2, 128), f32)
            else:
                base = (even, even + 28, None, odd, odd + 28)[place]
                out_ref[base : base + 28] = block


def forward_kernel(in_ref, high_ref, low_ref, out_ref):
    totals = []
    for half in range(2):
        pieces = []
        for start in (14 * half, 28 + 14 * half, 56):
            pieces.append(
                jnp.concatenate(
                    [in_ref[LON_CHUNK * q + start : LON_CHUNK * q + start + 16] for q in range(LON)],
                    axis=0,
                )
            )
        x = split(jnp.concatenate(pieces, axis=1))
        lanes = slice(256 * half, 256 * half + 256)
        totals.append(dot3((high_ref[:, lanes], low_ref[:, lanes]), x))
    both = totals[0][:, :256] + totals[1][:, :256]
    g0, g1 = totals[0][:, 256:], totals[1][:, 256:]
    half_rows = KEPT * LAT
    first = lane_slot(8) % 2 == 0
    last = jnp.where(
        first,
        g0[:half_rows] + pltpu.roll(g1[:half_rows], 120, 1),
        pltpu.roll(g0[half_rows:], 8, 1) + g1[half_rows:],
    )
    for row in range(2 * KEPT):
        part = both[LAT * row : LAT * row + LAT]
        out_ref[pl.ds(row, LAT, stride=LAT_CHUNK), :] = part[:, :128]
        out_ref[pl.ds(14 + row, LAT, stride=LAT_CHUNK), :] = part[:, 128:]
    for row in range(KEPT):
        out_ref[pl.ds(28 + row, LAT, stride=LAT_CHUNK), :] = last[LAT * row : LAT * row + LAT]


def legendre_kernel(owner_ref, angle_ref, seed_ref, high_ref, low_ref, left_ref, right_ref):
    slot = lax.broadcasted_iota(jnp.int32, (8, 256), 0)
    order_at = jnp.where(slot < OWN, owner_ref[0] * OWN + slot, 2 * MODES)
    order = order_at.astype(f32)
    degree = lax.broadcasted_iota(jnp.int32, (8, 256), 1).astype(f32)
    square, below = degree * degree, (degree - 1.0) * (degree - 1.0)
    upper = jnp.sqrt(
        jnp.maximum(4.0 * square - 1.0, 1.0) / jnp.maximum(square - order * order, 1.0)
    )
    lower = jnp.sqrt(
        jnp.maximum(below - order * order, 0.0) / jnp.maximum(4.0 * below - 1.0, 1.0)
    )
    product = upper * lower
    cosine = jnp.broadcast_to(angle_ref[0:1, :], (8, 256))
    diagonal = jnp.exp(seed_ref[:, 0:1] + order * angle_ref[1:2, :])
    previous = jnp.zeros((8, 256), f32)
    earlier = previous
    for l in range(MODES):
        current = jnp.where(
            order_at == l,
            diagonal,
            (upper[:, l : l + 1] * cosine) * previous - product[:, l : l + 1] * earlier,
        )
        left_ref[8 * l : 8 * l + 8] = current[:, :128]
        right_ref[8 * l : 8 * l + 8] = current[:, 128:]
        previous, earlier = current, previous
    for k in range(OWN):
        for part, source in enumerate((left_ref, right_ref)):
            high, low = split(source[pl.ds(k, MODES, stride=8), :])
            high_ref[k, :, 128 * part : 128 * part + 128] = high
            low_ref[k, :, 128 * part : 128 * part + 128] = low


def spectral_kernel(in_ref, high_ref, low_ref, taps_ref, gain_ref, angle_ref, out_ref, u_ref, v_ref, f_ref):
    lane = lax.broadcasted_iota(jnp.int32, (1, 128), 1) % LAT

    def fill_edges(ref):
        for part in range(2):
            for group in range(2):
                for e in (0, 1):
                    block = pltpu.roll(ref[part, group, 2 + e], 127, 1)
                    ref[part, group, 10 + e] = jnp.where(lane == LAT - 1, 0.0, block)
                    block = pltpu.roll(ref[part, group, 8 + e], 1, 1)
                    ref[part, group, e] = jnp.where(lane == 0, 0.0, block)

    def stencil(ref, which, store):
        for group in range(2):
            for tile in range(5):
                rows = slice(8 * tile, 8 * tile + 8)
                taps = []
                for a in range(5):
                    base = (which * 5 + a) * SLICE + 8 * tile
                    taps.append(
                        [
                            taps_ref[base : base + 8, (group * 3 + kind) * 128 : (group * 3 + kind) * 128 + 128]
                            for kind in range(3)
                        ]
                    )
                real = [ref[0, group, e, rows] for e in range(12)]
                imag = [ref[1, group, e, rows] for e in range(12)]
                for e in range(ROWS):
                    total_r, total_i = real[e + 2], imag[e + 2]
                    for a in range(5):
                        r_tap, s_tap, i_tap = taps[a]
                        total_r = total_r + (r_tap * real[e + a] - i_tap * imag[e + a])
                        total_i = total_i + (s_tap * imag[e + a] + i_tap * real[e + a])
                    store(group, rows, e, total_r, total_i)

    def rows_of(start, count):
        pieces = [in_ref[pl.ds(start + n, LAT, stride=LAT_CHUNK), :] for n in range(count)]
        if count < 4:
            pieces.append(jnp.zeros((LAT * (4 - count), 128), f32))
        return jnp.concatenate(pieces, axis=0).T

    for group in range(2):
        count = min(4, KEPT - 4 * group)
        for tile in range(2):
            for part in range(2):
                block = rows_of(14 * tile + KEPT * part + 4 * group, count)
                for e in range(ROWS):
                    u_ref[part, group, 2 + e, 16 * tile : 16 * tile + 16] = block[16 * e : 16 * e + 16]
        block = rows_of(28 + 4 * group, count)
        for e in range(ROWS):
            for part in range(2):
                start = 16 * e + 8 * part
                u_ref[part, group, 2 + e, 32:40] = block[start : start + 8]
    fill_edges(u_ref)

    def keep_first(group, rows, e, total_r, total_i):
        v_ref[0, group, 2 + e, rows] = total_r
        v_ref[1, group, 2 + e, rows] = total_i

    stencil(u_ref, 0, keep_first)

    weight = angle_ref[2:3, :]
    for part in range(2):
        for group in range(2):
            halves = [
                swap_blocks([v_ref[part, group, 2 + 4 * j + e] for e in range(4)], 32) for j in range(2)
            ]
            for n in range(4):
                if 4 * group + n < OWN:
                    f_ref[4 * group + n, SLICE * part : SLICE * part + SLICE] = (
                        jnp.concatenate([halves[0][n], halves[1][n]], axis=1) * weight
                    )
    for k in range(OWN):
        table = (high_ref[k], low_ref[k])
        spectrum = dot3(split(f_ref[k]), table, ((1,), (1,)))
        gain = gain_ref[80:160] if k == 0 else gain_ref[0:80]
        f_ref[k] = dot3(split(spectrum * gain), table)
    for part in range(2):
        for group in range(2):
            rows = slice(SLICE * part, SLICE * part + SLICE)
            for j in range(2):
                values = [
                    f_ref[4 * group + n, rows, 128 * j : 128 * j + 128]
                    if 4 * group + n < OWN
                    else jnp.zeros((SLICE, 128), f32)
                    for n in range(4)
                ]
                for e, value in enumerate(swap_blocks(values, 32)):
                    v_ref[part, group, 2 + 4 * j + e] = v_ref[part, group, 2 + 4 * j + e] + value
    fill_edges(v_ref)

    def keep_second(group, rows, e, total_r, total_i):
        u_ref[0, group, 2 + e, rows] = total_r
        u_ref[1, group, 2 + e, rows] = total_i

    stencil(v_ref, 1, keep_second)

    def give(start, count, pieces):
        block = jnp.concatenate(pieces, axis=0).T
        for n in range(count):
            out_ref[pl.ds(start + n, LAT, stride=LAT_CHUNK), :] = block[LAT * n : LAT * n + LAT]

    for group in range(2):
        count = min(4, KEPT - 4 * group)
        for tile in range(2):
            for part in range(2):
                give(
                    14 * tile + KEPT * part + 4 * group,
                    count,
                    [u_ref[part, group, 2 + e, 16 * tile : 16 * tile + 16] for e in range(ROWS)],
                )
        give(
            28 + 4 * group,
            count,
            [u_ref[part, group, 2 + e, 32:40] for e in range(ROWS) for part in range(2)],
        )


def inverse_kernel(in_ref, high_ref, low_ref, out_ref):
    totals = []
    for part in range(2):
        columns = []
        for start in (KEPT * part, 14 + KEPT * part, 28):
            pieces = [in_ref[pl.ds(start + k, LAT, stride=LAT_CHUNK), :] for k in range(KEPT)]
            columns.append(jnp.concatenate(pieces + [jnp.zeros((LAT, 128), f32)], axis=0))
        x = split(jnp.concatenate(columns, axis=1))
        totals.append(dot3((high_ref[part], low_ref[part]), x))
    both = totals[0][:, :256] + totals[1][:, :256]
    g0, g1 = totals[0][:, 256:], totals[1][:, 256:]
    first = lane_slot(8) % 2 == 0
    last = jnp.where(
        first,
        g0[:256] + pltpu.roll(g1[:256], 120, 1),
        pltpu.roll(g0[256:], 8, 1) + g1[256:],
    )
    for q in range(LON):
        base = LON_CHUNK * q
        for tile in range(2):
            for half in range(2):
                row = 256 * half + 16 * q
                start = base + 28 * tile + 14 * half
                out_ref[start : start + 14] = both[row : row + 14, 128 * tile : 128 * tile + 128]
        out_ref[base + 56 : base + 72] = last[16 * q : 16 * q + 16]


def mlp_kernel(in_ref, gain_ref, up_ref, down_hbm, out_ref, x_ref, down_ref, arrival):
    fetch = pltpu.make_async_copy(down_hbm, down_ref, arrival)
    fetch.start()
    first = lane_slot(8) % 2 == 0
    for j in range(5):
        blocks = []
        for b in range(8):
            pair, place = divmod(8 * j + b, 5)
            even, odd = 2 * pair * LON_CHUNK, (2 * pair + 1) * LON_CHUNK
            if place == 2:
                e, o = in_ref[even + 56 : even + 70], in_ref[odd + 56 : odd + 70]
                top = jnp.where(first, e, pltpu.roll(o, 8, 1))
                bottom = jnp.where(first, pltpu.roll(e, 120, 1), o)
                blocks.append(jnp.concatenate([top, bottom], axis=0))
            else:
                base = (even, even + 28, None, odd, odd + 28)[place]
                blocks.append(in_ref[base : base + 28])
        for i, value in enumerate(swap_blocks(blocks, 16)):
            x_ref[:, i, 128 * j : 128 * j + 128] = value
    x = x_ref[...].reshape(COLS * ROWS, CHANNELS)
    average = jnp.mean(x, axis=-1, keepdims=True)
    centred = x - average
    spread = jnp.mean(centred * centred, axis=-1, keepdims=True)
    normed = (centred * lax.rsqrt(spread + 1e-05) * gain_ref[...]).astype(bf16)
    total = x
    fetch.wait()
    for n in range(5):
        cut = slice(256 * n, 256 * n + 256)
        hidden = dot(normed, up_ref[:, cut])
        active = jax.nn.gelu(hidden, approximate=True).astype(bf16)
        total = total + dot(active, down_ref[cut, :])
    out_ref[...] = total.reshape(COLS, ROWS, CHANNELS)


def vmem(count):
    return [pl.BlockSpec(memory_space=pltpu.VMEM)] * count


def run(kernel, shape, *operands, scratch=(), cost=(0, 0), grant=24, far=0):
    return pl.pallas_call(
        kernel,
        out_shape=jax.ShapeDtypeStruct(shape, f32),
        in_specs=vmem(len(operands) - far) + [pl.BlockSpec(memory_space=pl.ANY)] * far,
        out_specs=pl.BlockSpec(memory_space=pltpu.VMEM),
        scratch_shapes=list(scratch),
        compiler_params=pltpu.CompilerParams(vmem_limit_bytes=grant << 20),
        cost_estimate=pl.CostEstimate(flops=cost[0], bytes_accessed=cost[1], transcendentals=0),
    )(*operands)


def legendre(owner, angles, seeds):
    table = jax.ShapeDtypeStruct((OWN, MODES, NLAT), bf16)
    return pl.pallas_call(
        legendre_kernel,
        out_shape=(table, table),
        in_specs=[pl.BlockSpec(memory_space=pltpu.SMEM)] + vmem(2),
        out_specs=vmem(2),
        scratch_shapes=[pltpu.VMEM((8 * MODES, 128), f32)] * 2,
        compiler_params=pltpu.CompilerParams(vmem_limit_bytes=16 << 20),
        cost_estimate=pl.CostEstimate(flops=10**7, bytes_accessed=10**7, transcendentals=0),
    )(owner, angles, seeds)


def own_channels(array, axis, start, odd):
    part = lax.dynamic_slice_in_dim(array, start, SLICE, axis)
    return jnp.where(odd, jnp.roll(part, -8, axis), part)


def exchange(array, axis, count):
    rows = array.shape[0] // count
    shape = (count, rows, 128) if rows % 8 == 0 else (count, 1, rows * 128)
    moved = lax.all_to_all(array.reshape(shape), axis, split_axis=0, concat_axis=0, tiled=True)
    return moved.reshape(array.shape)


def per_device(latent, conv_first, conv_second, filter_gains, norm_gain, up_weight, down_weight):
    band = lax.axis_index("lat")
    sector = lax.axis_index("lon")
    odd = sector % 2 == 1
    forward, inverse = fourier_np()
    forward, inverse = split_np(forward), split_np(inverse)
    angles = jnp.asarray(latitude_np())

    packed = run(pack_kernel, (LON * LON_CHUNK, 128), latent.transpose(1, 0, 2))
    circles = exchange(packed, "lon", LON)

    seeds = lax.dynamic_index_in_dim(jnp.asarray(seed_np()), band, 0, False)
    high, low = legendre(band.astype(jnp.int32).reshape(1), angles, seeds)
    phases = lax.dynamic_index_in_dim(jnp.asarray(phase_np()), band, 0, False)
    spread_np = np.kron(np.eye(24, dtype=np.float32), np.ones((1, LAT), np.float32))
    taps = jnp.stack([conv_first, conv_second]).reshape(2, 5, 5, CHANNELS)
    taps = own_channels(taps, 3, sector * SLICE, odd).transpose(0, 1, 3, 2).reshape(10 * SLICE, 5)
    taps = jnp.dot(taps, phases, precision=lax.Precision.HIGHEST)
    taps = jnp.dot(taps, jnp.asarray(spread_np), precision=lax.Precision.HIGHEST)
    gains = own_channels(filter_gains, 1, 0, odd).T
    gains = jnp.concatenate([gains, gains, gains, jnp.where(band == 0, 0.0, gains)], axis=0)

    coeffs = run(forward_kernel, (LAT * LAT_CHUNK, 128), circles, *map(jnp.asarray, forward))
    orders = exchange(coeffs, "lat", LAT)
    state = pltpu.VMEM((2, 2, 12, SLICE, 128), f32)
    third = run(
        spectral_kernel,
        (LAT * LAT_CHUNK, 128),
        orders,
        high,
        low,
        taps,
        gains,
        angles,
        scratch=[state, state, pltpu.VMEM((OWN, 2 * SLICE, NLAT), f32)],
    )
    returned = exchange(third, "lat", LAT)
    restored = run(inverse_kernel, (LON * LON_CHUNK, 128), returned, *map(jnp.asarray, inverse))
    arrived = exchange(restored, "lon", LON)
    result = run(
        mlp_kernel,
        (COLS, ROWS, CHANNELS),
        arrived,
        norm_gain.reshape(1, CHANNELS),
        up_weight,
        down_weight,
        scratch=[
            pltpu.VMEM((COLS, ROWS, CHANNELS), f32),
            pltpu.VMEM((HIDDEN, CHANNELS), bf16),
            pltpu.SemaphoreType.DMA,
        ],
        far=1,
    )
    return result.transpose(1, 0, 2)


def solution(mesh):
    return jax.shard_map(
        per_device,
        mesh=mesh,
        in_specs=(P("lat", "lon", None), P(), P(), P(None, "lon"), P(), P(), P()),
        out_specs=P("lat", "lon", None),
        check_vma=False,
    )
```

```python
import math

import jax
import jax.numpy as jnp
import numpy as np
from jax import lax
from jax.experimental import pallas as pl
from jax.experimental.pallas import tpu as pltpu
from jax.sharding import PartitionSpec as P

ROWS, COLS, CHANNELS, HIDDEN = 8, 28, 640, 1280
LAT, LON, SLICE = 32, 16, 40
NLAT, NLON, MODES = 256, 448, 192
OWN = MODES // LAT
KEPT = OWN + 1
LON_CHUNK = 72
LAT_CHUNK = 35
f32, bf16 = jnp.float32, jnp.bfloat16


def split_np(table):
    high = table.astype(np.float32).astype(jnp.bfloat16)
    low = (table - high.astype(np.float64)).astype(np.float32).astype(jnp.bfloat16)
    return high, low


def order_of(owner, slot):
    return owner * OWN + slot if slot < OWN else MODES + owner


def fourier_np():
    half, sector, step = np.meshgrid(np.arange(2), np.arange(LON), np.arange(16), indexing="ij")
    place = (sector * COLS + half * 14 + step).reshape(-1)
    valid = (step < 14).reshape(-1)
    forward = np.zeros((2, KEPT, LAT, 512))
    inverse = np.zeros((2, 512, 8, LAT))
    for slot in range(KEPT):
        for owner in range(LAT):
            order = order_of(owner, slot)
            angle = 2.0 * np.pi * ((order * place) % NLON) / NLON
            double = 1.0 if order == 0 else 2.0
            real, imag = np.cos(angle), -np.sin(angle)
            if order == 0:
                imag = np.cos(np.pi * (place % 2))
            forward[0, slot, owner] = real / NLON * valid
            forward[1, slot, owner] = imag / NLON * valid
            inverse[0, :, slot, owner] = real * double * valid
            inverse[1, :, slot, owner] = imag * double * valid
    return forward.reshape(2 * KEPT * LAT, 512), inverse.reshape(2, 512, 8 * LAT)


def phase_np():
    table = np.zeros((LAT, 5, 2, 3, 4))
    for owner in range(LAT):
        for slot in range(KEPT):
            order = order_of(owner, slot)
            for b in range(-2, 3):
                angle = 2.0 * np.pi * ((order * b) % NLON) / NLON
                where = (owner, b + 2, slot // 4)
                table[where + (0, slot % 4)] = np.cos(angle)
                table[where + (1, slot % 4)] = np.cos(np.pi * b) if order == 0 else np.cos(angle)
                table[where + (2, slot % 4)] = np.sin(angle)
    return table.reshape(LAT, 5, 24).astype(np.float32)


def latitude_np():
    e, q = np.meshgrid(np.arange(ROWS), np.arange(LAT), indexing="ij")
    theta = np.pi * ((q * ROWS + e).reshape(-1) + 0.5) / NLAT
    weight = 2.0 * np.pi * np.pi * np.sin(theta) / NLAT
    rows = np.stack([np.cos(theta), np.log(np.sin(theta)), weight])
    return np.concatenate([rows, np.zeros((5, NLAT))]).astype(np.float32)


def seed_np():
    seeds = np.zeros((LAT, 8, 128), np.float32)
    for m in range(MODES):
        value = 0.5 * (
            math.log((2 * m + 1) / (4 * math.pi))
            + math.lgamma(2 * m + 1)
            - 2 * m * math.log(2)
            - 2 * math.lgamma(m + 1)
        )
        seeds[m // OWN, m % OWN] = value
    return seeds


def lane_slot(width):
    return lax.broadcasted_iota(jnp.int32, (1, 128), 1) // width


def swap_blocks(values, width):
    values = list(values)
    step = len(values) // 2
    while step:
        shift = step * width
        first = lane_slot(shift) % 2 == 0
        for a in range(len(values)):
            if not a & step:
                low, high = values[a], values[a | step]
                values[a] = jnp.where(first, low, pltpu.roll(high, shift, 1))
                values[a | step] = jnp.where(first, pltpu.roll(low, 128 - shift, 1), high)
        step //= 2
    return values


def split(value):
    high = value.astype(bf16)
    return high, (value - high.astype(f32)).astype(bf16)


def dot(a, b, dims=((1,), (0,))):
    return lax.dot_general(a, b, (dims, ((), ())), preferred_element_type=f32)


def dot3(a, b, dims=((1,), (0,))):
    return dot(a[0], b[0], dims) + (dot(a[1], b[0], dims) + dot(a[0], b[1], dims))


def pack_kernel(x_hbm, out_ref, x_ref, arrivals):
    first = lane_slot(8) % 2 == 0
    fetches = []
    for j in range(5):
        lanes = pl.ds(128 * j, 128)
        fetches.append(pltpu.make_async_copy(x_hbm.at[:, :, lanes], x_ref.at[:, :, lanes], arrivals.at[j]))
        fetches[j].start()
    for j in range(5):
        fetches[j].wait()
        blocks = swap_blocks([x_ref[:, i, 128 * j : 128 * j + 128] for i in range(ROWS)], 16)
        for b in range(8):
            pair, place = divmod(8 * j + b, 5)
            even, odd = 2 * pair * LON_CHUNK, (2 * pair + 1) * LON_CHUNK
            block = blocks[b]
            if place == 2:
                top, bottom = block[:14], block[14:]
                out_ref[even + 56 : even + 70] = jnp.where(first, top, pltpu.roll(bottom, 8, 1))
                out_ref[odd + 56 : odd + 70] = jnp.where(first, pltpu.roll(top, 120, 1), bottom)
                out_ref[even + 70 : even + 72] = jnp.zeros((2, 128), f32)
                out_ref[odd + 70 : odd + 72] = jnp.zeros((2, 128), f32)
            else:
                base = (even, even + 28, None, odd, odd + 28)[place]
                out_ref[base : base + 28] = block


def forward_kernel(in_ref, high_ref, low_ref, out_ref):
    totals = []
    for half in range(2):
        pieces = []
        for start in (14 * half, 28 + 14 * half, 56):
            pieces.append(
                jnp.concatenate(
                    [in_ref[LON_CHUNK * q + start : LON_CHUNK * q + start + 16] for q in range(LON)],
                    axis=0,
                )
            )
        x = split(jnp.concatenate(pieces, axis=1))
        lanes = slice(256 * half, 256 * half + 256)
        totals.append(dot3((high_ref[:, lanes], low_ref[:, lanes]), x))
    both = totals[0][:, :256] + totals[1][:, :256]
    g0, g1 = totals[0][:, 256:], totals[1][:, 256:]
    half_rows = KEPT * LAT
    first = lane_slot(8) % 2 == 0
    last = jnp.where(
        first,
        g0[:half_rows] + pltpu.roll(g1[:half_rows], 120, 1),
        pltpu.roll(g0[half_rows:], 8, 1) + g1[half_rows:],
    )
    for row in range(2 * KEPT):
        part = both[LAT * row : LAT * row + LAT]
        out_ref[pl.ds(row, LAT, stride=LAT_CHUNK), :] = part[:, :128]
        out_ref[pl.ds(14 + row, LAT, stride=LAT_CHUNK), :] = part[:, 128:]
    for row in range(KEPT):
        out_ref[pl.ds(28 + row, LAT, stride=LAT_CHUNK), :] = last[LAT * row : LAT * row + LAT]


def legendre_kernel(owner_ref, angle_ref, seed_ref, high_ref, low_ref, left_ref, right_ref):
    slot = lax.broadcasted_iota(jnp.int32, (8, 256), 0)
    order_at = jnp.where(slot < OWN, owner_ref[0] * OWN + slot, 2 * MODES)
    order = order_at.astype(f32)
    degree = lax.broadcasted_iota(jnp.int32, (8, 256), 1).astype(f32)
    square, below = degree * degree, (degree - 1.0) * (degree - 1.0)
    upper = jnp.sqrt(
        jnp.maximum(4.0 * square - 1.0, 1.0) / jnp.maximum(square - order * order, 1.0)
    )
    lower = jnp.sqrt(
        jnp.maximum(below - order * order, 0.0) / jnp.maximum(4.0 * below - 1.0, 1.0)
    )
    product = upper * lower
    cosine = jnp.broadcast_to(angle_ref[0:1, :], (8, 256))
    diagonal = jnp.exp(seed_ref[:, 0:1] + order * angle_ref[1:2, :])
    previous = jnp.zeros((8, 256), f32)
    earlier = previous
    for l in range(MODES):
        current = jnp.where(
            order_at == l,
            diagonal,
            (upper[:, l : l + 1] * cosine) * previous - product[:, l : l + 1] * earlier,
        )
        left_ref[8 * l : 8 * l + 8] = current[:, :128]
        right_ref[8 * l : 8 * l + 8] = current[:, 128:]
        previous, earlier = current, previous
    for k in range(OWN):
        for part, source in enumerate((left_ref, right_ref)):
            high, low = split(source[pl.ds(k, MODES, stride=8), :])
            high_ref[k, :, 128 * part : 128 * part + 128] = high
            low_ref[k, :, 128 * part : 128 * part + 128] = low


def spectral_kernel(in_ref, high_ref, low_ref, taps_ref, gain_ref, angle_ref, out_ref, u_ref, v_ref, f_ref):
    lane = lax.broadcasted_iota(jnp.int32, (1, 128), 1) % LAT

    def fill_edges(ref):
        for part in range(2):
            for group in range(2):
                for e in (0, 1):
                    block = pltpu.roll(ref[part, group, 2 + e], 127, 1)
                    ref[part, group, 10 + e] = jnp.where(lane == LAT - 1, 0.0, block)
                    block = pltpu.roll(ref[part, group, 8 + e], 1, 1)
                    ref[part, group, e] = jnp.where(lane == 0, 0.0, block)

    def stencil(ref, which, store):
        for group in range(2):
            for tile in range(5):
                rows = slice(8 * tile, 8 * tile + 8)
                taps = []
                for a in range(5):
                    base = (which * 5 + a) * SLICE + 8 * tile
                    taps.append(
                        [
                            taps_ref[base : base + 8, (group * 3 + kind) * 128 : (group * 3 + kind) * 128 + 128]
                            for kind in range(3)
                        ]
                    )
                real = [ref[0, group, e, rows] for e in range(12)]
                imag = [ref[1, group, e, rows] for e in range(12)]
                for e in range(ROWS):
                    total_r, total_i = real[e + 2], imag[e + 2]
                    for a in range(5):
                        r_tap, s_tap, i_tap = taps[a]
                        total_r = total_r + (r_tap * real[e + a] - i_tap * imag[e + a])
                        total_i = total_i + (s_tap * imag[e + a] + i_tap * real[e + a])
                    store(group, rows, e, total_r, total_i)

    def rows_of(start, count):
        pieces = [in_ref[pl.ds(start + n, LAT, stride=LAT_CHUNK), :] for n in range(count)]
        if count < 4:
            pieces.append(jnp.zeros((LAT * (4 - count), 128), f32))
        return jnp.concatenate(pieces, axis=0).T

    for group in range(2):
        count = min(4, KEPT - 4 * group)
        for tile in range(2):
            for part in range(2):
                block = rows_of(14 * tile + KEPT * part + 4 * group, count)
                for e in range(ROWS):
                    u_ref[part, group, 2 + e, 16 * tile : 16 * tile + 16] = block[16 * e : 16 * e + 16]
        block = rows_of(28 + 4 * group, count)
        for e in range(ROWS):
            for part in range(2):
                start = 16 * e + 8 * part
                u_ref[part, group, 2 + e, 32:40] = block[start : start + 8]
    fill_edges(u_ref)

    def keep_first(group, rows, e, total_r, total_i):
        v_ref[0, group, 2 + e, rows] = total_r
        v_ref[1, group, 2 + e, rows] = total_i

    stencil(u_ref, 0, keep_first)

    weight = angle_ref[2:3, :]
    for part in range(2):
        for group in range(2):
            halves = [
                swap_blocks([v_ref[part, group, 2 + 4 * j + e] for e in range(4)], 32) for j in range(2)
            ]
            for n in range(4):
                if 4 * group + n < OWN:
                    f_ref[4 * group + n, SLICE * part : SLICE * part + SLICE] = (
                        jnp.concatenate([halves[0][n], halves[1][n]], axis=1) * weight
                    )
    for k in range(OWN):
        table = (high_ref[k], low_ref[k])
        spectrum = dot3(split(f_ref[k]), table, ((1,), (1,)))
        gain = gain_ref[80:160] if k == 0 else gain_ref[0:80]
        f_ref[k] = dot3(split(spectrum * gain), table)
    for part in range(2):
        for group in range(2):
            rows = slice(SLICE * part, SLICE * part + SLICE)
            for j in range(2):
                values = [
                    f_ref[4 * group + n, rows, 128 * j : 128 * j + 128]
                    if 4 * group + n < OWN
                    else jnp.zeros((SLICE, 128), f32)
                    for n in range(4)
                ]
                for e, value in enumerate(swap_blocks(values, 32)):
                    v_ref[part, group, 2 + 4 * j + e] = v_ref[part, group, 2 + 4 * j + e] + value
    fill_edges(v_ref)

    def keep_second(group, rows, e, total_r, total_i):
        u_ref[0, group, 2 + e, rows] = total_r
        u_ref[1, group, 2 + e, rows] = total_i

    stencil(v_ref, 1, keep_second)

    def give(start, count, pieces):
        block = jnp.concatenate(pieces, axis=0).T
        for n in range(count):
            out_ref[pl.ds(start + n, LAT, stride=LAT_CHUNK), :] = block[LAT * n : LAT * n + LAT]

    for group in range(2):
        count = min(4, KEPT - 4 * group)
        for tile in range(2):
            for part in range(2):
                give(
                    14 * tile + KEPT * part + 4 * group,
                    count,
                    [u_ref[part, group, 2 + e, 16 * tile : 16 * tile + 16] for e in range(ROWS)],
                )
        give(
            28 + 4 * group,
            count,
            [u_ref[part, group, 2 + e, 32:40] for e in range(ROWS) for part in range(2)],
        )


def inverse_kernel(in_ref, high_ref, low_ref, out_ref):
    totals = []
    for part in range(2):
        columns = []
        for start in (KEPT * part, 14 + KEPT * part, 28):
            pieces = [in_ref[pl.ds(start + k, LAT, stride=LAT_CHUNK), :] for k in range(KEPT)]
            columns.append(jnp.concatenate(pieces + [jnp.zeros((LAT, 128), f32)], axis=0))
        x = split(jnp.concatenate(columns, axis=1))
        totals.append(dot3((high_ref[part], low_ref[part]), x))
    both = totals[0][:, :256] + totals[1][:, :256]
    g0, g1 = totals[0][:, 256:], totals[1][:, 256:]
    first = lane_slot(8) % 2 == 0
    last = jnp.where(
        first,
        g0[:256] + pltpu.roll(g1[:256], 120, 1),
        pltpu.roll(g0[256:], 8, 1) + g1[256:],
    )
    for q in range(LON):
        base = LON_CHUNK * q
        for tile in range(2):
            for half in range(2):
                row = 256 * half + 16 * q
                start = base + 28 * tile + 14 * half
                out_ref[start : start + 14] = both[row : row + 14, 128 * tile : 128 * tile + 128]
        out_ref[base + 56 : base + 72] = last[16 * q : 16 * q + 16]


def mlp_kernel(in_ref, gain_ref, up_ref, down_ref, out_hbm, x_ref, y_ref, sent):
    first = lane_slot(8) % 2 == 0
    for j in range(5):
        blocks = []
        for b in range(8):
            pair, place = divmod(8 * j + b, 5)
            even, odd = 2 * pair * LON_CHUNK, (2 * pair + 1) * LON_CHUNK
            if place == 2:
                e, o = in_ref[even + 56 : even + 70], in_ref[odd + 56 : odd + 70]
                top = jnp.where(first, e, pltpu.roll(o, 8, 1))
                bottom = jnp.where(first, pltpu.roll(e, 120, 1), o)
                blocks.append(jnp.concatenate([top, bottom], axis=0))
            else:
                base = (even, even + 28, None, odd, odd + 28)[place]
                blocks.append(in_ref[base : base + 28])
        for i, value in enumerate(swap_blocks(blocks, 16)):
            x_ref[:, i, 128 * j : 128 * j + 128] = value
    x = x_ref[...].reshape(COLS * ROWS, CHANNELS)
    average = jnp.mean(x, axis=-1, keepdims=True)
    centred = x - average
    spread = jnp.mean(centred * centred, axis=-1, keepdims=True)
    normed = (centred * lax.rsqrt(spread + 1e-05) * gain_ref[...].reshape(1, CHANNELS)).astype(bf16)
    active = []
    for n in range(5):
        hidden = dot(normed, up_ref[:, 256 * n : 256 * n + 256])
        active.append(jax.nn.gelu(hidden, approximate=True).astype(bf16))
    active = jnp.concatenate(active, axis=1)
    stores = []
    for n, (start, width) in enumerate(((0, 256), (256, 256), (512, 128))):
        lanes = pl.ds(start, width)
        total = x[:, start : start + width] + dot(active, down_ref[:, start : start + width])
        y_ref[:, :, start : start + width] = total.reshape(COLS, ROWS, width)
        stores.append(pltpu.make_async_copy(y_ref.at[:, :, lanes], out_hbm.at[:, :, lanes], sent.at[n]))
        stores[n].start()
    for store in stores:
        store.wait()


def vmem(count):
    return [pl.BlockSpec(memory_space=pltpu.VMEM)] * count


def run(kernel, shape, *operands, scratch=(), cost=(0, 0), grant=24, far=0, out=pltpu.VMEM):
    return pl.pallas_call(
        kernel,
        out_shape=jax.ShapeDtypeStruct(shape, f32),
        in_specs=vmem(len(operands) - far) + [pl.BlockSpec(memory_space=pltpu.HBM)] * far,
        out_specs=pl.BlockSpec(memory_space=out),
        scratch_shapes=list(scratch),
        compiler_params=pltpu.CompilerParams(vmem_limit_bytes=grant << 20),
        cost_estimate=pl.CostEstimate(flops=cost[0], bytes_accessed=cost[1], transcendentals=0),
    )(*operands)


def legendre(owner, angles, seeds):
    table = jax.ShapeDtypeStruct((OWN, MODES, NLAT), bf16)
    return pl.pallas_call(
        legendre_kernel,
        out_shape=(table, table),
        in_specs=[pl.BlockSpec(memory_space=pltpu.SMEM)] + vmem(2),
        out_specs=vmem(2),
        scratch_shapes=[pltpu.VMEM((8 * MODES, 128), f32)] * 2,
        compiler_params=pltpu.CompilerParams(vmem_limit_bytes=16 << 20),
        cost_estimate=pl.CostEstimate(flops=10**7, bytes_accessed=10**7, transcendentals=0),
    )(owner, angles, seeds)


def own_channels(array, axis, start, odd):
    part = lax.dynamic_slice_in_dim(array, start, SLICE, axis)
    return jnp.where(odd, jnp.roll(part, -8, axis), part)


def exchange(array, axis, count):
    rows = array.shape[0] // count
    shape = (count, rows, 128) if rows % 8 == 0 else (count, 1, rows * 128)
    moved = lax.all_to_all(array.reshape(shape), axis, split_axis=0, concat_axis=0, tiled=True)
    return moved.reshape(array.shape)


def per_device(latent, conv_first, conv_second, filter_gains, norm_gain, up_weight, down_weight):
    band = lax.axis_index("lat")
    sector = lax.axis_index("lon")
    odd = sector % 2 == 1
    forward, inverse = fourier_np()
    forward, inverse = split_np(forward), split_np(inverse)
    angles = jnp.asarray(latitude_np())

    packed = run(
        pack_kernel,
        (LON * LON_CHUNK, 128),
        latent.transpose(1, 0, 2),
        scratch=[pltpu.VMEM((COLS, ROWS, CHANNELS), f32), pltpu.SemaphoreType.DMA((5,))],
        far=1,
        grant=60,
    )
    circles = exchange(packed, "lon", LON)

    seeds = lax.dynamic_index_in_dim(jnp.asarray(seed_np()), band, 0, False)
    high, low = legendre(band.astype(jnp.int32).reshape(1), angles, seeds)
    phases = lax.dynamic_index_in_dim(jnp.asarray(phase_np()), band, 0, False)
    spread_np = np.kron(np.eye(24, dtype=np.float32), np.ones((1, LAT), np.float32))
    taps = jnp.stack([conv_first, conv_second]).reshape(2, 5, 5, CHANNELS)
    taps = own_channels(taps, 3, sector * SLICE, odd).transpose(0, 1, 3, 2).reshape(10 * SLICE, 5)
    taps = jnp.dot(taps, phases, precision=lax.Precision.HIGHEST)
    taps = jnp.dot(taps, jnp.asarray(spread_np), precision=lax.Precision.HIGHEST)
    gains = own_channels(filter_gains, 1, 0, odd).T
    gains = jnp.concatenate([gains, gains, gains, jnp.where(band == 0, 0.0, gains)], axis=0)

    coeffs = run(forward_kernel, (LAT * LAT_CHUNK, 128), circles, *map(jnp.asarray, forward))
    orders = exchange(coeffs, "lat", LAT)
    state = pltpu.VMEM((2, 2, 12, SLICE, 128), f32)
    third = run(
        spectral_kernel,
        (LAT * LAT_CHUNK, 128),
        orders,
        high,
        low,
        taps,
        gains,
        angles,
        scratch=[state, state, pltpu.VMEM((OWN, 2 * SLICE, NLAT), f32)],
    )
    returned = exchange(third, "lat", LAT)
    restored = run(inverse_kernel, (LON * LON_CHUNK, 128), returned, *map(jnp.asarray, inverse))
    arrived = exchange(restored, "lon", LON)
    result = run(
        mlp_kernel,
        (COLS, ROWS, CHANNELS),
        arrived,
        norm_gain,
        up_weight,
        down_weight,
        scratch=[
            pltpu.VMEM((COLS, ROWS, CHANNELS), f32),
            pltpu.VMEM((COLS, ROWS, CHANNELS), f32),
            pltpu.SemaphoreType.DMA((3,)),
        ],
        out=pltpu.HBM,
    )
    return result.transpose(1, 0, 2)


def solution(mesh):
    return jax.shard_map(
        per_device,
        mesh=mesh,
        in_specs=(P("lat", "lon", None), P(), P(), P(None, "lon"), P(), P(), P()),
        out_specs=P("lat", "lon", None),
        check_vma=False,
    )
```

```python
import math

import jax
import jax.numpy as jnp
import numpy as np
from jax import lax
from jax.experimental import pallas as pl
from jax.experimental.pallas import tpu as pltpu
from jax.sharding import PartitionSpec as P

ROWS, COLS, CHANNELS, HIDDEN = 8, 28, 640, 1280
LAT, LON, SLICE = 32, 16, 40
NLAT, NLON, MODES = 256, 448, 192
OWN = MODES // LAT
KEPT = OWN + 1
LON_CHUNK = 72
LAT_CHUNK = 30
f32, bf16 = jnp.float32, jnp.bfloat16


def split_np(table):
    high = table.astype(np.float32).astype(jnp.bfloat16)
    low = (table - high.astype(np.float64)).astype(np.float32).astype(jnp.bfloat16)
    return high, low


def order_of(owner, slot):
    return owner * OWN + slot if slot < OWN else MODES + owner


def fourier_np():
    half, sector, step = np.meshgrid(np.arange(2), np.arange(LON), np.arange(16), indexing="ij")
    place = (sector * COLS + half * 14 + step).reshape(-1)
    valid = (step < 14).reshape(-1)
    forward = np.zeros((2, KEPT, LAT, 512))
    inverse = np.zeros((2, 512, 8, LAT))
    for slot in range(KEPT):
        for owner in range(LAT):
            order = order_of(owner, slot)
            angle = 2.0 * np.pi * ((order * place) % NLON) / NLON
            double = 1.0 if order == 0 else 2.0
            real, imag = np.cos(angle), -np.sin(angle)
            if order == 0:
                imag = np.cos(np.pi * (place % 2))
            forward[0, slot, owner] = real / NLON * valid
            forward[1, slot, owner] = imag / NLON * valid
            inverse[0, :, slot, owner] = real * double * valid
            inverse[1, :, slot, owner] = imag * double * valid
    return forward.reshape(2 * KEPT * LAT, 512), inverse.reshape(2, 512, 8 * LAT)


def phase_np():
    table = np.zeros((LAT, 8, 2, 3, 4))
    for owner in range(LAT):
        for slot in range(KEPT):
            order = order_of(owner, slot)
            for b in range(-2, 3):
                angle = 2.0 * np.pi * ((order * b) % NLON) / NLON
                where = (owner, b + 2, slot // 4)
                table[where + (0, slot % 4)] = np.cos(angle)
                table[where + (1, slot % 4)] = np.cos(np.pi * b) if order == 0 else np.cos(angle)
                table[where + (2, slot % 4)] = np.sin(angle)
    return table.reshape(LAT, 8, 24).astype(np.float32)


def latitude_np():
    e, q = np.meshgrid(np.arange(ROWS), np.arange(LAT), indexing="ij")
    theta = np.pi * ((q * ROWS + e).reshape(-1) + 0.5) / NLAT
    weight = 2.0 * np.pi * np.pi * np.sin(theta) / NLAT
    rows = np.stack([np.cos(theta), np.log(np.sin(theta)), weight])
    return np.concatenate([rows, np.zeros((5, NLAT))]).astype(np.float32)


def seed_np():
    seeds = np.zeros((LAT, 8, 128), np.float32)
    for m in range(MODES):
        value = 0.5 * (
            math.log((2 * m + 1) / (4 * math.pi))
            + math.lgamma(2 * m + 1)
            - 2 * m * math.log(2)
            - 2 * math.lgamma(m + 1)
        )
        seeds[m // OWN, m % OWN] = value
    return seeds


def lane_slot(width):
    return lax.broadcasted_iota(jnp.int32, (1, 128), 1) // width


def swap_blocks(values, width):
    values = list(values)
    step = len(values) // 2
    while step:
        shift = step * width
        first = lane_slot(shift) % 2 == 0
        for a in range(len(values)):
            if not a & step:
                low, high = values[a], values[a | step]
                values[a] = jnp.where(first, low, pltpu.roll(high, shift, 1))
                values[a | step] = jnp.where(first, pltpu.roll(low, 128 - shift, 1), high)
        step //= 2
    return values


def split(value):
    high = value.astype(bf16)
    return high, (value - high.astype(f32)).astype(bf16)


def dot(a, b, dims=((1,), (0,))):
    return lax.dot_general(a, b, (dims, ((), ())), preferred_element_type=f32)


def dot3(a, b, dims=((1,), (0,))):
    return dot(a[0], b[0], dims) + (dot(a[1], b[0], dims) + dot(a[0], b[1], dims))


def pack_kernel(x_hbm, out_hbm, x_ref, out_ref, arrivals, sent):
    first = lane_slot(8) % 2 == 0
    fetches = []
    for j in range(5):
        lanes = pl.ds(128 * j, 128)
        fetches.append(pltpu.make_async_copy(x_hbm.at[:, :, lanes], x_ref.at[:, :, lanes], arrivals.at[j]))
        fetches[j].start()
    stores = []
    for j in range(5):
        fetches[j].wait()
        blocks = swap_blocks([x_ref[:, i, 128 * j : 128 * j + 128] for i in range(ROWS)], 16)
        for b in range(8):
            pair, place = divmod(8 * j + b, 5)
            even, odd = 2 * pair * LON_CHUNK, (2 * pair + 1) * LON_CHUNK
            block = blocks[b]
            if place == 2:
                top, bottom = block[:14], block[14:]
                out_ref[even + 56 : even + 70] = jnp.where(first, top, pltpu.roll(bottom, 8, 1))
                out_ref[odd + 56 : odd + 70] = jnp.where(first, pltpu.roll(top, 120, 1), bottom)
                out_ref[even + 70 : even + 72] = jnp.zeros((2, 128), f32)
                out_ref[odd + 70 : odd + 72] = jnp.zeros((2, 128), f32)
            else:
                base = (even, even + 28, None, odd, odd + 28)[place]
                out_ref[base : base + 28] = block
            if place == 4:
                rows = pl.ds(even, 2 * LON_CHUNK)
                stores.append(pltpu.make_async_copy(out_ref.at[rows], out_hbm.at[rows], sent.at[pair]))
                stores[pair].start()
    for store in stores:
        store.wait()


def forward_kernel(in_ref, high_ref, low_ref, out_ref, local_ref, up_ref, down_ref):
    totals = []
    for half in range(2):
        pieces = []
        for start in (14 * half, 28 + 14 * half, 56):
            pieces.append(
                jnp.concatenate(
                    [in_ref[LON_CHUNK * q + start : LON_CHUNK * q + start + 16] for q in range(LON)],
                    axis=0,
                )
            )
        x = split(jnp.concatenate(pieces, axis=1))
        lanes = slice(256 * half, 256 * half + 256)
        totals.append(dot3((high_ref[:, lanes], low_ref[:, lanes]), x))
    both = totals[0][:, :256] + totals[1][:, :256]
    g0, g1 = totals[0][:, 256:], totals[1][:, 256:]
    half_rows = KEPT * LAT
    first = lane_slot(8) % 2 == 0
    last = jnp.where(
        first,
        g0[:half_rows] + pltpu.roll(g1[:half_rows], 120, 1),
        pltpu.roll(g0[half_rows:], 8, 1) + g1[half_rows:],
    )
    for r in range(2):
        for k in range(OWN):
            part = both[LAT * (KEPT * r + k) : LAT * (KEPT * r + k) + LAT]
            row = OWN * r + k
            out_ref[pl.ds(row, LAT, stride=LAT_CHUNK), :] = part[:, :128]
            out_ref[pl.ds(2 * OWN + row, LAT, stride=LAT_CHUNK), :] = part[:, 128:]
    for k in range(OWN):
        out_ref[pl.ds(4 * OWN + k, LAT, stride=LAT_CHUNK), :] = last[LAT * k : LAT * k + LAT]
    left = lane_slot(64) == 0
    for r in range(2):
        part = both[LAT * (KEPT * r + OWN) : LAT * (KEPT * r + OWN) + LAT]
        a, b = part[:, :128], part[:, 128:]
        rows = slice(LAT * r, LAT * r + LAT)
        local_ref[rows, :128] = a
        local_ref[rows, 128:256] = b
        up_ref[rows] = jnp.where(left, pltpu.roll(a, 64, 1), b)
        down_ref[rows] = jnp.where(left, a, pltpu.roll(b, 64, 1))
    part = last[LAT * OWN : LAT * OWN + LAT]
    local_ref[0:LAT, 256:] = part
    local_ref[LAT:, 256:] = jnp.zeros((LAT, 128), f32)
    up_ref[2 * LAT :] = part
    down_ref[2 * LAT :] = part


def local_kernel(band_ref, own_ref, below_ref, above_ref, taps_ref, wave_ref, out_ref):
    lane = lax.broadcasted_iota(jnp.int32, (1, 128), 1)
    left = lane < 64
    south = jnp.where(band_ref[0] == 0, 0.0, 1.0)
    north = jnp.where(band_ref[0] == LAT - 1, 0.0, 1.0)
    masks = (jnp.where(left, south, 1.0), jnp.where(left, 1.0, north))

    def extend(own, below, above):
        turned = pltpu.roll(own, 64, 1)
        return jnp.where(left, below, turned), jnp.where(left, turned, above)

    def turn(value):
        return pltpu.roll(value, 64, 1)

    def shifted(tiles, a):
        if a == 0:
            return tiles
        amount = (-16 * a) % 128
        first, second = (pltpu.roll(tile, amount, 1) for tile in tiles)
        if a > 0:
            keep = lane < 128 - 16 * a
            return jnp.where(keep, first, second), jnp.where(keep, second, first)
        keep = lane >= -16 * a
        return jnp.where(keep, first, second), jnp.where(keep, second, first)

    def weights(which, a, tile):
        rows = [taps_ref[(which * 5 + a) * 5 + b : (which * 5 + a) * 5 + b + 1, 128 * tile : 128 * tile + 128] for b in range(5)]
        cos1, cos2, sin1, sin2 = (wave_ref[:, 128 * n : 128 * n + 128] for n in range(4))
        real = rows[2] + (rows[3] + rows[1]) * cos1 + (rows[4] + rows[0]) * cos2
        imag = (rows[3] - rows[1]) * sin1 + (rows[4] - rows[0]) * sin2
        return real, imag

    for tile in range(2):
        parts = []
        for r in range(2):
            rows = slice(LAT * r, LAT * r + LAT)
            own = own_ref[rows, 128 * tile : 128 * tile + 128]
            below, above = below_ref[rows], above_ref[rows]
            if tile == 0:
                parts.append(extend(own, below, turn(above)))
            else:
                parts.append(extend(own, turn(below), above))
        for which in range(2):
            real, imag = [list(value) for value in parts]
            for a in range(-2, 3):
                w_r, w_i = weights(which, a + 2, tile)
                e_r, e_i = shifted(parts[0], a), shifted(parts[1], a)
                for n in range(2):
                    real[n] = real[n] + (w_r * e_r[n] - w_i * e_i[n])
                    imag[n] = imag[n] + (w_r * e_i[n] + w_i * e_r[n])
            parts = [tuple(v * m for v, m in zip(value, masks)) for value in (real, imag)]
        for r in range(2):
            result = jnp.where(left, turn(parts[r][0]), turn(parts[r][1]))
            out_ref[LAT * r : LAT * r + LAT, 128 * tile : 128 * tile + 128] = result
    second = lane_slot(8) % 2 == 1
    value = extend(own_ref[0:LAT, 256:], turn(below_ref[2 * LAT :]), turn(above_ref[2 * LAT :]))
    for which in range(2):
        total = list(value)
        swapped = [jnp.where(second, pltpu.roll(v, 8, 1), pltpu.roll(v, 120, 1)) for v in value]
        for a in range(-2, 3):
            w_r, w_i = weights(which, a + 2, 2)
            w_i = jnp.where(second, w_i, -w_i)
            e, f = shifted(value, a), shifted(swapped, a)
            for n in range(2):
                total[n] = total[n] + (w_r * e[n] + w_i * f[n])
        value = tuple(v * m for v, m in zip(total, masks))
    out_ref[0:LAT, 256:] = jnp.where(left, turn(value[0]), turn(value[1]))
    out_ref[LAT:, 256:] = jnp.zeros((LAT, 128), f32)


def taps_kernel(rows_ref, phase_ref, plain_ref, lanes_ref, taps_ref, spread_ref):
    spread_ref[...] = jnp.dot(plain_ref[...], lanes_ref[...], precision=lax.Precision.HIGHEST)
    for tile in range(6):
        phase = phase_ref[:, 4 * tile : 4 * tile + 1]
        for n in range(1, 4):
            column = phase_ref[:, 4 * tile + n : 4 * tile + n + 1]
            phase = jnp.where(lane_slot(LAT) >= n, column, phase)
        total = rows_ref[:, 0:1] * phase[0:1]
        for b in range(1, 5):
            total = total + rows_ref[:, b : b + 1] * phase[b : b + 1]
        taps_ref[:, 128 * tile : 128 * tile + 128] = total


def legendre_kernel(owner_ref, angle_ref, seed_ref, high_ref, low_ref, left_ref, right_ref):
    slot = lax.broadcasted_iota(jnp.int32, (8, 256), 0)
    order_at = jnp.where(slot < OWN, owner_ref[0] * OWN + slot, 2 * MODES)
    order = order_at.astype(f32)
    degree = lax.broadcasted_iota(jnp.int32, (8, 256), 1).astype(f32)
    square, below = degree * degree, (degree - 1.0) * (degree - 1.0)
    upper = jnp.sqrt(
        jnp.maximum(4.0 * square - 1.0, 1.0) / jnp.maximum(square - order * order, 1.0)
    )
    lower = jnp.sqrt(
        jnp.maximum(below - order * order, 0.0) / jnp.maximum(4.0 * below - 1.0, 1.0)
    )
    product = upper * lower
    cosine = jnp.broadcast_to(angle_ref[0:1, :], (8, 256))
    diagonal = jnp.exp(seed_ref[:, 0:1] + order * angle_ref[1:2, :])
    previous = jnp.zeros((8, 256), f32)
    earlier = previous
    for l in range(MODES):
        current = jnp.where(
            order_at == l,
            diagonal,
            (upper[:, l : l + 1] * cosine) * previous - product[:, l : l + 1] * earlier,
        )
        left_ref[8 * l : 8 * l + 8] = current[:, :128]
        right_ref[8 * l : 8 * l + 8] = current[:, 128:]
        previous, earlier = current, previous
    for k in range(OWN):
        for part, source in enumerate((left_ref, right_ref)):
            high, low = split(source[pl.ds(k, MODES, stride=8), :])
            high_ref[k, :, 128 * part : 128 * part + 128] = high
            low_ref[k, :, 128 * part : 128 * part + 128] = low

def spectral_kernel(in_ref, high_ref, low_ref, taps_ref, gain_ref, angle_ref, out_ref, u_ref, v_ref, f_ref):
    lane = lax.broadcasted_iota(jnp.int32, (1, 128), 1) % LAT

    def fill_edges(ref):
        for part in range(2):
            for group in range(2):
                for e in (0, 1):
                    block = pltpu.roll(ref[part, group, 2 + e], 127, 1)
                    ref[part, group, 10 + e] = jnp.where(lane == LAT - 1, 0.0, block)
                    block = pltpu.roll(ref[part, group, 8 + e], 1, 1)
                    ref[part, group, e] = jnp.where(lane == 0, 0.0, block)

    def stencil(ref, which, store):
        for group in range(2):
            for tile in range(5):
                rows = slice(8 * tile, 8 * tile + 8)
                taps = []
                for a in range(5):
                    base = (which * 5 + a) * SLICE + 8 * tile
                    taps.append(
                        [
                            taps_ref[base : base + 8, (group * 3 + kind) * 128 : (group * 3 + kind) * 128 + 128]
                            for kind in range(3)
                        ]
                    )
                real = [ref[0, group, e, rows] for e in range(12)]
                imag = [ref[1, group, e, rows] for e in range(12)]
                for e in range(ROWS):
                    total_r, total_i = real[e + 2], imag[e + 2]
                    for a in range(5):
                        r_tap, s_tap, i_tap = taps[a]
                        total_r = total_r + (r_tap * real[e + a] - i_tap * imag[e + a])
                        total_i = total_i + (s_tap * imag[e + a] + i_tap * real[e + a])
                    store(group, rows, e, total_r, total_i)

    def rows_of(start, count):
        pieces = [in_ref[pl.ds(start + n, LAT, stride=LAT_CHUNK), :] for n in range(count)]
        if count < 4:
            pieces.append(jnp.zeros((LAT * (4 - count), 128), f32))
        return jnp.concatenate(pieces, axis=0).T

    for group in range(2):
        count = min(4, OWN - 4 * group)
        for tile in range(2):
            for part in range(2):
                block = rows_of(OWN * (2 * tile + part) + 4 * group, count)
                for e in range(ROWS):
                    u_ref[part, group, 2 + e, 16 * tile : 16 * tile + 16] = block[16 * e : 16 * e + 16]
        block = rows_of(4 * OWN + 4 * group, count)
        for e in range(ROWS):
            for part in range(2):
                start = 16 * e + 8 * part
                u_ref[part, group, 2 + e, 32:40] = block[start : start + 8]
    fill_edges(u_ref)

    def keep_first(group, rows, e, total_r, total_i):
        v_ref[0, group, 2 + e, rows] = total_r
        v_ref[1, group, 2 + e, rows] = total_i

    stencil(u_ref, 0, keep_first)

    weight = angle_ref[2:3, :]
    for part in range(2):
        for group in range(2):
            halves = [
                swap_blocks([v_ref[part, group, 2 + 4 * j + e] for e in range(4)], 32) for j in range(2)
            ]
            for n in range(4):
                if 4 * group + n < OWN:
                    f_ref[4 * group + n, SLICE * part : SLICE * part + SLICE] = (
                        jnp.concatenate([halves[0][n], halves[1][n]], axis=1) * weight
                    )
    for k in range(OWN):
        table = (high_ref[k], low_ref[k])
        spectrum = dot3(split(f_ref[k]), table, ((1,), (1,)))
        gain = gain_ref[80:160] if k == 0 else gain_ref[0:80]
        f_ref[k] = dot3(split(spectrum * gain), table)
    for part in range(2):
        for group in range(2):
            rows = slice(SLICE * part, SLICE * part + SLICE)
            for j in range(2):
                values = [
                    f_ref[4 * group + n, rows, 128 * j : 128 * j + 128]
                    if 4 * group + n < OWN
                    else jnp.zeros((SLICE, 128), f32)
                    for n in range(4)
                ]
                for e, value in enumerate(swap_blocks(values, 32)):
                    v_ref[part, group, 2 + 4 * j + e] = v_ref[part, group, 2 + 4 * j + e] + value
    fill_edges(v_ref)

    def keep_second(group, rows, e, total_r, total_i):
        u_ref[0, group, 2 + e, rows] = total_r
        u_ref[1, group, 2 + e, rows] = total_i

    stencil(v_ref, 1, keep_second)

    def give(start, count, pieces):
        block = jnp.concatenate(pieces, axis=0).T
        for n in range(count):
            out_ref[pl.ds(start + n, LAT, stride=LAT_CHUNK), :] = block[LAT * n : LAT * n + LAT]

    for group in range(2):
        count = min(4, OWN - 4 * group)
        for tile in range(2):
            for part in range(2):
                give(
                    OWN * (2 * tile + part) + 4 * group,
                    count,
                    [u_ref[part, group, 2 + e, 16 * tile : 16 * tile + 16] for e in range(ROWS)],
                )
        give(
            4 * OWN + 4 * group,
            count,
            [u_ref[part, group, 2 + e, 32:40] for e in range(ROWS) for part in range(2)],
        )


def inverse_kernel(in_ref, local_ref, high_ref, low_ref, out_ref):
    totals = []
    for part in range(2):
        columns = []
        for tile, start in enumerate((OWN * part, OWN * (2 + part), 4 * OWN)):
            pieces = [in_ref[pl.ds(start + k, LAT, stride=LAT_CHUNK), :] for k in range(OWN)]
            row = LAT * part if tile < 2 else 0
            pieces.append(local_ref[row : row + LAT, 128 * tile : 128 * tile + 128])
            columns.append(jnp.concatenate(pieces + [jnp.zeros((LAT, 128), f32)], axis=0))
        x = split(jnp.concatenate(columns, axis=1))
        totals.append(dot3((high_ref[part], low_ref[part]), x))
    both = totals[0][:, :256] + totals[1][:, :256]
    g0, g1 = totals[0][:, 256:], totals[1][:, 256:]
    first = lane_slot(8) % 2 == 0
    last = jnp.where(
        first,
        g0[:256] + pltpu.roll(g1[:256], 120, 1),
        pltpu.roll(g0[256:], 8, 1) + g1[256:],
    )
    for q in range(LON):
        base = LON_CHUNK * q
        for tile in range(2):
            for half in range(2):
                row = 256 * half + 16 * q
                start = base + 28 * tile + 14 * half
                out_ref[start : start + 14] = both[row : row + 14, 128 * tile : 128 * tile + 128]
        out_ref[base + 56 : base + 72] = last[16 * q : 16 * q + 16]


def mlp_kernel(in_ref, gain_ref, up_ref, down_ref, out_hbm, x_ref, y_ref, sent):
    first = lane_slot(8) % 2 == 0
    for j in range(5):
        blocks = []
        for b in range(8):
            pair, place = divmod(8 * j + b, 5)
            even, odd = 2 * pair * LON_CHUNK, (2 * pair + 1) * LON_CHUNK
            if place == 2:
                e, o = in_ref[even + 56 : even + 70], in_ref[odd + 56 : odd + 70]
                top = jnp.where(first, e, pltpu.roll(o, 8, 1))
                bottom = jnp.where(first, pltpu.roll(e, 120, 1), o)
                blocks.append(jnp.concatenate([top, bottom], axis=0))
            else:
                base = (even, even + 28, None, odd, odd + 28)[place]
                blocks.append(in_ref[base : base + 28])
        for i, value in enumerate(swap_blocks(blocks, 16)):
            x_ref[:, i, 128 * j : 128 * j + 128] = value
    x = x_ref[...].reshape(COLS * ROWS, CHANNELS)
    average = jnp.mean(x, axis=-1, keepdims=True)
    centred = x - average
    spread = jnp.mean(centred * centred, axis=-1, keepdims=True)
    normed = (centred * lax.rsqrt(spread + 1e-05) * gain_ref[...].reshape(1, CHANNELS)).astype(bf16)
    active = []
    for n in range(5):
        hidden = dot(normed, up_ref[:, 256 * n : 256 * n + 256])
        active.append(jax.nn.gelu(hidden, approximate=True).astype(bf16))
    active = jnp.concatenate(active, axis=1)
    stores = []
    for n, (start, width) in enumerate(((0, 256), (256, 256), (512, 128))):
        lanes = pl.ds(start, width)
        total = x[:, start : start + width] + dot(active, down_ref[:, start : start + width])
        y_ref[:, :, start : start + width] = total.reshape(COLS, ROWS, width)
        stores.append(pltpu.make_async_copy(y_ref.at[:, :, lanes], out_hbm.at[:, :, lanes], sent.at[n]))
        stores[n].start()
    for store in stores:
        store.wait()


def vmem(count):
    return [pl.BlockSpec(memory_space=pltpu.VMEM)] * count


def run(kernel, shape, *operands, scratch=(), cost=(0, 0), grant=24, far=0, out=pltpu.VMEM):
    return pl.pallas_call(
        kernel,
        out_shape=jax.ShapeDtypeStruct(shape, f32),
        in_specs=vmem(len(operands) - far) + [pl.BlockSpec(memory_space=pltpu.HBM)] * far,
        out_specs=pl.BlockSpec(memory_space=out),
        scratch_shapes=list(scratch),
        compiler_params=pltpu.CompilerParams(vmem_limit_bytes=grant << 20),
        cost_estimate=pl.CostEstimate(flops=cost[0], bytes_accessed=cost[1], transcendentals=0),
    )(*operands)


def legendre(*operands):
    table = jax.ShapeDtypeStruct((OWN, MODES, NLAT), bf16)
    return pl.pallas_call(
        legendre_kernel,
        out_shape=(table, table),
        in_specs=[pl.BlockSpec(memory_space=pltpu.SMEM)] + vmem(2),
        out_specs=vmem(2),
        scratch_shapes=[pltpu.VMEM((8 * MODES, 128), f32)] * 2,
        compiler_params=pltpu.CompilerParams(vmem_limit_bytes=16 << 20),
        cost_estimate=pl.CostEstimate(flops=10**7, bytes_accessed=10**7, transcendentals=0),
    )(*operands)


def factors(*operands):
    return pl.pallas_call(
        taps_kernel,
        out_shape=tuple(jax.ShapeDtypeStruct(shape, f32) for shape in ((10 * SLICE, 768), (50, 384))),
        in_specs=vmem(4),
        out_specs=vmem(2),
        compiler_params=pltpu.CompilerParams(vmem_limit_bytes=16 << 20),
        cost_estimate=pl.CostEstimate(flops=10**7, bytes_accessed=10**7, transcendentals=0),
    )(*operands)


def own_channels(array, axis, start, odd):
    part = lax.dynamic_slice_in_dim(array, start, SLICE, axis)
    return jnp.where(odd, jnp.roll(part, -8, axis), part)


def wave_np():
    angle = 2.0 * np.pi * (MODES + np.arange(LAT)) / NLON
    waves = [np.cos(angle), np.cos(2.0 * angle), np.sin(angle), np.sin(2.0 * angle)]
    return np.repeat(np.stack(waves, axis=1), 128, axis=1).astype(np.float32)


def lanes_np():
    lane = np.arange(128)
    channel = np.concatenate([lane % 16, 16 + lane % 16, 32 + lane % 8])
    return (np.arange(SLICE)[:, None] == channel[None, :]).astype(np.float32)


def exchange(array, axis, count):
    rows = array.shape[0] // count
    shape = (count, rows, 128) if rows % 8 == 0 else (count, 1, rows * 128)
    moved = lax.all_to_all(array.reshape(shape), axis, split_axis=0, concat_axis=0, tiled=True)
    return moved.reshape(array.shape)


def per_device(latent, conv_first, conv_second, filter_gains, norm_gain, up_weight, down_weight):
    band = lax.axis_index("lat")
    sector = lax.axis_index("lon")
    odd = sector % 2 == 1
    forward, inverse = fourier_np()
    forward, inverse = split_np(forward), split_np(inverse)
    angles = jnp.asarray(latitude_np())

    packed = run(
        pack_kernel,
        (LON * LON_CHUNK, 128),
        latent.transpose(1, 0, 2),
        scratch=[
            pltpu.VMEM((COLS, ROWS, CHANNELS), f32),
            pltpu.VMEM((LON * LON_CHUNK, 128), f32),
            pltpu.SemaphoreType.DMA((5,)),
            pltpu.SemaphoreType.DMA((8,)),
        ],
        far=1,
        grant=60,
        out=pltpu.HBM,
    )
    circles = exchange(packed, "lon", LON)

    seeds = lax.dynamic_index_in_dim(jnp.asarray(seed_np()), band, 0, False)
    owner = band.astype(jnp.int32).reshape(1)
    high, low = legendre(owner, angles, seeds)
    gains = own_channels(filter_gains, 1, 0, odd).T
    gains = jnp.concatenate([gains, gains, gains, jnp.where(band == 0, 0.0, gains)], axis=0)

    circles, high, low = lax.optimization_barrier((circles, high, low))

    shapes = ((LAT * LAT_CHUNK, 128), (2 * LAT, 384), (3 * LAT, 128), (3 * LAT, 128))
    coeffs, local, up, down = pl.pallas_call(
        forward_kernel,
        out_shape=tuple(jax.ShapeDtypeStruct(shape, f32) for shape in shapes),
        in_specs=vmem(3),
        out_specs=vmem(4),
        compiler_params=pltpu.CompilerParams(vmem_limit_bytes=24 << 20),
    )(circles, *map(jnp.asarray, forward))
    orders = exchange(coeffs, "lat", LAT)
    local, conv_first, conv_second = lax.optimization_barrier((local, conv_first, conv_second))
    phases = lax.dynamic_index_in_dim(jnp.asarray(phase_np()), band, 0, False)
    own_taps = jnp.stack([conv_first, conv_second]).reshape(2, 5, 5, CHANNELS)
    own_taps = own_channels(own_taps, 3, sector * SLICE, odd)
    taps, lane_taps = factors(
        own_taps.transpose(0, 1, 3, 2).reshape(10 * SLICE, 5),
        phases,
        own_taps.reshape(50, SLICE),
        jnp.asarray(lanes_np()),
    )
    rising = [(n, n + 1) for n in range(LAT - 1)]
    below = lax.ppermute(up, "lat", rising)
    above = lax.ppermute(down, "lat", [(target, source) for source, target in rising])
    stay = pl.pallas_call(
        local_kernel,
        out_shape=jax.ShapeDtypeStruct((2 * LAT, 384), f32),
        in_specs=[pl.BlockSpec(memory_space=pltpu.SMEM)] + vmem(5),
        out_specs=vmem(1)[0],
        compiler_params=pltpu.CompilerParams(vmem_limit_bytes=16 << 20),
        cost_estimate=pl.CostEstimate(flops=10**7, bytes_accessed=10**6, transcendentals=0),
    )(owner, local, below, above, lane_taps, jnp.asarray(wave_np()))
    orders, stay, taps = lax.optimization_barrier((orders, stay, taps))
    state = pltpu.VMEM((2, 2, 12, SLICE, 128), f32)
    third = run(
        spectral_kernel,
        (LAT * LAT_CHUNK, 128),
        orders,
        high,
        low,
        taps,
        gains,
        angles,
        scratch=[state, state, pltpu.VMEM((OWN, 2 * SLICE, NLAT), f32)],
    )
    returned = exchange(third, "lat", LAT)
    restored = run(inverse_kernel, (LON * LON_CHUNK, 128), returned, stay, *map(jnp.asarray, inverse))
    arrived = exchange(restored, "lon", LON)
    result = run(
        mlp_kernel,
        (COLS, ROWS, CHANNELS),
        arrived,
        norm_gain,
        up_weight,
        down_weight,
        scratch=[
            pltpu.VMEM((COLS, ROWS, CHANNELS), f32),
            pltpu.VMEM((COLS, ROWS, CHANNELS), f32),
            pltpu.SemaphoreType.DMA((3,)),
        ],
        out=pltpu.HBM,
    )
    return result.transpose(1, 0, 2)


def solution(mesh):
    return jax.shard_map(
        per_device,
        mesh=mesh,
        in_specs=(P("lat", "lon", None), P(), P(), P(None, "lon"), P(), P(), P()),
        out_specs=P("lat", "lon", None),
        check_vma=False,
    )
```

```python
import math

import jax
import jax.numpy as jnp
import numpy as np
from jax import lax
from jax.experimental import pallas as pl
from jax.experimental.pallas import tpu as pltpu
from jax.sharding import PartitionSpec as P

ROWS, COLS, CHANNELS, HIDDEN = 8, 28, 640, 1280
LAT, LON, SLICE = 32, 16, 40
NLAT, NLON, MODES = 256, 448, 192
OWN = MODES // LAT
KEPT = OWN + 1
LON_CHUNK = 70
LAT_CHUNK = 30
f32, bf16 = jnp.float32, jnp.bfloat16


def split_np(table):
    high = table.astype(np.float32).astype(jnp.bfloat16)
    low = (table - high.astype(np.float64)).astype(np.float32).astype(jnp.bfloat16)
    return high, low


def order_of(owner, slot):
    return owner * OWN + slot if slot < OWN else MODES + owner


def fourier_np():
    half, sector, step = np.meshgrid(np.arange(2), np.arange(LON), np.arange(16), indexing="ij")
    place = (sector * COLS + half * 14 + step).reshape(-1)
    valid = (step < 14).reshape(-1)
    forward = np.zeros((2, KEPT, LAT, 512))
    inverse = np.zeros((2, 512, 8, LAT))
    for slot in range(KEPT):
        for owner in range(LAT):
            order = order_of(owner, slot)
            angle = 2.0 * np.pi * ((order * place) % NLON) / NLON
            double = 1.0 if order == 0 else 2.0
            real, imag = np.cos(angle), -np.sin(angle)
            if order == 0:
                imag = np.cos(np.pi * (place % 2))
            forward[0, slot, owner] = real / NLON * valid
            forward[1, slot, owner] = imag / NLON * valid
            inverse[0, :, slot, owner] = real * double * valid
            inverse[1, :, slot, owner] = imag * double * valid
    return forward.reshape(2 * KEPT * LAT, 512), inverse.reshape(2, 512, 8 * LAT)


FACTOR_TILES = ((0, 1, 2), (3, 3, 4))


def phase_np():
    table = np.zeros((LAT, 8, 5, 4))
    for owner in range(LAT):
        for slot in range(OWN):
            order = order_of(owner, slot)
            real, second, imag = FACTOR_TILES[slot // 4]
            for b in range(-2, 3):
                angle = 2.0 * np.pi * ((order * b) % NLON) / NLON
                table[owner, b + 2, real, slot % 4] = np.cos(angle)
                if second != real:
                    table[owner, b + 2, second, slot % 4] = np.cos(np.pi * b) if order == 0 else np.cos(angle)
                table[owner, b + 2, imag, slot % 4] = np.sin(angle)
    return table.reshape(LAT, 8, 20).astype(np.float32)


def latitude_np():
    e, q = np.meshgrid(np.arange(ROWS), np.arange(LAT), indexing="ij")
    theta = np.pi * ((q * ROWS + e).reshape(-1) + 0.5) / NLAT
    weight = 2.0 * np.pi * np.pi * np.sin(theta) / NLAT
    rows = np.stack([np.cos(theta), np.log(np.sin(theta)), weight])
    return np.concatenate([rows, np.zeros((5, NLAT))]).astype(np.float32)


def seed_np():
    seeds = np.zeros((LAT, 8, 128), np.float32)
    for m in range(MODES):
        value = 0.5 * (
            math.log((2 * m + 1) / (4 * math.pi))
            + math.lgamma(2 * m + 1)
            - 2 * m * math.log(2)
            - 2 * math.lgamma(m + 1)
        )
        seeds[m // OWN, m % OWN] = value
    return seeds


def lane_slot(width):
    return lax.broadcasted_iota(jnp.int32, (1, 128), 1) // width


def swap_blocks(values, width):
    values = list(values)
    step = len(values) // 2
    while step:
        shift = step * width
        first = lane_slot(shift) % 2 == 0
        for a in range(len(values)):
            if not a & step:
                low, high = values[a], values[a | step]
                values[a] = jnp.where(first, low, pltpu.roll(high, shift, 1))
                values[a | step] = jnp.where(first, pltpu.roll(low, 128 - shift, 1), high)
        step //= 2
    return values


def split(value):
    high = value.astype(bf16)
    return high, (value - high.astype(f32)).astype(bf16)


def dot(a, b, dims=((1,), (0,))):
    return lax.dot_general(a, b, (dims, ((), ())), preferred_element_type=f32)


def dot3(a, b, dims=((1,), (0,))):
    return dot(a[0], b[0], dims) + (dot(a[1], b[0], dims) + dot(a[0], b[1], dims))


def pack_kernel(x_hbm, out_hbm, x_ref, out_ref, arrivals, sent):
    first = lane_slot(8) % 2 == 0
    fetches = []
    for j in range(5):
        lanes = pl.ds(128 * j, 128)
        fetches.append(pltpu.make_async_copy(x_hbm.at[:, :, lanes], x_ref.at[:, :, lanes], arrivals.at[j]))
        fetches[j].start()
    stores = []
    for j in range(5):
        fetches[j].wait()
        blocks = swap_blocks([x_ref[:, i, 128 * j : 128 * j + 128] for i in range(ROWS)], 16)
        for b in range(8):
            pair, place = divmod(8 * j + b, 5)
            even, odd = 2 * pair * LON_CHUNK, (2 * pair + 1) * LON_CHUNK
            block = blocks[b]
            if place == 2:
                top, bottom = block[:14], block[14:]
                out_ref[even + 56 : even + 70] = jnp.where(first, top, pltpu.roll(bottom, 8, 1))
                out_ref[odd + 56 : odd + 70] = jnp.where(first, pltpu.roll(top, 120, 1), bottom)
            else:
                base = (even, even + 28, None, odd, odd + 28)[place]
                out_ref[base : base + 28] = block
            if place == 4 and pair % 2:
                rows = pl.ds(even - 2 * LON_CHUNK, 4 * LON_CHUNK)
                stores.append(pltpu.make_async_copy(out_ref.at[rows], out_hbm.at[rows], sent.at[pair // 2]))
                stores[-1].start()
    for store in stores:
        store.wait()


def forward_kernel(in_ref, high_ref, low_ref, out_ref, local_ref, up_ref, down_ref):
    totals = []
    for half in range(2):
        pieces = []
        for start in (14 * half, 28 + 14 * half, 56):
            blocks = [in_ref[LON_CHUNK * q + start : LON_CHUNK * q + start + 16] for q in range(LON - 1)]
            tail = LON_CHUNK * (LON - 1) + start
            blocks += [in_ref[tail : tail + 14], jnp.zeros((2, 128), f32)]
            pieces.append(jnp.concatenate(blocks, axis=0))
        x = split(jnp.concatenate(pieces, axis=1))
        lanes = slice(256 * half, 256 * half + 256)
        totals.append(dot3((high_ref[:, lanes], low_ref[:, lanes]), x))
    both = totals[0][:, :256] + totals[1][:, :256]
    g0, g1 = totals[0][:, 256:], totals[1][:, 256:]
    half_rows = KEPT * LAT
    first = lane_slot(8) % 2 == 0
    last = jnp.where(
        first,
        g0[:half_rows] + pltpu.roll(g1[:half_rows], 120, 1),
        pltpu.roll(g0[half_rows:], 8, 1) + g1[half_rows:],
    )
    for r in range(2):
        for k in range(OWN):
            part = both[LAT * (KEPT * r + k) : LAT * (KEPT * r + k) + LAT]
            row = OWN * r + k
            out_ref[pl.ds(row, LAT, stride=LAT_CHUNK), :] = part[:, :128]
            out_ref[pl.ds(2 * OWN + row, LAT, stride=LAT_CHUNK), :] = part[:, 128:]
    for k in range(OWN):
        out_ref[pl.ds(4 * OWN + k, LAT, stride=LAT_CHUNK), :] = last[LAT * k : LAT * k + LAT]
    left = lane_slot(64) == 0
    for r in range(2):
        part = both[LAT * (KEPT * r + OWN) : LAT * (KEPT * r + OWN) + LAT]
        a, b = part[:, :128], part[:, 128:]
        rows = slice(LAT * r, LAT * r + LAT)
        local_ref[rows, :128] = a
        local_ref[rows, 128:256] = b
        up_ref[rows] = jnp.where(left, pltpu.roll(a, 64, 1), b)
        down_ref[rows] = jnp.where(left, a, pltpu.roll(b, 64, 1))
    part = last[LAT * OWN : LAT * OWN + LAT]
    local_ref[0:LAT, 256:] = part
    local_ref[LAT:, 256:] = jnp.zeros((LAT, 128), f32)
    up_ref[2 * LAT :] = part
    down_ref[2 * LAT :] = part


def local_kernel(band_ref, own_ref, below_ref, above_ref, taps_ref, wave_ref, out_ref):
    lane = lax.broadcasted_iota(jnp.int32, (1, 128), 1)
    left = lane < 64
    south = jnp.where(band_ref[0] == 0, 0.0, 1.0)
    north = jnp.where(band_ref[0] == LAT - 1, 0.0, 1.0)
    masks = (jnp.where(left, south, 1.0), jnp.where(left, 1.0, north))

    def extend(own, below, above):
        turned = pltpu.roll(own, 64, 1)
        return jnp.where(left, below, turned), jnp.where(left, turned, above)

    def turn(value):
        return pltpu.roll(value, 64, 1)

    def shifted(tiles, a):
        if a == 0:
            return tiles
        amount = (-16 * a) % 128
        first, second = (pltpu.roll(tile, amount, 1) for tile in tiles)
        if a > 0:
            keep = lane < 128 - 16 * a
            return jnp.where(keep, first, second), jnp.where(keep, second, first)
        keep = lane >= -16 * a
        return jnp.where(keep, first, second), jnp.where(keep, second, first)

    def weights(which, a, tile):
        rows = [taps_ref[(which * 5 + a) * 5 + b : (which * 5 + a) * 5 + b + 1, 128 * tile : 128 * tile + 128] for b in range(5)]
        cos1, cos2, sin1, sin2 = (wave_ref[:, 128 * n : 128 * n + 128] for n in range(4))
        real = rows[2] + (rows[3] + rows[1]) * cos1 + (rows[4] + rows[0]) * cos2
        imag = (rows[3] - rows[1]) * sin1 + (rows[4] - rows[0]) * sin2
        return real, imag

    for tile in range(2):
        parts = []
        for r in range(2):
            rows = slice(LAT * r, LAT * r + LAT)
            own = own_ref[rows, 128 * tile : 128 * tile + 128]
            below, above = below_ref[rows], above_ref[rows]
            if tile == 0:
                parts.append(extend(own, below, turn(above)))
            else:
                parts.append(extend(own, turn(below), above))
        for which in range(2):
            real, imag = [list(value) for value in parts]
            for a in range(-2, 3):
                w_r, w_i = weights(which, a + 2, tile)
                e_r, e_i = shifted(parts[0], a), shifted(parts[1], a)
                for n in range(2):
                    real[n] = real[n] + (w_r * e_r[n] - w_i * e_i[n])
                    imag[n] = imag[n] + (w_r * e_i[n] + w_i * e_r[n])
            parts = [tuple(v * m for v, m in zip(value, masks)) for value in (real, imag)]
        for r in range(2):
            result = jnp.where(left, turn(parts[r][0]), turn(parts[r][1]))
            out_ref[LAT * r : LAT * r + LAT, 128 * tile : 128 * tile + 128] = result
    second = lane_slot(8) % 2 == 1
    value = extend(own_ref[0:LAT, 256:], turn(below_ref[2 * LAT :]), turn(above_ref[2 * LAT :]))
    for which in range(2):
        total = list(value)
        swapped = [jnp.where(second, pltpu.roll(v, 8, 1), pltpu.roll(v, 120, 1)) for v in value]
        for a in range(-2, 3):
            w_r, w_i = weights(which, a + 2, 2)
            w_i = jnp.where(second, w_i, -w_i)
            e, f = shifted(value, a), shifted(swapped, a)
            for n in range(2):
                total[n] = total[n] + (w_r * e[n] + w_i * f[n])
        value = tuple(v * m for v, m in zip(total, masks))
    out_ref[0:LAT, 256:] = jnp.where(left, turn(value[0]), turn(value[1]))
    out_ref[LAT:, 256:] = jnp.zeros((LAT, 128), f32)


def taps_kernel(rows_ref, phase_ref, plain_ref, lanes_ref, taps_ref, spread_ref):
    spread_ref[...] = jnp.dot(plain_ref[...], lanes_ref[...], precision=lax.Precision.HIGHEST)
    for tile in range(5):
        phase = phase_ref[:, 4 * tile : 4 * tile + 1]
        for n in range(1, 4):
            column = phase_ref[:, 4 * tile + n : 4 * tile + n + 1]
            phase = jnp.where(lane_slot(LAT) >= n, column, phase)
        total = rows_ref[:, 0:1] * phase[0:1]
        for b in range(1, 5):
            total = total + rows_ref[:, b : b + 1] * phase[b : b + 1]
        taps_ref[:, 128 * tile : 128 * tile + 128] = total


def legendre_kernel(owner_ref, angle_ref, seed_ref, high_ref, low_ref, left_ref, right_ref):
    slot = lax.broadcasted_iota(jnp.int32, (8, 256), 0)
    order_at = jnp.where(slot < OWN, owner_ref[0] * OWN + slot, 2 * MODES)
    order = order_at.astype(f32)
    degree = lax.broadcasted_iota(jnp.int32, (8, 256), 1).astype(f32)
    square, below = degree * degree, (degree - 1.0) * (degree - 1.0)
    upper = jnp.sqrt(
        jnp.maximum(4.0 * square - 1.0, 1.0) / jnp.maximum(square - order * order, 1.0)
    )
    lower = jnp.sqrt(
        jnp.maximum(below - order * order, 0.0) / jnp.maximum(4.0 * below - 1.0, 1.0)
    )
    product = upper * lower
    cosine = jnp.broadcast_to(angle_ref[0:1, :], (8, 256))
    diagonal = jnp.exp(seed_ref[:, 0:1] + order * angle_ref[1:2, :])
    previous = jnp.zeros((8, 256), f32)
    earlier = previous
    for l in range(MODES):
        current = jnp.where(
            order_at == l,
            diagonal,
            (upper[:, l : l + 1] * cosine) * previous - product[:, l : l + 1] * earlier,
        )
        left_ref[8 * l : 8 * l + 8] = current[:, :128]
        right_ref[8 * l : 8 * l + 8] = current[:, 128:]
        previous, earlier = current, previous
    for k in range(OWN):
        for part, source in enumerate((left_ref, right_ref)):
            high, low = split(source[pl.ds(k, MODES, stride=8), :])
            high_ref[k, :, 128 * part : 128 * part + 128] = high
            low_ref[k, :, 128 * part : 128 * part + 128] = low

def spectral_kernel(in_ref, high_ref, low_ref, taps_ref, gain_ref, angle_ref, out_ref, u_ref, v_ref, f_ref):
    lane = lax.broadcasted_iota(jnp.int32, (1, 128), 1) % LAT

    def fill_edges(ref):
        for part in range(2):
            for group in range(2):
                for e in (0, 1):
                    block = pltpu.roll(ref[part, group, 2 + e], 127, 1)
                    ref[part, group, 10 + e] = jnp.where(lane == LAT - 1, 0.0, block)
                    block = pltpu.roll(ref[part, group, 8 + e], 1, 1)
                    ref[part, group, e] = jnp.where(lane == 0, 0.0, block)

    def stencil(ref, which, store):
        for group in range(2):
            for tile in range(5):
                rows = slice(8 * tile, 8 * tile + 8)
                taps = []
                for a in range(5):
                    base = (which * 5 + a) * SLICE + 8 * tile
                    taps.append(
                        [
                            taps_ref[base : base + 8, 128 * column : 128 * column + 128]
                            for column in FACTOR_TILES[group]
                        ]
                    )
                real = [ref[0, group, e, rows] for e in range(12)]
                imag = [ref[1, group, e, rows] for e in range(12)]
                for e in range(ROWS):
                    total_r, total_i = real[e + 2], imag[e + 2]
                    for a in range(5):
                        r_tap, s_tap, i_tap = taps[a]
                        total_r = total_r + (r_tap * real[e + a] - i_tap * imag[e + a])
                        total_i = total_i + (s_tap * imag[e + a] + i_tap * real[e + a])
                    store(group, rows, e, total_r, total_i)

    def rows_of(start, count):
        pieces = [in_ref[pl.ds(start + n, LAT, stride=LAT_CHUNK), :] for n in range(count)]
        if count < 4:
            pieces.append(jnp.zeros((LAT * (4 - count), 128), f32))
        return jnp.concatenate(pieces, axis=0).T

    for group in range(2):
        count = min(4, OWN - 4 * group)
        for tile in range(2):
            for part in range(2):
                block = rows_of(OWN * (2 * tile + part) + 4 * group, count)
                for e in range(ROWS):
                    u_ref[part, group, 2 + e, 16 * tile : 16 * tile + 16] = block[16 * e : 16 * e + 16]
        block = rows_of(4 * OWN + 4 * group, count)
        for e in range(ROWS):
            for part in range(2):
                start = 16 * e + 8 * part
                u_ref[part, group, 2 + e, 32:40] = block[start : start + 8]
    fill_edges(u_ref)

    def keep_first(group, rows, e, total_r, total_i):
        v_ref[0, group, 2 + e, rows] = total_r
        v_ref[1, group, 2 + e, rows] = total_i

    stencil(u_ref, 0, keep_first)

    weight = angle_ref[2:3, :]
    for part in range(2):
        for group in range(2):
            halves = [
                swap_blocks([v_ref[part, group, 2 + 4 * j + e] for e in range(4)], 32) for j in range(2)
            ]
            for n in range(4):
                if 4 * group + n < OWN:
                    f_ref[4 * group + n, SLICE * part : SLICE * part + SLICE] = (
                        jnp.concatenate([halves[0][n], halves[1][n]], axis=1) * weight
                    )
    for k in range(OWN):
        table = (high_ref[k], low_ref[k])
        spectrum = dot3(split(f_ref[k]), table, ((1,), (1,)))
        gain = gain_ref[80:160] if k == 0 else gain_ref[0:80]
        f_ref[k] = dot3(split(spectrum * gain), table)
    for part in range(2):
        for group in range(2):
            rows = slice(SLICE * part, SLICE * part + SLICE)
            for j in range(2):
                values = [
                    f_ref[4 * group + n, rows, 128 * j : 128 * j + 128]
                    if 4 * group + n < OWN
                    else jnp.zeros((SLICE, 128), f32)
                    for n in range(4)
                ]
                for e, value in enumerate(swap_blocks(values, 32)):
                    v_ref[part, group, 2 + 4 * j + e] = v_ref[part, group, 2 + 4 * j + e] + value
    fill_edges(v_ref)

    def keep_second(group, rows, e, total_r, total_i):
        u_ref[0, group, 2 + e, rows] = total_r
        u_ref[1, group, 2 + e, rows] = total_i

    stencil(v_ref, 1, keep_second)

    def give(start, count, pieces):
        block = jnp.concatenate(pieces, axis=0).T
        for n in range(count):
            out_ref[pl.ds(start + n, LAT, stride=LAT_CHUNK), :] = block[LAT * n : LAT * n + LAT]

    for group in range(2):
        count = min(4, OWN - 4 * group)
        for tile in range(2):
            for part in range(2):
                give(
                    OWN * (2 * tile + part) + 4 * group,
                    count,
                    [u_ref[part, group, 2 + e, 16 * tile : 16 * tile + 16] for e in range(ROWS)],
                )
        give(
            4 * OWN + 4 * group,
            count,
            [u_ref[part, group, 2 + e, 32:40] for e in range(ROWS) for part in range(2)],
        )


def inverse_kernel(in_ref, local_ref, high_ref, low_ref, out_ref):
    totals = []
    for part in range(2):
        columns = []
        for tile, start in enumerate((OWN * part, OWN * (2 + part), 4 * OWN)):
            pieces = [in_ref[pl.ds(start + k, LAT, stride=LAT_CHUNK), :] for k in range(OWN)]
            row = LAT * part if tile < 2 else 0
            pieces.append(local_ref[row : row + LAT, 128 * tile : 128 * tile + 128])
            columns.append(jnp.concatenate(pieces + [jnp.zeros((LAT, 128), f32)], axis=0))
        x = split(jnp.concatenate(columns, axis=1))
        totals.append(dot3((high_ref[part], low_ref[part]), x))
    both = totals[0][:, :256] + totals[1][:, :256]
    g0, g1 = totals[0][:, 256:], totals[1][:, 256:]
    first = lane_slot(8) % 2 == 0
    last = jnp.where(
        first,
        g0[:256] + pltpu.roll(g1[:256], 120, 1),
        pltpu.roll(g0[256:], 8, 1) + g1[256:],
    )
    for q in range(LON):
        base = LON_CHUNK * q
        for tile in range(2):
            for half in range(2):
                row = 256 * half + 16 * q
                start = base + 28 * tile + 14 * half
                out_ref[start : start + 14] = both[row : row + 14, 128 * tile : 128 * tile + 128]
        out_ref[base + 56 : base + 70] = last[16 * q : 16 * q + 14]


def mlp_kernel(in_ref, gain_ref, up_ref, down_ref, out_hbm, x_ref, y_ref, sent):
    first = lane_slot(8) % 2 == 0
    for j in range(5):
        blocks = []
        for b in range(8):
            pair, place = divmod(8 * j + b, 5)
            even, odd = 2 * pair * LON_CHUNK, (2 * pair + 1) * LON_CHUNK
            if place == 2:
                e, o = in_ref[even + 56 : even + 70], in_ref[odd + 56 : odd + 70]
                top = jnp.where(first, e, pltpu.roll(o, 8, 1))
                bottom = jnp.where(first, pltpu.roll(e, 120, 1), o)
                blocks.append(jnp.concatenate([top, bottom], axis=0))
            else:
                base = (even, even + 28, None, odd, odd + 28)[place]
                blocks.append(in_ref[base : base + 28])
        for i, value in enumerate(swap_blocks(blocks, 16)):
            x_ref[:, i, 128 * j : 128 * j + 128] = value
    x = x_ref[...].reshape(COLS * ROWS, CHANNELS)
    average = jnp.mean(x, axis=-1, keepdims=True)
    centred = x - average
    spread = jnp.mean(centred * centred, axis=-1, keepdims=True)
    normed = (centred * lax.rsqrt(spread + 1e-05) * gain_ref[...].reshape(1, CHANNELS)).astype(bf16)
    active = []
    for n in range(5):
        hidden = dot(normed, up_ref[:, 256 * n : 256 * n + 256])
        active.append(jax.nn.gelu(hidden, approximate=True).astype(bf16))
    active = jnp.concatenate(active, axis=1)
    stores = []
    for n, (start, width) in enumerate(((0, 256), (256, 256), (512, 128))):
        lanes = pl.ds(start, width)
        total = x[:, start : start + width] + dot(active, down_ref[:, start : start + width])
        y_ref[:, :, start : start + width] = total.reshape(COLS, ROWS, width)
        stores.append(pltpu.make_async_copy(y_ref.at[:, :, lanes], out_hbm.at[:, :, lanes], sent.at[n]))
        stores[n].start()
    for store in stores:
        store.wait()


def vmem(count):
    return [pl.BlockSpec(memory_space=pltpu.VMEM)] * count


def run(kernel, shape, *operands, scratch=(), cost=(0, 0), grant=24, far=0, out=pltpu.VMEM):
    return pl.pallas_call(
        kernel,
        out_shape=jax.ShapeDtypeStruct(shape, f32),
        in_specs=vmem(len(operands) - far) + [pl.BlockSpec(memory_space=pltpu.HBM)] * far,
        out_specs=pl.BlockSpec(memory_space=out),
        scratch_shapes=list(scratch),
        compiler_params=pltpu.CompilerParams(vmem_limit_bytes=grant << 20),
        cost_estimate=pl.CostEstimate(flops=cost[0], bytes_accessed=cost[1], transcendentals=0),
    )(*operands)


def legendre(*operands):
    table = jax.ShapeDtypeStruct((OWN, MODES, NLAT), bf16)
    return pl.pallas_call(
        legendre_kernel,
        out_shape=(table, table),
        in_specs=[pl.BlockSpec(memory_space=pltpu.SMEM)] + vmem(2),
        out_specs=vmem(2),
        scratch_shapes=[pltpu.VMEM((8 * MODES, 128), f32)] * 2,
        compiler_params=pltpu.CompilerParams(vmem_limit_bytes=16 << 20),
        cost_estimate=pl.CostEstimate(flops=10**7, bytes_accessed=10**7, transcendentals=0),
    )(*operands)


def factors(*operands):
    return pl.pallas_call(
        taps_kernel,
        out_shape=tuple(jax.ShapeDtypeStruct(shape, f32) for shape in ((10 * SLICE, 640), (50, 384))),
        in_specs=vmem(4),
        out_specs=vmem(2),
        compiler_params=pltpu.CompilerParams(vmem_limit_bytes=16 << 20),
        cost_estimate=pl.CostEstimate(flops=10**7, bytes_accessed=10**7, transcendentals=0),
    )(*operands)


def own_channels(array, axis, start, odd):
    part = lax.dynamic_slice_in_dim(array, start, SLICE, axis)
    return jnp.where(odd, jnp.roll(part, -8, axis), part)


def wave_np():
    angle = 2.0 * np.pi * (MODES + np.arange(LAT)) / NLON
    waves = [np.cos(angle), np.cos(2.0 * angle), np.sin(angle), np.sin(2.0 * angle)]
    return np.repeat(np.stack(waves, axis=1), 128, axis=1).astype(np.float32)


def lanes_np():
    lane = np.arange(128)
    channel = np.concatenate([lane % 16, 16 + lane % 16, 32 + lane % 8])
    return (np.arange(SLICE)[:, None] == channel[None, :]).astype(np.float32)


def exchange(array, axis, count):
    rows = array.shape[0] // count
    shape = (count, rows, 128) if rows % 8 == 0 else (count, 1, rows * 128)
    moved = lax.all_to_all(array.reshape(shape), axis, split_axis=0, concat_axis=0, tiled=True)
    return moved.reshape(array.shape)


def per_device(latent, conv_first, conv_second, filter_gains, norm_gain, up_weight, down_weight):
    band = lax.axis_index("lat")
    sector = lax.axis_index("lon")
    odd = sector % 2 == 1
    forward, inverse = fourier_np()
    forward, inverse = split_np(forward), split_np(inverse)
    angles = jnp.asarray(latitude_np())

    packed = run(
        pack_kernel,
        (LON * LON_CHUNK, 128),
        latent.transpose(1, 0, 2),
        scratch=[
            pltpu.VMEM((COLS, ROWS, CHANNELS), f32),
            pltpu.VMEM((LON * LON_CHUNK, 128), f32),
            pltpu.SemaphoreType.DMA((5,)),
            pltpu.SemaphoreType.DMA((4,)),
        ],
        far=1,
        grant=60,
        out=pltpu.HBM,
    )
    circles = exchange(packed, "lon", LON)

    seeds = lax.dynamic_index_in_dim(jnp.asarray(seed_np()), band, 0, False)
    owner = band.astype(jnp.int32).reshape(1)
    high, low = legendre(owner, angles, seeds)
    gains = own_channels(filter_gains, 1, 0, odd).T
    gains = jnp.concatenate([gains, gains, gains, jnp.where(band == 0, 0.0, gains)], axis=0)

    circles, high, low = lax.optimization_barrier((circles, high, low))

    shapes = ((LAT * LAT_CHUNK, 128), (2 * LAT, 384), (3 * LAT, 128), (3 * LAT, 128))
    coeffs, local, up, down = pl.pallas_call(
        forward_kernel,
        out_shape=tuple(jax.ShapeDtypeStruct(shape, f32) for shape in shapes),
        in_specs=vmem(3),
        out_specs=vmem(4),
        compiler_params=pltpu.CompilerParams(vmem_limit_bytes=24 << 20),
    )(circles, *map(jnp.asarray, forward))
    orders = exchange(coeffs, "lat", LAT)
    local, conv_first, conv_second = lax.optimization_barrier((local, conv_first, conv_second))
    phases = lax.dynamic_index_in_dim(jnp.asarray(phase_np()), band, 0, False)
    own_taps = jnp.stack([conv_first, conv_second]).reshape(2, 5, 5, CHANNELS)
    own_taps = own_channels(own_taps, 3, sector * SLICE, odd)
    taps, lane_taps = factors(
        own_taps.transpose(0, 1, 3, 2).reshape(10 * SLICE, 5),
        phases,
        own_taps.reshape(50, SLICE),
        jnp.asarray(lanes_np()),
    )
    rising = [(n, n + 1) for n in range(LAT - 1)]
    below = lax.ppermute(up, "lat", rising)
    above = lax.ppermute(down, "lat", [(target, source) for source, target in rising])
    stay = pl.pallas_call(
        local_kernel,
        out_shape=jax.ShapeDtypeStruct((2 * LAT, 384), f32),
        in_specs=[pl.BlockSpec(memory_space=pltpu.SMEM)] + vmem(5),
        out_specs=vmem(1)[0],
        compiler_params=pltpu.CompilerParams(vmem_limit_bytes=16 << 20),
        cost_estimate=pl.CostEstimate(flops=10**7, bytes_accessed=10**6, transcendentals=0),
    )(owner, local, below, above, lane_taps, jnp.asarray(wave_np()))
    orders, taps = lax.optimization_barrier((orders, taps))
    state = pltpu.VMEM((2, 2, 12, SLICE, 128), f32)
    third = run(
        spectral_kernel,
        (LAT * LAT_CHUNK, 128),
        orders,
        high,
        low,
        taps,
        gains,
        angles,
        scratch=[state, state, pltpu.VMEM((OWN, 2 * SLICE, NLAT), f32)],
    )
    returned = exchange(third, "lat", LAT)
    restored = run(inverse_kernel, (LON * LON_CHUNK, 128), returned, stay, *map(jnp.asarray, inverse))
    arrived = exchange(restored, "lon", LON)
    result = run(
        mlp_kernel,
        (COLS, ROWS, CHANNELS),
        arrived,
        norm_gain,
        up_weight,
        down_weight,
        scratch=[
            pltpu.VMEM((COLS, ROWS, CHANNELS), f32),
            pltpu.VMEM((COLS, ROWS, CHANNELS), f32),
            pltpu.SemaphoreType.DMA((3,)),
        ],
        out=pltpu.HBM,
    )
    return result.transpose(1, 0, 2)


def solution(mesh):
    return jax.shard_map(
        per_device,
        mesh=mesh,
        in_specs=(P("lat", "lon", None), P(), P(), P(None, "lon"), P(), P(), P()),
        out_specs=P("lat", "lon", None),
        check_vma=False,
    )
```

```python
import math

import jax
import jax.numpy as jnp
import numpy as np
from jax import lax
from jax.experimental import pallas as pl
from jax.experimental.pallas import tpu as pltpu
from jax.sharding import PartitionSpec as P

ROWS, COLS, CHANNELS, HIDDEN = 8, 28, 640, 1280
LAT, LON, SLICE = 32, 16, 40
NLAT, NLON, MODES = 256, 448, 192
OWN = MODES // LAT
KEPT = OWN + 1
LON_CHUNK = 70
LAT_CHUNK = 30
f32, bf16 = jnp.float32, jnp.bfloat16


def split_np(table):
    high = table.astype(np.float32).astype(jnp.bfloat16)
    low = (table - high.astype(np.float64)).astype(np.float32).astype(jnp.bfloat16)
    return high, low


def order_of(owner, slot):
    return owner * OWN + slot if slot < OWN else MODES + owner


def fourier_np():
    half, sector, step = np.meshgrid(np.arange(2), np.arange(LON), np.arange(16), indexing="ij")
    place = (sector * COLS + half * 14 + step).reshape(-1)
    valid = (step < 14).reshape(-1)
    forward = np.zeros((2, KEPT, LAT, 512))
    inverse = np.zeros((2, 512, 8, LAT))
    for slot in range(KEPT):
        for owner in range(LAT):
            order = order_of(owner, slot)
            angle = 2.0 * np.pi * ((order * place) % NLON) / NLON
            double = 1.0 if order == 0 else 2.0
            real, imag = np.cos(angle), -np.sin(angle)
            if order == 0:
                imag = np.cos(np.pi * (place % 2))
            forward[0, slot, owner] = real / NLON * valid
            forward[1, slot, owner] = imag / NLON * valid
            inverse[0, :, slot, owner] = real * double * valid
            inverse[1, :, slot, owner] = imag * double * valid
    return forward.reshape(2 * KEPT * LAT, 512), inverse.reshape(2, 512, 8 * LAT)


FACTOR_TILES = ((0, 1, 2), (3, 3, 4))


def phase_np():
    table = np.zeros((LAT, 8, 5, 4))
    for owner in range(LAT):
        for slot in range(OWN):
            order = order_of(owner, slot)
            real, second, imag = FACTOR_TILES[slot // 4]
            for b in range(-2, 3):
                angle = 2.0 * np.pi * ((order * b) % NLON) / NLON
                table[owner, b + 2, real, slot % 4] = np.cos(angle)
                if second != real:
                    table[owner, b + 2, second, slot % 4] = np.cos(np.pi * b) if order == 0 else np.cos(angle)
                table[owner, b + 2, imag, slot % 4] = np.sin(angle)
    return table.reshape(LAT, 8, 20).astype(np.float32)


def latitude_np():
    e, q = np.meshgrid(np.arange(ROWS), np.arange(LAT), indexing="ij")
    theta = np.pi * ((q * ROWS + e).reshape(-1) + 0.5) / NLAT
    weight = 2.0 * np.pi * np.pi * np.sin(theta) / NLAT
    rows = np.stack([np.cos(theta), np.log(np.sin(theta)), weight])
    return np.concatenate([rows, np.zeros((5, NLAT))]).astype(np.float32)


def seed_np():
    seeds = np.zeros((LAT, 8, 128), np.float32)
    for m in range(MODES):
        value = 0.5 * (
            math.log((2 * m + 1) / (4 * math.pi))
            + math.lgamma(2 * m + 1)
            - 2 * m * math.log(2)
            - 2 * math.lgamma(m + 1)
        )
        seeds[m // OWN, m % OWN] = value
    return seeds


def lane_slot(width):
    return lax.broadcasted_iota(jnp.int32, (1, 128), 1) // width


def swap_blocks(values, width):
    values = list(values)
    step = len(values) // 2
    while step:
        shift = step * width
        first = lane_slot(shift) % 2 == 0
        for a in range(len(values)):
            if not a & step:
                low, high = values[a], values[a | step]
                values[a] = jnp.where(first, low, pltpu.roll(high, shift, 1))
                values[a | step] = jnp.where(first, pltpu.roll(low, 128 - shift, 1), high)
        step //= 2
    return values


def split(value):
    high = value.astype(bf16)
    return high, (value - high.astype(f32)).astype(bf16)


def dot(a, b, dims=((1,), (0,))):
    return lax.dot_general(a, b, (dims, ((), ())), preferred_element_type=f32)


def dot3(a, b, dims=((1,), (0,))):
    rows = a[0].shape[0]
    both = dot(jnp.concatenate(a, axis=0), b[0], dims)
    return both[:rows] + (both[rows:] + dot(a[0], b[1], dims))


def pack_kernel(x_hbm, out_ref, x_ref, arrivals):
    first = lane_slot(8) % 2 == 0
    fetches = []
    for j in range(5):
        lanes = pl.ds(128 * j, 128)
        fetches.append(pltpu.make_async_copy(x_hbm.at[:, :, lanes], x_ref.at[:, :, lanes], arrivals.at[j]))
        fetches[j].start()
    for j in range(5):
        fetches[j].wait()
        blocks = swap_blocks([x_ref[:, i, 128 * j : 128 * j + 128] for i in range(ROWS)], 16)
        for b in range(8):
            pair, place = divmod(8 * j + b, 5)
            even, odd = 2 * pair * LON_CHUNK, (2 * pair + 1) * LON_CHUNK
            block = blocks[b]
            if place == 2:
                top, bottom = block[:14], block[14:]
                out_ref[even + 56 : even + 70] = jnp.where(first, top, pltpu.roll(bottom, 8, 1))
                out_ref[odd + 56 : odd + 70] = jnp.where(first, pltpu.roll(top, 120, 1), bottom)
            else:
                base = (even, even + 28, None, odd, odd + 28)[place]
                out_ref[base : base + 28] = block


def forward_kernel(in_ref, high_ref, low_ref, out_ref, local_ref):
    totals = []
    for half in range(2):
        pieces = []
        for start in (14 * half, 28 + 14 * half, 56):
            blocks = [in_ref[LON_CHUNK * q + start : LON_CHUNK * q + start + 16] for q in range(LON - 1)]
            tail = LON_CHUNK * (LON - 1) + start
            blocks += [in_ref[tail : tail + 14], jnp.zeros((2, 128), f32)]
            pieces.append(jnp.concatenate(blocks, axis=0))
        x = split(jnp.concatenate(pieces, axis=1))
        lanes = slice(256 * half, 256 * half + 256)
        totals.append(dot3((high_ref[:, lanes], low_ref[:, lanes]), x))
    both = totals[0][:, :256] + totals[1][:, :256]
    g0, g1 = totals[0][:, 256:], totals[1][:, 256:]
    half_rows = KEPT * LAT
    first = lane_slot(8) % 2 == 0
    last = jnp.where(
        first,
        g0[:half_rows] + pltpu.roll(g1[:half_rows], 120, 1),
        pltpu.roll(g0[half_rows:], 8, 1) + g1[half_rows:],
    )
    for r in range(2):
        for k in range(OWN):
            part = both[LAT * (KEPT * r + k) : LAT * (KEPT * r + k) + LAT]
            row = OWN * r + k
            out_ref[pl.ds(row, LAT, stride=LAT_CHUNK), :] = part[:, :128]
            out_ref[pl.ds(2 * OWN + row, LAT, stride=LAT_CHUNK), :] = part[:, 128:]
    for k in range(OWN):
        out_ref[pl.ds(4 * OWN + k, LAT, stride=LAT_CHUNK), :] = last[LAT * k : LAT * k + LAT]
    for r in range(2):
        rows = slice(LAT * r, LAT * r + LAT)
        local_ref[rows, :256] = both[LAT * (KEPT * r + OWN) : LAT * (KEPT * r + OWN) + LAT]
    local_ref[0:LAT, 256:] = last[LAT * OWN : LAT * OWN + LAT]
    local_ref[LAT:, 256:] = jnp.zeros((LAT, 128), f32)


def local_kernel(place_ref, own_ref, below_ref, above_ref, first_ref, second_ref, wave_ref, out_ref, taps_ref):
    shape = (CHANNELS, 384)
    at = lax.broadcasted_iota(jnp.int32, shape, 1)
    tail = at % 8 + 32
    at = jnp.where(at >= 256, tail, at // 128 * 16 + at % 16)
    chosen = (lax.broadcasted_iota(jnp.int32, shape, 0) == channel_at(place_ref, at)).astype(f32)
    taps_ref[0:25] = pick(first_ref[...], chosen, ((1,), (0,)))
    taps_ref[32:57] = pick(second_ref[...], chosen, ((1,), (0,)))
    lane = lax.broadcasted_iota(jnp.int32, (1, 128), 1)
    left = lane < 64
    south = jnp.where(place_ref[0] == 0, 0.0, 1.0)
    north = jnp.where(place_ref[0] == LAT - 1, 0.0, 1.0)
    masks = (jnp.where(left, south, 1.0), jnp.where(left, 1.0, north))

    def extend(own, below, above):
        turned = pltpu.roll(own, 64, 1)
        return jnp.where(left, below, turned), jnp.where(left, turned, above)

    def turn(value):
        return pltpu.roll(value, 64, 1)

    def shifted(tiles, a):
        if a == 0:
            return tiles
        amount = (-16 * a) % 128
        first, second = (pltpu.roll(tile, amount, 1) for tile in tiles)
        if a > 0:
            keep = lane < 128 - 16 * a
            return jnp.where(keep, first, second), jnp.where(keep, second, first)
        keep = lane >= -16 * a
        return jnp.where(keep, first, second), jnp.where(keep, second, first)

    def weights(which, a, tile):
        rows = [taps_ref[32 * which + 5 * a + b : 32 * which + 5 * a + b + 1, 128 * tile : 128 * tile + 128] for b in range(5)]
        cos1, cos2, sin1, sin2 = (wave_ref[:, 128 * n : 128 * n + 128] for n in range(4))
        real = rows[2] + (rows[3] + rows[1]) * cos1 + (rows[4] + rows[0]) * cos2
        imag = (rows[3] - rows[1]) * sin1 + (rows[4] - rows[0]) * sin2
        return real, imag

    for tile in range(2):
        parts = []
        for r in range(2):
            rows = slice(LAT * r, LAT * r + LAT)
            own = own_ref[rows, 128 * tile : 128 * tile + 128]
            below, above = below_ref[rows], above_ref[rows]
            if tile == 0:
                parts.append(extend(own, below, turn(above)))
            else:
                parts.append(extend(own, turn(below), above))
        for which in range(2):
            real, imag = [list(value) for value in parts]
            for a in range(-2, 3):
                w_r, w_i = weights(which, a + 2, tile)
                e_r, e_i = shifted(parts[0], a), shifted(parts[1], a)
                for n in range(2):
                    real[n] = real[n] + (w_r * e_r[n] - w_i * e_i[n])
                    imag[n] = imag[n] + (w_r * e_i[n] + w_i * e_r[n])
            parts = [tuple(v * m for v, m in zip(value, masks)) for value in (real, imag)]
        for r in range(2):
            result = jnp.where(left, turn(parts[r][0]), turn(parts[r][1]))
            out_ref[LAT * r : LAT * r + LAT, 128 * tile : 128 * tile + 128] = result
    second = lane_slot(8) % 2 == 1
    value = extend(own_ref[0:LAT, 256:], turn(below_ref[2 * LAT :]), turn(above_ref[2 * LAT :]))
    for which in range(2):
        total = list(value)
        swapped = [jnp.where(second, pltpu.roll(v, 8, 1), pltpu.roll(v, 120, 1)) for v in value]
        for a in range(-2, 3):
            w_r, w_i = weights(which, a + 2, 2)
            w_i = jnp.where(second, w_i, -w_i)
            e, f = shifted(value, a), shifted(swapped, a)
            for n in range(2):
                total[n] = total[n] + (w_r * e[n] + w_i * f[n])
        value = tuple(v * m for v, m in zip(total, masks))
    out_ref[0:LAT, 256:] = jnp.where(left, turn(value[0]), turn(value[1]))
    out_ref[LAT:, 256:] = jnp.zeros((LAT, 128), f32)


def channel_at(place_ref, local):
    turned = jnp.where(local >= 32, local - 32, local + 8)
    return place_ref[2] * SLICE + jnp.where(place_ref[1] == 1, turned, local)


def pick(a, b, dims):
    return lax.dot_general(a, b, (dims, ((), ())), precision=lax.Precision.HIGHEST, preferred_element_type=f32)


def taps_kernel(place_ref, first_ref, second_ref, phase_ref, local_ref, taps_ref, up_ref, down_ref):
    left = lane_slot(64) == 0
    a, b = local_ref[:, :128], local_ref[:, 128:256]
    up_ref[: 2 * LAT] = jnp.where(left, pltpu.roll(a, 64, 1), b)
    down_ref[: 2 * LAT] = jnp.where(left, a, pltpu.roll(b, 64, 1))
    up_ref[2 * LAT :] = local_ref[:LAT, 256:]
    down_ref[2 * LAT :] = local_ref[:LAT, 256:]
    shape = (SLICE, CHANNELS)
    wanted = channel_at(place_ref, lax.broadcasted_iota(jnp.int32, shape, 0))
    chosen = (lax.broadcasted_iota(jnp.int32, shape, 1) == wanted).astype(f32)
    rows = [pick(chosen, ref[...], ((1,), (1,))) for ref in (first_ref, second_ref)]
    for tile in range(5):
        phase = phase_ref[:, 4 * tile : 4 * tile + 1]
        for n in range(1, 4):
            column = phase_ref[:, 4 * tile + n : 4 * tile + n + 1]
            phase = jnp.where(lane_slot(LAT) >= n, column, phase)
        for which in range(2):
            for a in range(5):
                total = rows[which][:, 5 * a : 5 * a + 1] * phase[0:1]
                for b in range(1, 5):
                    total = total + rows[which][:, 5 * a + b : 5 * a + b + 1] * phase[b : b + 1]
                base = (5 * which + a) * SLICE
                taps_ref[base : base + SLICE, 128 * tile : 128 * tile + 128] = total


def legendre_kernel(owner_ref, angle_ref, seed_ref, high_ref, low_ref, left_ref, right_ref):
    slot = lax.broadcasted_iota(jnp.int32, (8, 256), 0)
    order_at = jnp.where(slot < OWN, owner_ref[0] * OWN + slot, 2 * MODES)
    order = order_at.astype(f32)
    degree = lax.broadcasted_iota(jnp.int32, (8, 256), 1).astype(f32)
    square, below = degree * degree, (degree - 1.0) * (degree - 1.0)
    upper = jnp.sqrt(
        jnp.maximum(4.0 * square - 1.0, 1.0) / jnp.maximum(square - order * order, 1.0)
    )
    lower = jnp.sqrt(
        jnp.maximum(below - order * order, 0.0) / jnp.maximum(4.0 * below - 1.0, 1.0)
    )
    product = upper * lower
    cosine = jnp.broadcast_to(angle_ref[0:1, :], (8, 256))
    diagonal = jnp.exp(seed_ref[:, 0:1] + order * angle_ref[1:2, :])
    previous = jnp.zeros((8, 256), f32)
    earlier = previous
    for l in range(MODES):
        current = jnp.where(
            order_at == l,
            diagonal,
            (upper[:, l : l + 1] * cosine) * previous - product[:, l : l + 1] * earlier,
        )
        left_ref[8 * l : 8 * l + 8] = current[:, :128]
        right_ref[8 * l : 8 * l + 8] = current[:, 128:]
        previous, earlier = current, previous
    for k in range(OWN):
        for part, source in enumerate((left_ref, right_ref)):
            high, low = split(source[pl.ds(k, MODES, stride=8), :])
            high_ref[k, :, 128 * part : 128 * part + 128] = high
            low_ref[k, :, 128 * part : 128 * part + 128] = low

def spectral_kernel(place_ref, in_ref, high_ref, low_ref, taps_ref, gain_ref, angle_ref, out_ref, u_ref, v_ref, f_ref):
    lane = lax.broadcasted_iota(jnp.int32, (1, 128), 1) % LAT

    def fill_edges(ref):
        for part in range(2):
            for group in range(2):
                for e in (0, 1):
                    block = pltpu.roll(ref[part, group, 2 + e], 127, 1)
                    ref[part, group, 10 + e] = jnp.where(lane == LAT - 1, 0.0, block)
                    block = pltpu.roll(ref[part, group, 8 + e], 1, 1)
                    ref[part, group, e] = jnp.where(lane == 0, 0.0, block)

    def stencil(ref, which, store):
        for group in range(2):
            for tile in range(5):
                rows = slice(8 * tile, 8 * tile + 8)
                taps = []
                for a in range(5):
                    base = (which * 5 + a) * SLICE + 8 * tile
                    taps.append(
                        [
                            taps_ref[base : base + 8, 128 * column : 128 * column + 128]
                            for column in FACTOR_TILES[group]
                        ]
                    )
                real = [ref[0, group, e, rows] for e in range(12)]
                imag = [ref[1, group, e, rows] for e in range(12)]
                for e in range(ROWS):
                    total_r, total_i = real[e + 2], imag[e + 2]
                    for a in range(5):
                        r_tap, s_tap, i_tap = taps[a]
                        total_r = total_r + (r_tap * real[e + a] - i_tap * imag[e + a])
                        total_i = total_i + (s_tap * imag[e + a] + i_tap * real[e + a])
                    store(group, rows, e, total_r, total_i)

    def rows_of(start, count):
        pieces = [in_ref[pl.ds(start + n, LAT, stride=LAT_CHUNK), :] for n in range(count)]
        if count < 4:
            pieces.append(jnp.zeros((LAT * (4 - count), 128), f32))
        return jnp.concatenate(pieces, axis=0).T

    for group in range(2):
        count = min(4, OWN - 4 * group)
        for tile in range(2):
            for part in range(2):
                block = rows_of(OWN * (2 * tile + part) + 4 * group, count)
                for e in range(ROWS):
                    u_ref[part, group, 2 + e, 16 * tile : 16 * tile + 16] = block[16 * e : 16 * e + 16]
        block = rows_of(4 * OWN + 4 * group, count)
        for e in range(ROWS):
            for part in range(2):
                start = 16 * e + 8 * part
                u_ref[part, group, 2 + e, 32:40] = block[start : start + 8]
    fill_edges(u_ref)

    def keep_first(group, rows, e, total_r, total_i):
        v_ref[0, group, 2 + e, rows] = total_r
        v_ref[1, group, 2 + e, rows] = total_i

    stencil(u_ref, 0, keep_first)

    weight = angle_ref[2:3, :]
    for part in range(2):
        for group in range(2):
            halves = [
                swap_blocks([v_ref[part, group, 2 + 4 * j + e] for e in range(4)], 32) for j in range(2)
            ]
            for n in range(4):
                if 4 * group + n < OWN:
                    f_ref[4 * group + n, SLICE * part : SLICE * part + SLICE] = (
                        jnp.concatenate([halves[0][n], halves[1][n]], axis=1) * weight
                    )
    gain = gain_ref[...]
    gain = jnp.where(place_ref[1] == 1, jnp.concatenate([gain[8:], gain[:8]], axis=0), gain)
    for k in range(OWN):
        table = (high_ref[k], low_ref[k])
        spectrum = dot3(split(f_ref[k]), table, ((1,), (1,)))
        second = jnp.where(place_ref[0] == 0, 0.0, gain) if k == 0 else gain
        f_ref[k] = dot3(split(spectrum * jnp.concatenate([gain, second], axis=0)), table)
    for part in range(2):
        for group in range(2):
            rows = slice(SLICE * part, SLICE * part + SLICE)
            for j in range(2):
                values = [
                    f_ref[4 * group + n, rows, 128 * j : 128 * j + 128]
                    if 4 * group + n < OWN
                    else jnp.zeros((SLICE, 128), f32)
                    for n in range(4)
                ]
                for e, value in enumerate(swap_blocks(values, 32)):
                    v_ref[part, group, 2 + 4 * j + e] = v_ref[part, group, 2 + 4 * j + e] + value
    fill_edges(v_ref)

    def keep_second(group, rows, e, total_r, total_i):
        u_ref[0, group, 2 + e, rows] = total_r
        u_ref[1, group, 2 + e, rows] = total_i

    stencil(v_ref, 1, keep_second)

    def give(start, count, pieces):
        block = jnp.concatenate(pieces, axis=0).T
        for n in range(count):
            out_ref[pl.ds(start + n, LAT, stride=LAT_CHUNK), :] = block[LAT * n : LAT * n + LAT]

    for group in range(2):
        count = min(4, OWN - 4 * group)
        for tile in range(2):
            for part in range(2):
                give(
                    OWN * (2 * tile + part) + 4 * group,
                    count,
                    [u_ref[part, group, 2 + e, 16 * tile : 16 * tile + 16] for e in range(ROWS)],
                )
        give(
            4 * OWN + 4 * group,
            count,
            [u_ref[part, group, 2 + e, 32:40] for e in range(ROWS) for part in range(2)],
        )


def inverse_kernel(in_ref, local_ref, high_ref, low_ref, out_ref):
    totals = []
    for part in range(2):
        columns = []
        for tile, start in enumerate((OWN * part, OWN * (2 + part), 4 * OWN)):
            pieces = [in_ref[pl.ds(start + k, LAT, stride=LAT_CHUNK), :] for k in range(OWN)]
            row = LAT * part if tile < 2 else 0
            pieces.append(local_ref[row : row + LAT, 128 * tile : 128 * tile + 128])
            columns.append(jnp.concatenate(pieces + [jnp.zeros((LAT, 128), f32)], axis=0))
        x = split(jnp.concatenate(columns, axis=1))
        totals.append(dot3((high_ref[part], low_ref[part]), x))
    both = totals[0][:, :256] + totals[1][:, :256]
    g0, g1 = totals[0][:, 256:], totals[1][:, 256:]
    first = lane_slot(8) % 2 == 0
    last = jnp.where(
        first,
        g0[:256] + pltpu.roll(g1[:256], 120, 1),
        pltpu.roll(g0[256:], 8, 1) + g1[256:],
    )
    for q in range(LON):
        base = LON_CHUNK * q
        for tile in range(2):
            for half in range(2):
                row = 256 * half + 16 * q
                start = base + 28 * tile + 14 * half
                out_ref[start : start + 14] = both[row : row + 14, 128 * tile : 128 * tile + 128]
        out_ref[base + 56 : base + 70] = last[16 * q : 16 * q + 14]


def mlp_kernel(in_ref, gain_ref, up_ref, down_ref, out_hbm, x_ref, y_ref, sent):
    first = lane_slot(8) % 2 == 0
    for j in range(5):
        blocks = []
        for b in range(8):
            pair, place = divmod(8 * j + b, 5)
            even, odd = 2 * pair * LON_CHUNK, (2 * pair + 1) * LON_CHUNK
            if place == 2:
                e, o = in_ref[even + 56 : even + 70], in_ref[odd + 56 : odd + 70]
                top = jnp.where(first, e, pltpu.roll(o, 8, 1))
                bottom = jnp.where(first, pltpu.roll(e, 120, 1), o)
                blocks.append(jnp.concatenate([top, bottom], axis=0))
            else:
                base = (even, even + 28, None, odd, odd + 28)[place]
                blocks.append(in_ref[base : base + 28])
        for i, value in enumerate(swap_blocks(blocks, 16)):
            x_ref[:, i, 128 * j : 128 * j + 128] = value
    x = x_ref[...].reshape(COLS * ROWS, CHANNELS)
    average = jnp.mean(x, axis=-1, keepdims=True)
    centred = x - average
    spread = jnp.mean(centred * centred, axis=-1, keepdims=True)
    normed = (centred * lax.rsqrt(spread + 1e-05) * gain_ref[...].reshape(1, CHANNELS)).astype(bf16)
    active = []
    for n in range(5):
        hidden = dot(normed, up_ref[:, 256 * n : 256 * n + 256])
        active.append(jax.nn.gelu(hidden, approximate=True).astype(bf16))
    active = jnp.concatenate(active, axis=1)
    stores = []
    for n, (start, width) in enumerate(((0, 256), (256, 256), (512, 128))):
        lanes = pl.ds(start, width)
        total = x[:, start : start + width] + dot(active, down_ref[:, start : start + width])
        y_ref[:, :, start : start + width] = total.reshape(COLS, ROWS, width)
        stores.append(pltpu.make_async_copy(y_ref.at[:, :, lanes], out_hbm.at[:, :, lanes], sent.at[n]))
        stores[n].start()
    for store in stores:
        store.wait()


def vmem(count):
    return [pl.BlockSpec(memory_space=pltpu.VMEM)] * count


def run(kernel, shape, *operands, scratch=(), cost=(0, 0), grant=24, far=0, out=pltpu.VMEM):
    return pl.pallas_call(
        kernel,
        out_shape=jax.ShapeDtypeStruct(shape, f32),
        in_specs=vmem(len(operands) - far) + [pl.BlockSpec(memory_space=pltpu.HBM)] * far,
        out_specs=pl.BlockSpec(memory_space=out),
        scratch_shapes=list(scratch),
        compiler_params=pltpu.CompilerParams(vmem_limit_bytes=grant << 20),
        cost_estimate=pl.CostEstimate(flops=cost[0], bytes_accessed=cost[1], transcendentals=0),
    )(*operands)


def legendre(*operands):
    table = jax.ShapeDtypeStruct((OWN, MODES, NLAT), bf16)
    return pl.pallas_call(
        legendre_kernel,
        out_shape=(table, table),
        in_specs=[pl.BlockSpec(memory_space=pltpu.SMEM)] + vmem(2),
        out_specs=vmem(2),
        scratch_shapes=[pltpu.VMEM((8 * MODES, 128), f32)] * 2,
        compiler_params=pltpu.CompilerParams(vmem_limit_bytes=16 << 20),
        cost_estimate=pl.CostEstimate(flops=10**7, bytes_accessed=10**7, transcendentals=0),
    )(*operands)


def wave_np():
    angle = 2.0 * np.pi * (MODES + np.arange(LAT)) / NLON
    waves = [np.cos(angle), np.cos(2.0 * angle), np.sin(angle), np.sin(2.0 * angle)]
    return np.repeat(np.stack(waves, axis=1), 128, axis=1).astype(np.float32)


def exchange(array, axis, count):
    rows = array.shape[0] // count
    shape = (count, rows, 128) if rows % 8 == 0 else (count, 1, rows * 128)
    moved = lax.all_to_all(array.reshape(shape), axis, split_axis=0, concat_axis=0, tiled=True)
    return moved.reshape(array.shape)


def per_device(latent, conv_first, conv_second, filter_gains, norm_gain, up_weight, down_weight):
    band = lax.axis_index("lat")
    sector = lax.axis_index("lon")
    odd = sector % 2 == 1
    forward, inverse = fourier_np()
    forward, inverse = split_np(forward), split_np(inverse)
    angles = jnp.asarray(latitude_np())

    packed = run(
        pack_kernel,
        (LON * LON_CHUNK, 128),
        latent.transpose(1, 0, 2),
        scratch=[
            pltpu.VMEM((COLS, ROWS, CHANNELS), f32),
            pltpu.SemaphoreType.DMA((5,)),
        ],
        far=1,
        grant=53,
    )
    circles = exchange(packed, "lon", LON)

    shapes = ((LAT * LAT_CHUNK, 128), (2 * LAT, 384))
    coeffs, local = pl.pallas_call(
        forward_kernel,
        out_shape=tuple(jax.ShapeDtypeStruct(shape, f32) for shape in shapes),
        in_specs=vmem(3),
        out_specs=vmem(2),
        compiler_params=pltpu.CompilerParams(vmem_limit_bytes=24 << 20),
    )(circles, *map(jnp.asarray, forward))
    orders = exchange(coeffs, "lat", LAT)
    local, conv_first, conv_second, band = lax.optimization_barrier(
        (local, conv_first, conv_second, band)
    )
    seeds = lax.dynamic_index_in_dim(jnp.asarray(seed_np()), band, 0, False)
    owner = band.astype(jnp.int32).reshape(1)
    high, low = legendre(owner, angles, seeds)
    phases = lax.dynamic_index_in_dim(jnp.asarray(phase_np()), band, 0, False)
    place = jnp.stack([band, odd, sector]).astype(jnp.int32)
    shapes = ((10 * SLICE, 640), (3 * LAT, 128), (3 * LAT, 128))
    taps, up, down = pl.pallas_call(
        taps_kernel,
        out_shape=tuple(jax.ShapeDtypeStruct(shape, f32) for shape in shapes),
        in_specs=[pl.BlockSpec(memory_space=pltpu.SMEM)] + vmem(4),
        out_specs=vmem(3),
        compiler_params=pltpu.CompilerParams(vmem_limit_bytes=16 << 20),
        cost_estimate=pl.CostEstimate(flops=10**7, bytes_accessed=10**7, transcendentals=0),
    )(place, conv_first, conv_second, phases, local)
    rising = [(n, n + 1) for n in range(LAT - 1)]
    below = lax.ppermute(up, "lat", rising)
    above = lax.ppermute(down, "lat", [(target, source) for source, target in rising])
    stay = pl.pallas_call(
        local_kernel,
        out_shape=jax.ShapeDtypeStruct((2 * LAT, 384), f32),
        in_specs=[pl.BlockSpec(memory_space=pltpu.SMEM)] + vmem(6),
        out_specs=vmem(1)[0],
        scratch_shapes=[pltpu.VMEM((64, 384), f32)],
        compiler_params=pltpu.CompilerParams(vmem_limit_bytes=16 << 20),
        cost_estimate=pl.CostEstimate(flops=10**7, bytes_accessed=10**6, transcendentals=0),
    )(place, local, below, above, conv_first, conv_second, jnp.asarray(wave_np()))
    orders, taps, high, low = lax.optimization_barrier((orders, taps, high, low))
    state = pltpu.VMEM((2, 2, 12, SLICE, 128), f32)
    third = pl.pallas_call(
        spectral_kernel,
        out_shape=jax.ShapeDtypeStruct((LAT * LAT_CHUNK, 128), f32),
        in_specs=[pl.BlockSpec(memory_space=pltpu.SMEM)] + vmem(6),
        out_specs=vmem(1)[0],
        scratch_shapes=[state, state, pltpu.VMEM((OWN, 2 * SLICE, NLAT), f32)],
        compiler_params=pltpu.CompilerParams(vmem_limit_bytes=24 << 20),
    )(place, orders, high, low, taps, filter_gains.T, angles)
    returned = exchange(third, "lat", LAT)
    restored = run(inverse_kernel, (LON * LON_CHUNK, 128), returned, stay, *map(jnp.asarray, inverse))
    arrived = exchange(restored, "lon", LON)
    result = run(
        mlp_kernel,
        (COLS, ROWS, CHANNELS),
        arrived,
        norm_gain,
        up_weight,
        down_weight,
        scratch=[
            pltpu.VMEM((COLS, ROWS, CHANNELS), f32),
            pltpu.VMEM((COLS, ROWS, CHANNELS), f32),
            pltpu.SemaphoreType.DMA((3,)),
        ],
        out=pltpu.HBM,
    )
    return result.transpose(1, 0, 2)


def solution(mesh):
    return jax.shard_map(
        per_device,
        mesh=mesh,
        in_specs=(P("lat", "lon", None), P(), P(), P(None, "lon"), P(), P(), P()),
        out_specs=P("lat", "lon", None),
        check_vma=False,
    )
```

```python
import math

import jax
import jax.numpy as jnp
import numpy as np
from jax import lax
from jax.experimental import pallas as pl
from jax.experimental.pallas import tpu as pltpu
from jax.sharding import PartitionSpec as P

ROWS, COLS, CHANNELS, HIDDEN = 8, 28, 640, 1280
LAT, LON, SLICE = 32, 16, 40
NLAT, NLON, MODES = 256, 448, 192
OWN = MODES // LAT
KEPT = OWN + 1
LON_CHUNK = 70
LAT_CHUNK = 30
f32, bf16 = jnp.float32, jnp.bfloat16


def split_np(table):
    high = table.astype(np.float32).astype(jnp.bfloat16)
    low = (table - high.astype(np.float64)).astype(np.float32).astype(jnp.bfloat16)
    return high, low


def order_of(owner, slot):
    return owner * OWN + slot if slot < OWN else MODES + owner


def fourier_np():
    half, sector, step = np.meshgrid(np.arange(2), np.arange(LON), np.arange(16), indexing="ij")
    place = (sector * COLS + half * 14 + step).reshape(-1)
    valid = (step < 14).reshape(-1)
    forward = np.zeros((2, KEPT, LAT, 512))
    inverse = np.zeros((2, 512, 8, LAT))
    for slot in range(KEPT):
        for owner in range(LAT):
            order = order_of(owner, slot)
            angle = 2.0 * np.pi * ((order * place) % NLON) / NLON
            double = 1.0 if order == 0 else 2.0
            real, imag = np.cos(angle), -np.sin(angle)
            if order == 0:
                imag = np.cos(np.pi * (place % 2))
            forward[0, slot, owner] = real / NLON * valid
            forward[1, slot, owner] = imag / NLON * valid
            inverse[0, :, slot, owner] = real * double * valid
            inverse[1, :, slot, owner] = imag * double * valid
    return forward.reshape(2 * KEPT * LAT, 512), inverse.reshape(2, 512, 8 * LAT)


FACTOR_TILES = ((0, 1, 2), (3, 3, 4))


def phase_np():
    table = np.zeros((LAT, 8, 5, 4))
    for owner in range(LAT):
        for slot in range(OWN):
            order = order_of(owner, slot)
            real, second, imag = FACTOR_TILES[slot // 4]
            for b in range(-2, 3):
                angle = 2.0 * np.pi * ((order * b) % NLON) / NLON
                table[owner, b + 2, real, slot % 4] = np.cos(angle)
                if second != real:
                    table[owner, b + 2, second, slot % 4] = np.cos(np.pi * b) if order == 0 else np.cos(angle)
                table[owner, b + 2, imag, slot % 4] = np.sin(angle)
    return table.reshape(LAT, 8, 20).astype(np.float32)


def latitude_np():
    e, q = np.meshgrid(np.arange(ROWS), np.arange(LAT), indexing="ij")
    theta = np.pi * ((q * ROWS + e).reshape(-1) + 0.5) / NLAT
    weight = 2.0 * np.pi * np.pi * np.sin(theta) / NLAT
    rows = np.stack([np.cos(theta), np.log(np.sin(theta)), weight])
    return np.concatenate([rows, np.zeros((5, NLAT))]).astype(np.float32)


def seed_np():
    seeds = np.zeros((LAT, 8, 128), np.float32)
    for m in range(MODES):
        value = 0.5 * (
            math.log((2 * m + 1) / (4 * math.pi))
            + math.lgamma(2 * m + 1)
            - 2 * m * math.log(2)
            - 2 * math.lgamma(m + 1)
        )
        seeds[m // OWN, m % OWN] = value
    return seeds


def lane_slot(width):
    return lax.broadcasted_iota(jnp.int32, (1, 128), 1) // width


def swap_blocks(values, width):
    values = list(values)
    step = len(values) // 2
    while step:
        shift = step * width
        first = lane_slot(shift) % 2 == 0
        for a in range(len(values)):
            if not a & step:
                low, high = values[a], values[a | step]
                values[a] = jnp.where(first, low, pltpu.roll(high, shift, 1))
                values[a | step] = jnp.where(first, pltpu.roll(low, 128 - shift, 1), high)
        step //= 2
    return values


def split(value):
    high = value.astype(bf16)
    return high, (value - high.astype(f32)).astype(bf16)


def dot(a, b, dims=((1,), (0,))):
    return lax.dot_general(a, b, (dims, ((), ())), preferred_element_type=f32)


def dot3(a, b, dims=((1,), (0,))):
    rows = a[0].shape[0]
    both = dot(jnp.concatenate(a, axis=0), b[0], dims)
    return both[:rows] + (both[rows:] + dot(a[0], b[1], dims))


def pack_kernel(x_hbm, out_ref, x_ref, arrivals):
    first = lane_slot(8) % 2 == 0
    fetches = []
    for j in range(5):
        lanes = pl.ds(128 * j, 128)
        fetches.append(pltpu.make_async_copy(x_hbm.at[:, :, lanes], x_ref.at[:, :, lanes], arrivals.at[j]))
        fetches[j].start()
    for j in range(5):
        fetches[j].wait()
        blocks = swap_blocks([x_ref[:, i, 128 * j : 128 * j + 128] for i in range(ROWS)], 16)
        for b in range(8):
            pair, place = divmod(8 * j + b, 5)
            even, odd = 2 * pair * LON_CHUNK, (2 * pair + 1) * LON_CHUNK
            block = blocks[b]
            if place == 2:
                top, bottom = block[:14], block[14:]
                out_ref[even + 56 : even + 70] = jnp.where(first, top, pltpu.roll(bottom, 8, 1))
                out_ref[odd + 56 : odd + 70] = jnp.where(first, pltpu.roll(top, 120, 1), bottom)
            else:
                base = (even, even + 28, None, odd, odd + 28)[place]
                out_ref[base : base + 28] = block


def forward_kernel(in_ref, high_ref, low_ref, out_ref, local_ref):
    totals = []
    for half in range(2):
        pieces = []
        for start in (14 * half, 28 + 14 * half, 56):
            blocks = [in_ref[LON_CHUNK * q + start : LON_CHUNK * q + start + 16] for q in range(LON - 1)]
            tail = LON_CHUNK * (LON - 1) + start
            blocks += [in_ref[tail : tail + 14], jnp.zeros((2, 128), f32)]
            pieces.append(jnp.concatenate(blocks, axis=0))
        x = split(jnp.concatenate(pieces, axis=1))
        lanes = slice(256 * half, 256 * half + 256)
        totals.append(dot3((high_ref[:, lanes], low_ref[:, lanes]), x))
    both = totals[0][:, :256] + totals[1][:, :256]
    g0, g1 = totals[0][:, 256:], totals[1][:, 256:]
    half_rows = KEPT * LAT
    first = lane_slot(8) % 2 == 0
    last = jnp.where(
        first,
        g0[:half_rows] + pltpu.roll(g1[:half_rows], 120, 1),
        pltpu.roll(g0[half_rows:], 8, 1) + g1[half_rows:],
    )
    for r in range(2):
        for k in range(OWN):
            part = both[LAT * (KEPT * r + k) : LAT * (KEPT * r + k) + LAT]
            row = OWN * r + k
            out_ref[pl.ds(row, LAT, stride=LAT_CHUNK), :] = part[:, :128]
            out_ref[pl.ds(2 * OWN + row, LAT, stride=LAT_CHUNK), :] = part[:, 128:]
    for k in range(OWN):
        out_ref[pl.ds(4 * OWN + k, LAT, stride=LAT_CHUNK), :] = last[LAT * k : LAT * k + LAT]
    for r in range(2):
        rows = slice(LAT * r, LAT * r + LAT)
        local_ref[rows, :256] = both[LAT * (KEPT * r + OWN) : LAT * (KEPT * r + OWN) + LAT]
    local_ref[0:LAT, 256:] = last[LAT * OWN : LAT * OWN + LAT]
    local_ref[LAT:, 256:] = jnp.zeros((LAT, 128), f32)


def local_kernel(place_ref, own_ref, below_ref, above_ref, taps_ref, out_ref):
    lane = lax.broadcasted_iota(jnp.int32, (1, 128), 1)
    left = lane < 64
    south = jnp.where(place_ref[0] == 0, 0.0, 1.0)
    north = jnp.where(place_ref[0] == LAT - 1, 0.0, 1.0)
    masks = (jnp.where(left, south, 1.0), jnp.where(left, 1.0, north))

    def extend(own, below, above):
        turned = pltpu.roll(own, 64, 1)
        return jnp.where(left, below, turned), jnp.where(left, turned, above)

    def turn(value):
        return pltpu.roll(value, 64, 1)

    def shifted(tiles, a):
        if a == 0:
            return tiles
        amount = (-16 * a) % 128
        first, second = (pltpu.roll(tile, amount, 1) for tile in tiles)
        if a > 0:
            keep = lane < 128 - 16 * a
            return jnp.where(keep, first, second), jnp.where(keep, second, first)
        keep = lane >= -16 * a
        return jnp.where(keep, first, second), jnp.where(keep, second, first)

    def weights(which, a, tile):
        start = 480 + 32 * which + 5 * a
        rows = [taps_ref[start + b : start + b + 1, 128 * tile : 128 * tile + 128] for b in range(5)]
        cos1, cos2, sin1, sin2 = (taps_ref[544:576, 128 * n : 128 * n + 128] for n in range(4))
        real = rows[2] + (rows[3] + rows[1]) * cos1 + (rows[4] + rows[0]) * cos2
        imag = (rows[3] - rows[1]) * sin1 + (rows[4] - rows[0]) * sin2
        return real, imag

    for tile in range(2):
        parts = []
        for r in range(2):
            rows = slice(LAT * r, LAT * r + LAT)
            own = own_ref[rows, 128 * tile : 128 * tile + 128]
            below, above = below_ref[rows], above_ref[rows]
            if tile == 0:
                parts.append(extend(own, below, turn(above)))
            else:
                parts.append(extend(own, turn(below), above))
        for which in range(2):
            real, imag = [list(value) for value in parts]
            for a in range(-2, 3):
                w_r, w_i = weights(which, a + 2, tile)
                e_r, e_i = shifted(parts[0], a), shifted(parts[1], a)
                for n in range(2):
                    real[n] = real[n] + (w_r * e_r[n] - w_i * e_i[n])
                    imag[n] = imag[n] + (w_r * e_i[n] + w_i * e_r[n])
            parts = [tuple(v * m for v, m in zip(value, masks)) for value in (real, imag)]
        for r in range(2):
            result = jnp.where(left, turn(parts[r][0]), turn(parts[r][1]))
            out_ref[LAT * r : LAT * r + LAT, 128 * tile : 128 * tile + 128] = result
    second = lane_slot(8) % 2 == 1
    value = extend(own_ref[0:LAT, 256:], turn(below_ref[2 * LAT :]), turn(above_ref[2 * LAT :]))
    for which in range(2):
        total = list(value)
        swapped = [jnp.where(second, pltpu.roll(v, 8, 1), pltpu.roll(v, 120, 1)) for v in value]
        for a in range(-2, 3):
            w_r, w_i = weights(which, a + 2, 2)
            w_i = jnp.where(second, w_i, -w_i)
            e, f = shifted(value, a), shifted(swapped, a)
            for n in range(2):
                total[n] = total[n] + (w_r * e[n] + w_i * f[n])
        value = tuple(v * m for v, m in zip(total, masks))
    out_ref[0:LAT, 256:] = jnp.where(left, turn(value[0]), turn(value[1]))
    out_ref[LAT:, 256:] = jnp.zeros((LAT, 128), f32)


def channel_at(place_ref, local):
    turned = jnp.where(local >= 32, local - 32, local + 8)
    return place_ref[2] * SLICE + jnp.where(place_ref[1] == 1, turned, local)


def pick(a, b, dims):
    return lax.dot_general(a, b, (dims, ((), ())), precision=lax.Precision.HIGHEST, preferred_element_type=f32)


def taps_kernel(place_ref, first_ref, second_ref, phase_ref, local_ref, gain_ref, wave_ref, taps_ref, up_ref, down_ref):
    gain = gain_ref[...]
    gain = jnp.where(place_ref[1] == 1, jnp.concatenate([gain[8:], gain[:8]], axis=0), gain)
    base = 10 * SLICE
    taps_ref[base : base + SLICE, :MODES] = gain
    taps_ref[base + SLICE : base + 2 * SLICE, :MODES] = jnp.where(place_ref[0] == 0, 0.0, gain)
    left = lane_slot(64) == 0
    a, b = local_ref[:, :128], local_ref[:, 128:256]
    up_ref[: 2 * LAT] = jnp.where(left, pltpu.roll(a, 64, 1), b)
    down_ref[: 2 * LAT] = jnp.where(left, a, pltpu.roll(b, 64, 1))
    up_ref[2 * LAT :] = local_ref[:LAT, 256:]
    down_ref[2 * LAT :] = local_ref[:LAT, 256:]
    taps_ref[544:576, :512] = wave_ref[...]
    shape = (CHANNELS, 384)
    at = lax.broadcasted_iota(jnp.int32, shape, 1)
    tail = at % 8 + 32
    at = jnp.where(at >= 256, tail, at // 128 * 16 + at % 16)
    chosen = (lax.broadcasted_iota(jnp.int32, shape, 0) == channel_at(place_ref, at)).astype(f32)
    taps_ref[480:505, :384] = pick(first_ref[...], chosen, ((1,), (0,)))
    taps_ref[512:537, :384] = pick(second_ref[...], chosen, ((1,), (0,)))
    shape = (SLICE, CHANNELS)
    wanted = channel_at(place_ref, lax.broadcasted_iota(jnp.int32, shape, 0))
    chosen = (lax.broadcasted_iota(jnp.int32, shape, 1) == wanted).astype(f32)
    rows = [pick(chosen, ref[...], ((1,), (1,))) for ref in (first_ref, second_ref)]
    for tile in range(5):
        phase = phase_ref[:, 4 * tile : 4 * tile + 1]
        for n in range(1, 4):
            column = phase_ref[:, 4 * tile + n : 4 * tile + n + 1]
            phase = jnp.where(lane_slot(LAT) >= n, column, phase)
        for which in range(2):
            for a in range(5):
                total = rows[which][:, 5 * a : 5 * a + 1] * phase[0:1]
                for b in range(1, 5):
                    total = total + rows[which][:, 5 * a + b : 5 * a + b + 1] * phase[b : b + 1]
                base = (5 * which + a) * SLICE
                taps_ref[base : base + SLICE, 128 * tile : 128 * tile + 128] = total


def legendre_kernel(owner_ref, angle_ref, seed_ref, high_ref, low_ref, left_ref, right_ref):
    slot = lax.broadcasted_iota(jnp.int32, (8, 256), 0)
    order_at = jnp.where(slot < OWN, owner_ref[0] * OWN + slot, 2 * MODES)
    order = order_at.astype(f32)
    degree = lax.broadcasted_iota(jnp.int32, (8, 256), 1).astype(f32)
    square, below = degree * degree, (degree - 1.0) * (degree - 1.0)
    upper = jnp.sqrt(
        jnp.maximum(4.0 * square - 1.0, 1.0) / jnp.maximum(square - order * order, 1.0)
    )
    lower = jnp.sqrt(
        jnp.maximum(below - order * order, 0.0) / jnp.maximum(4.0 * below - 1.0, 1.0)
    )
    product = upper * lower
    cosine = jnp.broadcast_to(angle_ref[0:1, :], (8, 256))
    diagonal = jnp.exp(seed_ref[:, 0:1] + order * angle_ref[1:2, :])
    previous = jnp.zeros((8, 256), f32)
    earlier = previous
    for l in range(MODES):
        current = jnp.where(
            order_at == l,
            diagonal,
            (upper[:, l : l + 1] * cosine) * previous - product[:, l : l + 1] * earlier,
        )
        left_ref[8 * l : 8 * l + 8] = current[:, :128]
        right_ref[8 * l : 8 * l + 8] = current[:, 128:]
        previous, earlier = current, previous
    for k in range(OWN):
        for part, source in enumerate((left_ref, right_ref)):
            high, low = split(source[pl.ds(k, MODES, stride=8), :])
            high_ref[k, :, 128 * part : 128 * part + 128] = high
            low_ref[k, :, 128 * part : 128 * part + 128] = low

def spectral_kernel(in_ref, high_ref, low_ref, taps_ref, angle_ref, out_ref, u_ref, v_ref, f_ref):
    lane = lax.broadcasted_iota(jnp.int32, (1, 128), 1) % LAT

    def fill_edges(ref):
        for part in range(2):
            for group in range(2):
                for e in (0, 1):
                    block = pltpu.roll(ref[part, group, 2 + e], 127, 1)
                    ref[part, group, 10 + e] = jnp.where(lane == LAT - 1, 0.0, block)
                    block = pltpu.roll(ref[part, group, 8 + e], 1, 1)
                    ref[part, group, e] = jnp.where(lane == 0, 0.0, block)

    def stencil(ref, which, store):
        for group in range(2):
            for tile in range(5):
                rows = slice(8 * tile, 8 * tile + 8)
                taps = []
                for a in range(5):
                    base = (which * 5 + a) * SLICE + 8 * tile
                    taps.append(
                        [
                            taps_ref[base : base + 8, 128 * column : 128 * column + 128]
                            for column in FACTOR_TILES[group]
                        ]
                    )
                real = [ref[0, group, e, rows] for e in range(12)]
                imag = [ref[1, group, e, rows] for e in range(12)]
                for e in range(ROWS):
                    total_r, total_i = real[e + 2], imag[e + 2]
                    for a in range(5):
                        r_tap, s_tap, i_tap = taps[a]
                        total_r = total_r + (r_tap * real[e + a] - i_tap * imag[e + a])
                        total_i = total_i + (s_tap * imag[e + a] + i_tap * real[e + a])
                    store(group, rows, e, total_r, total_i)

    def rows_of(start, count):
        pieces = [in_ref[pl.ds(start + n, LAT, stride=LAT_CHUNK), :] for n in range(count)]
        if count < 4:
            pieces.append(jnp.zeros((LAT * (4 - count), 128), f32))
        return jnp.concatenate(pieces, axis=0).T

    for group in range(2):
        count = min(4, OWN - 4 * group)
        for tile in range(2):
            for part in range(2):
                block = rows_of(OWN * (2 * tile + part) + 4 * group, count)
                for e in range(ROWS):
                    u_ref[part, group, 2 + e, 16 * tile : 16 * tile + 16] = block[16 * e : 16 * e + 16]
        block = rows_of(4 * OWN + 4 * group, count)
        for e in range(ROWS):
            for part in range(2):
                start = 16 * e + 8 * part
                u_ref[part, group, 2 + e, 32:40] = block[start : start + 8]
    fill_edges(u_ref)

    def keep_first(group, rows, e, total_r, total_i):
        v_ref[0, group, 2 + e, rows] = total_r
        v_ref[1, group, 2 + e, rows] = total_i

    stencil(u_ref, 0, keep_first)

    weight = angle_ref[2:3, :]
    for part in range(2):
        for group in range(2):
            halves = [
                swap_blocks([v_ref[part, group, 2 + 4 * j + e] for e in range(4)], 32) for j in range(2)
            ]
            for n in range(4):
                if 4 * group + n < OWN:
                    f_ref[4 * group + n, SLICE * part : SLICE * part + SLICE] = (
                        jnp.concatenate([halves[0][n], halves[1][n]], axis=1) * weight
                    )
    gain, masked = (taps_ref[SLICE * n : SLICE * n + SLICE, :MODES] for n in (10, 11))
    for k in range(OWN):
        table = (high_ref[k], low_ref[k])
        spectrum = dot3(split(f_ref[k]), table, ((1,), (1,)))
        second = masked if k == 0 else gain
        f_ref[k] = dot3(split(spectrum * jnp.concatenate([gain, second], axis=0)), table)
    for part in range(2):
        for group in range(2):
            rows = slice(SLICE * part, SLICE * part + SLICE)
            for j in range(2):
                values = [
                    f_ref[4 * group + n, rows, 128 * j : 128 * j + 128]
                    if 4 * group + n < OWN
                    else jnp.zeros((SLICE, 128), f32)
                    for n in range(4)
                ]
                for e, value in enumerate(swap_blocks(values, 32)):
                    v_ref[part, group, 2 + 4 * j + e] = v_ref[part, group, 2 + 4 * j + e] + value
    fill_edges(v_ref)

    def keep_second(group, rows, e, total_r, total_i):
        u_ref[0, group, 2 + e, rows] = total_r
        u_ref[1, group, 2 + e, rows] = total_i

    stencil(v_ref, 1, keep_second)

    def give(start, count, pieces):
        block = jnp.concatenate(pieces, axis=0).T
        for n in range(count):
            out_ref[pl.ds(start + n, LAT, stride=LAT_CHUNK), :] = block[LAT * n : LAT * n + LAT]

    for group in range(2):
        count = min(4, OWN - 4 * group)
        for tile in range(2):
            for part in range(2):
                give(
                    OWN * (2 * tile + part) + 4 * group,
                    count,
                    [u_ref[part, group, 2 + e, 16 * tile : 16 * tile + 16] for e in range(ROWS)],
                )
        give(
            4 * OWN + 4 * group,
            count,
            [u_ref[part, group, 2 + e, 32:40] for e in range(ROWS) for part in range(2)],
        )


def inverse_kernel(in_ref, local_ref, high_ref, low_ref, out_ref):
    totals = []
    for part in range(2):
        columns = []
        for tile, start in enumerate((OWN * part, OWN * (2 + part), 4 * OWN)):
            pieces = [in_ref[pl.ds(start + k, LAT, stride=LAT_CHUNK), :] for k in range(OWN)]
            row = LAT * part if tile < 2 else 0
            pieces.append(local_ref[row : row + LAT, 128 * tile : 128 * tile + 128])
            columns.append(jnp.concatenate(pieces + [jnp.zeros((LAT, 128), f32)], axis=0))
        x = split(jnp.concatenate(columns, axis=1))
        totals.append(dot3((high_ref[part], low_ref[part]), x))
    both = totals[0][:, :256] + totals[1][:, :256]
    g0, g1 = totals[0][:, 256:], totals[1][:, 256:]
    first = lane_slot(8) % 2 == 0
    last = jnp.where(
        first,
        g0[:256] + pltpu.roll(g1[:256], 120, 1),
        pltpu.roll(g0[256:], 8, 1) + g1[256:],
    )
    for q in range(LON):
        base = LON_CHUNK * q
        for tile in range(2):
            for half in range(2):
                row = 256 * half + 16 * q
                start = base + 28 * tile + 14 * half
                out_ref[start : start + 14] = both[row : row + 14, 128 * tile : 128 * tile + 128]
        out_ref[base + 56 : base + 70] = last[16 * q : 16 * q + 14]


def mlp_kernel(in_ref, gain_ref, up_ref, down_ref, out_hbm, x_ref, y_ref, sent):
    first = lane_slot(8) % 2 == 0
    for j in range(5):
        blocks = []
        for b in range(8):
            pair, place = divmod(8 * j + b, 5)
            even, odd = 2 * pair * LON_CHUNK, (2 * pair + 1) * LON_CHUNK
            if place == 2:
                e, o = in_ref[even + 56 : even + 70], in_ref[odd + 56 : odd + 70]
                top = jnp.where(first, e, pltpu.roll(o, 8, 1))
                bottom = jnp.where(first, pltpu.roll(e, 120, 1), o)
                blocks.append(jnp.concatenate([top, bottom], axis=0))
            else:
                base = (even, even + 28, None, odd, odd + 28)[place]
                blocks.append(in_ref[base : base + 28])
        for i, value in enumerate(swap_blocks(blocks, 16)):
            x_ref[:, i, 128 * j : 128 * j + 128] = value
    x = x_ref[...].reshape(COLS * ROWS, CHANNELS)
    average = jnp.mean(x, axis=-1, keepdims=True)
    centred = x - average
    spread = jnp.mean(centred * centred, axis=-1, keepdims=True)
    normed = (centred * lax.rsqrt(spread + 1e-05) * gain_ref[...].reshape(1, CHANNELS)).astype(bf16)
    active = []
    for n in range(5):
        hidden = dot(normed, up_ref[:, 256 * n : 256 * n + 256])
        active.append(jax.nn.gelu(hidden, approximate=True).astype(bf16))
    active = jnp.concatenate(active, axis=1)
    stores = []
    for n, (start, width) in enumerate(((0, 256), (256, 256), (512, 128))):
        lanes = pl.ds(start, width)
        total = x[:, start : start + width] + dot(active, down_ref[:, start : start + width])
        y_ref[:, :, start : start + width] = total.reshape(COLS, ROWS, width)
        stores.append(pltpu.make_async_copy(y_ref.at[:, :, lanes], out_hbm.at[:, :, lanes], sent.at[n]))
        stores[n].start()
    for store in stores:
        store.wait()


def vmem(count):
    return [pl.BlockSpec(memory_space=pltpu.VMEM)] * count


def run(kernel, shape, *operands, scratch=(), cost=(0, 0), grant=24, far=0, out=pltpu.VMEM):
    return pl.pallas_call(
        kernel,
        out_shape=jax.ShapeDtypeStruct(shape, f32),
        in_specs=vmem(len(operands) - far) + [pl.BlockSpec(memory_space=pltpu.HBM)] * far,
        out_specs=pl.BlockSpec(memory_space=out),
        scratch_shapes=list(scratch),
        compiler_params=pltpu.CompilerParams(vmem_limit_bytes=grant << 20),
        cost_estimate=pl.CostEstimate(flops=cost[0], bytes_accessed=cost[1], transcendentals=0),
    )(*operands)


def legendre(*operands):
    table = jax.ShapeDtypeStruct((OWN, MODES, NLAT), bf16)
    return pl.pallas_call(
        legendre_kernel,
        out_shape=(table, table),
        in_specs=[pl.BlockSpec(memory_space=pltpu.SMEM)] + vmem(2),
        out_specs=vmem(2),
        scratch_shapes=[pltpu.VMEM((8 * MODES, 128), f32)] * 2,
        compiler_params=pltpu.CompilerParams(vmem_limit_bytes=16 << 20),
        cost_estimate=pl.CostEstimate(flops=10**7, bytes_accessed=10**7, transcendentals=0),
    )(*operands)


def wave_np():
    angle = 2.0 * np.pi * (MODES + np.arange(LAT)) / NLON
    waves = [np.cos(angle), np.cos(2.0 * angle), np.sin(angle), np.sin(2.0 * angle)]
    return np.repeat(np.stack(waves, axis=1), 128, axis=1).astype(np.float32)


def exchange(array, axis, count):
    rows = array.shape[0] // count
    shape = (count, rows, 128) if rows % 8 == 0 else (count, 1, rows * 128)
    moved = lax.all_to_all(array.reshape(shape), axis, split_axis=0, concat_axis=0, tiled=True)
    return moved.reshape(array.shape)


def per_device(latent, conv_first, conv_second, filter_gains, norm_gain, up_weight, down_weight):
    band = lax.axis_index("lat")
    sector = lax.axis_index("lon")
    odd = sector % 2 == 1
    forward, inverse = fourier_np()
    forward, inverse = split_np(forward), split_np(inverse)
    angles = jnp.asarray(latitude_np())

    packed = run(
        pack_kernel,
        (LON * LON_CHUNK, 128),
        latent.transpose(1, 0, 2),
        scratch=[
            pltpu.VMEM((COLS, ROWS, CHANNELS), f32),
            pltpu.SemaphoreType.DMA((5,)),
        ],
        far=1,
        grant=53,
    )
    circles = exchange(packed, "lon", LON)

    shapes = ((LAT * LAT_CHUNK, 128), (2 * LAT, 384))
    coeffs, local = pl.pallas_call(
        forward_kernel,
        out_shape=tuple(jax.ShapeDtypeStruct(shape, f32) for shape in shapes),
        in_specs=vmem(3),
        out_specs=vmem(2),
        compiler_params=pltpu.CompilerParams(vmem_limit_bytes=24 << 20),
    )(circles, *map(jnp.asarray, forward))
    orders = exchange(coeffs, "lat", LAT)
    local, conv_first, conv_second, band = lax.optimization_barrier(
        (local, conv_first, conv_second, band)
    )
    seeds = lax.dynamic_index_in_dim(jnp.asarray(seed_np()), band, 0, False)
    owner = band.astype(jnp.int32).reshape(1)
    high, low = legendre(owner, angles, seeds)
    phases = lax.dynamic_index_in_dim(jnp.asarray(phase_np()), band, 0, False)
    place = jnp.stack([band, odd, sector]).astype(jnp.int32)
    shapes = ((576, 640), (3 * LAT, 128), (3 * LAT, 128))
    taps, up, down = pl.pallas_call(
        taps_kernel,
        out_shape=tuple(jax.ShapeDtypeStruct(shape, f32) for shape in shapes),
        in_specs=[pl.BlockSpec(memory_space=pltpu.SMEM)] + vmem(6),
        out_specs=vmem(3),
        compiler_params=pltpu.CompilerParams(vmem_limit_bytes=16 << 20),
        cost_estimate=pl.CostEstimate(flops=10**7, bytes_accessed=10**7, transcendentals=0),
    )(place, conv_first, conv_second, phases, local, filter_gains.T, jnp.asarray(wave_np()))
    rising = [(n, n + 1) for n in range(LAT - 1)]
    below = lax.ppermute(up, "lat", rising)
    above = lax.ppermute(down, "lat", [(target, source) for source, target in rising])
    stay = pl.pallas_call(
        local_kernel,
        out_shape=jax.ShapeDtypeStruct((2 * LAT, 384), f32),
        in_specs=[pl.BlockSpec(memory_space=pltpu.SMEM)] + vmem(4),
        out_specs=vmem(1)[0],
        compiler_params=pltpu.CompilerParams(vmem_limit_bytes=16 << 20),
        cost_estimate=pl.CostEstimate(flops=10**7, bytes_accessed=10**6, transcendentals=0),
    )(place, local, below, above, taps)
    orders, taps, high, low = lax.optimization_barrier((orders, taps, high, low))
    state = pltpu.VMEM((2, 2, 12, SLICE, 128), f32)
    third = run(
        spectral_kernel,
        (LAT * LAT_CHUNK, 128),
        orders,
        high,
        low,
        taps,
        angles,
        scratch=[state, state, pltpu.VMEM((OWN, 2 * SLICE, NLAT), f32)],
    )
    returned = exchange(third, "lat", LAT)
    restored = run(inverse_kernel, (LON * LON_CHUNK, 128), returned, stay, *map(jnp.asarray, inverse))
    arrived = exchange(restored, "lon", LON)
    result = run(
        mlp_kernel,
        (COLS, ROWS, CHANNELS),
        arrived,
        norm_gain,
        up_weight,
        down_weight,
        scratch=[
            pltpu.VMEM((COLS, ROWS, CHANNELS), f32),
            pltpu.VMEM((COLS, ROWS, CHANNELS), f32),
            pltpu.SemaphoreType.DMA((3,)),
        ],
        out=pltpu.HBM,
    )
    return result.transpose(1, 0, 2)


def solution(mesh):
    return jax.shard_map(
        per_device,
        mesh=mesh,
        in_specs=(P("lat", "lon", None), P(), P(), P(None, "lon"), P(), P(), P()),
        out_specs=P("lat", "lon", None),
        check_vma=False,
    )
```

```python
import math

import jax
import jax.numpy as jnp
import numpy as np
from jax import lax
from jax.experimental import pallas as pl
from jax.experimental.pallas import tpu as pltpu
from jax.sharding import PartitionSpec as P

ROWS, COLS, CHANNELS, HIDDEN = 8, 28, 640, 1280
LAT, LON, SLICE = 32, 16, 40
NLAT, NLON, MODES = 256, 448, 192
OWN = MODES // LAT
KEPT = OWN + 1
LON_CHUNK = 70
LAT_CHUNK = 30
f32, bf16 = jnp.float32, jnp.bfloat16


def split_np(table):
    high = table.astype(np.float32).astype(jnp.bfloat16)
    low = (table - high.astype(np.float64)).astype(np.float32).astype(jnp.bfloat16)
    return high, low


def order_of(owner, slot):
    return owner * OWN + slot if slot < OWN else MODES + owner


def fourier_np():
    half, sector, step = np.meshgrid(np.arange(2), np.arange(LON), np.arange(16), indexing="ij")
    place = (sector * COLS + half * 14 + step).reshape(-1)
    valid = (step < 14).reshape(-1)
    forward = np.zeros((2, KEPT, LAT, 512))
    inverse = np.zeros((2, 512, 8, LAT))
    for slot in range(KEPT):
        for owner in range(LAT):
            order = order_of(owner, slot)
            angle = 2.0 * np.pi * ((order * place) % NLON) / NLON
            double = 1.0 if order == 0 else 2.0
            real, imag = np.cos(angle), -np.sin(angle)
            if order == 0:
                imag = np.cos(np.pi * (place % 2))
            forward[0, slot, owner] = real / NLON * valid
            forward[1, slot, owner] = imag / NLON * valid
            inverse[0, :, slot, owner] = real * double * valid
            inverse[1, :, slot, owner] = imag * double * valid
    return forward.reshape(2 * KEPT * LAT, 512), inverse.reshape(2, 512, 8 * LAT)


FACTOR_TILES = ((0, 1, 2), (3, 3, 4))


def phase_np():
    table = np.zeros((LAT, 8, 5, 4))
    for owner in range(LAT):
        for slot in range(OWN):
            order = order_of(owner, slot)
            real, second, imag = FACTOR_TILES[slot // 4]
            for b in range(-2, 3):
                angle = 2.0 * np.pi * ((order * b) % NLON) / NLON
                table[owner, b + 2, real, slot % 4] = np.cos(angle)
                if second != real:
                    table[owner, b + 2, second, slot % 4] = np.cos(np.pi * b) if order == 0 else np.cos(angle)
                table[owner, b + 2, imag, slot % 4] = np.sin(angle)
    return table.reshape(LAT, 8, 20).astype(np.float32)


def latitude_np():
    e, q = np.meshgrid(np.arange(ROWS), np.arange(LAT), indexing="ij")
    theta = np.pi * ((q * ROWS + e).reshape(-1) + 0.5) / NLAT
    weight = 2.0 * np.pi * np.pi * np.sin(theta) / NLAT
    rows = np.stack([np.cos(theta), np.log(np.sin(theta)), weight])
    return np.concatenate([rows, np.zeros((5, NLAT))]).astype(np.float32)


def seed_np():
    seeds = np.zeros((LAT, 8, 128), np.float32)
    for m in range(MODES):
        value = 0.5 * (
            math.log((2 * m + 1) / (4 * math.pi))
            + math.lgamma(2 * m + 1)
            - 2 * m * math.log(2)
            - 2 * math.lgamma(m + 1)
        )
        seeds[m // OWN, m % OWN] = value
    return seeds


def lane_slot(width):
    return lax.broadcasted_iota(jnp.int32, (1, 128), 1) // width


def swap_blocks(values, width):
    values = list(values)
    step = len(values) // 2
    while step:
        shift = step * width
        first = lane_slot(shift) % 2 == 0
        for a in range(len(values)):
            if not a & step:
                low, high = values[a], values[a | step]
                values[a] = jnp.where(first, low, pltpu.roll(high, shift, 1))
                values[a | step] = jnp.where(first, pltpu.roll(low, 128 - shift, 1), high)
        step //= 2
    return values


def split(value):
    high = value.astype(bf16)
    return high, (value - high.astype(f32)).astype(bf16)


def dot(a, b, dims=((1,), (0,))):
    return lax.dot_general(a, b, (dims, ((), ())), preferred_element_type=f32)


def dot3(a, b, dims=((1,), (0,))):
    rows = a[0].shape[0]
    both = dot(jnp.concatenate(a, axis=0), b[0], dims)
    return both[:rows] + (both[rows:] + dot(a[0], b[1], dims))


def pack_kernel(x_hbm, out_ref, x_ref, arrivals):
    first = lane_slot(8) % 2 == 0
    fetches = []
    for j in range(5):
        lanes = pl.ds(128 * j, 128)
        fetches.append(pltpu.make_async_copy(x_hbm.at[:, :, lanes], x_ref.at[:, :, lanes], arrivals.at[j]))
        fetches[j].start()
    for j in range(5):
        fetches[j].wait()
        blocks = swap_blocks([x_ref[:, i, 128 * j : 128 * j + 128] for i in range(ROWS)], 16)
        for b in range(8):
            pair, place = divmod(8 * j + b, 5)
            even, odd = 2 * pair * LON_CHUNK, (2 * pair + 1) * LON_CHUNK
            block = blocks[b]
            if place == 2:
                top, bottom = block[:14], block[14:]
                out_ref[even + 56 : even + 70] = jnp.where(first, top, pltpu.roll(bottom, 8, 1))
                out_ref[odd + 56 : odd + 70] = jnp.where(first, pltpu.roll(top, 120, 1), bottom)
            else:
                base = (even, even + 28, None, odd, odd + 28)[place]
                out_ref[base : base + 28] = block


def forward_kernel(in_ref, high_ref, low_ref, out_ref, local_ref):
    totals = []
    for half in range(2):
        pieces = []
        for start in (14 * half, 28 + 14 * half, 56):
            blocks = [in_ref[LON_CHUNK * q + start : LON_CHUNK * q + start + 16] for q in range(LON - 1)]
            tail = LON_CHUNK * (LON - 1) + start
            blocks += [in_ref[tail : tail + 14], jnp.zeros((2, 128), f32)]
            pieces.append(jnp.concatenate(blocks, axis=0))
        x = split(jnp.concatenate(pieces, axis=1))
        lanes = slice(256 * half, 256 * half + 256)
        totals.append(dot3((high_ref[:, lanes], low_ref[:, lanes]), x))
    both = totals[0][:, :256] + totals[1][:, :256]
    g0, g1 = totals[0][:, 256:], totals[1][:, 256:]
    half_rows = KEPT * LAT
    first = lane_slot(8) % 2 == 0
    last = jnp.where(
        first,
        g0[:half_rows] + pltpu.roll(g1[:half_rows], 120, 1),
        pltpu.roll(g0[half_rows:], 8, 1) + g1[half_rows:],
    )
    for r in range(2):
        for k in range(OWN):
            part = both[LAT * (KEPT * r + k) : LAT * (KEPT * r + k) + LAT]
            row = OWN * r + k
            out_ref[pl.ds(row, LAT, stride=LAT_CHUNK), :] = part[:, :128]
            out_ref[pl.ds(2 * OWN + row, LAT, stride=LAT_CHUNK), :] = part[:, 128:]
    for k in range(OWN):
        out_ref[pl.ds(4 * OWN + k, LAT, stride=LAT_CHUNK), :] = last[LAT * k : LAT * k + LAT]
    for r in range(2):
        rows = slice(LAT * r, LAT * r + LAT)
        local_ref[rows, :256] = both[LAT * (KEPT * r + OWN) : LAT * (KEPT * r + OWN) + LAT]
    local_ref[0:LAT, 256:] = last[LAT * OWN : LAT * OWN + LAT]
    local_ref[LAT:, 256:] = jnp.zeros((LAT, 128), f32)


def local_kernel(own_ref, below_ref, above_ref, taps_ref, out_ref):
    lane = lax.broadcasted_iota(jnp.int32, (1, 128), 1)
    left = lane < 64
    masks = (taps_ref[576:577, :128], taps_ref[577:578, :128])

    def extend(own, below, above):
        turned = pltpu.roll(own, 64, 1)
        return jnp.where(left, below, turned), jnp.where(left, turned, above)

    def turn(value):
        return pltpu.roll(value, 64, 1)

    def shifted(tiles, a):
        if a == 0:
            return tiles
        amount = (-16 * a) % 128
        first, second = (pltpu.roll(tile, amount, 1) for tile in tiles)
        if a > 0:
            keep = lane < 128 - 16 * a
            return jnp.where(keep, first, second), jnp.where(keep, second, first)
        keep = lane >= -16 * a
        return jnp.where(keep, first, second), jnp.where(keep, second, first)

    def weights(which, a, tile):
        start = 480 + 32 * which + 5 * a
        rows = [taps_ref[start + b : start + b + 1, 128 * tile : 128 * tile + 128] for b in range(5)]
        cos1, cos2, sin1, sin2 = (taps_ref[544:576, 128 * n : 128 * n + 128] for n in range(4))
        real = rows[2] + (rows[3] + rows[1]) * cos1 + (rows[4] + rows[0]) * cos2
        imag = (rows[3] - rows[1]) * sin1 + (rows[4] - rows[0]) * sin2
        return real, imag

    for tile in range(2):
        parts = []
        for r in range(2):
            rows = slice(LAT * r, LAT * r + LAT)
            own = own_ref[rows, 128 * tile : 128 * tile + 128]
            below, above = below_ref[rows], above_ref[rows]
            if tile == 0:
                parts.append(extend(own, below, turn(above)))
            else:
                parts.append(extend(own, turn(below), above))
        for which in range(2):
            real, imag = [list(value) for value in parts]
            for a in range(-2, 3):
                w_r, w_i = weights(which, a + 2, tile)
                e_r, e_i = shifted(parts[0], a), shifted(parts[1], a)
                for n in range(2):
                    real[n] = real[n] + (w_r * e_r[n] - w_i * e_i[n])
                    imag[n] = imag[n] + (w_r * e_i[n] + w_i * e_r[n])
            parts = [tuple(v * m for v, m in zip(value, masks)) for value in (real, imag)]
        for r in range(2):
            result = jnp.where(left, turn(parts[r][0]), turn(parts[r][1]))
            out_ref[LAT * r : LAT * r + LAT, 128 * tile : 128 * tile + 128] = result
    second = lane_slot(8) % 2 == 1
    value = extend(own_ref[0:LAT, 256:], turn(below_ref[2 * LAT :]), turn(above_ref[2 * LAT :]))
    for which in range(2):
        total = list(value)
        swapped = [jnp.where(second, pltpu.roll(v, 8, 1), pltpu.roll(v, 120, 1)) for v in value]
        for a in range(-2, 3):
            w_r, w_i = weights(which, a + 2, 2)
            w_i = jnp.where(second, w_i, -w_i)
            e, f = shifted(value, a), shifted(swapped, a)
            for n in range(2):
                total[n] = total[n] + (w_r * e[n] + w_i * f[n])
        value = tuple(v * m for v, m in zip(total, masks))
    out_ref[0:LAT, 256:] = jnp.where(left, turn(value[0]), turn(value[1]))
    out_ref[LAT:, 256:] = jnp.zeros((LAT, 128), f32)


def channel_at(place_ref, local):
    turned = jnp.where(local >= 32, local - 32, local + 8)
    return place_ref[2] * SLICE + jnp.where(place_ref[1] == 1, turned, local)


def pick(a, b, dims):
    return lax.dot_general(a, b, (dims, ((), ())), precision=lax.Precision.HIGHEST, preferred_element_type=f32)


def taps_kernel(place_ref, first_ref, second_ref, phase_ref, local_ref, gain_ref, wave_ref, taps_ref, up_ref, down_ref):
    gain = gain_ref[...]
    gain = jnp.where(place_ref[1] == 1, jnp.concatenate([gain[8:], gain[:8]], axis=0), gain)
    base = 10 * SLICE
    taps_ref[base : base + SLICE, :MODES] = gain
    taps_ref[base + SLICE : base + 2 * SLICE, :MODES] = jnp.where(place_ref[0] == 0, 0.0, gain)
    left = lane_slot(64) == 0
    a, b = local_ref[:, :128], local_ref[:, 128:256]
    up_ref[: 2 * LAT] = jnp.where(left, pltpu.roll(a, 64, 1), b)
    down_ref[: 2 * LAT] = jnp.where(left, a, pltpu.roll(b, 64, 1))
    up_ref[2 * LAT :] = local_ref[:LAT, 256:]
    down_ref[2 * LAT :] = local_ref[:LAT, 256:]
    taps_ref[544:576, :512] = wave_ref[...]
    south = jnp.where(place_ref[0] == 0, 0.0, 1.0)
    north = jnp.where(place_ref[0] == LAT - 1, 0.0, 1.0)
    row = lax.broadcasted_iota(jnp.int32, (8, 128), 0)
    edges = jnp.where(row == 0, jnp.where(left, south, 1.0), jnp.where(left, 1.0, north))
    taps_ref[576:584, :128] = edges
    shape = (CHANNELS, 384)
    at = lax.broadcasted_iota(jnp.int32, shape, 1)
    tail = at % 8 + 32
    at = jnp.where(at >= 256, tail, at // 128 * 16 + at % 16)
    chosen = (lax.broadcasted_iota(jnp.int32, shape, 0) == channel_at(place_ref, at)).astype(f32)
    taps_ref[480:505, :384] = pick(first_ref[...], chosen, ((1,), (0,)))
    taps_ref[512:537, :384] = pick(second_ref[...], chosen, ((1,), (0,)))
    shape = (SLICE, CHANNELS)
    wanted = channel_at(place_ref, lax.broadcasted_iota(jnp.int32, shape, 0))
    chosen = (lax.broadcasted_iota(jnp.int32, shape, 1) == wanted).astype(f32)
    rows = [pick(chosen, ref[...], ((1,), (1,))) for ref in (first_ref, second_ref)]
    for tile in range(5):
        phase = phase_ref[:, 4 * tile : 4 * tile + 1]
        for n in range(1, 4):
            column = phase_ref[:, 4 * tile + n : 4 * tile + n + 1]
            phase = jnp.where(lane_slot(LAT) >= n, column, phase)
        for which in range(2):
            for a in range(5):
                total = rows[which][:, 5 * a : 5 * a + 1] * phase[0:1]
                for b in range(1, 5):
                    total = total + rows[which][:, 5 * a + b : 5 * a + b + 1] * phase[b : b + 1]
                base = (5 * which + a) * SLICE
                taps_ref[base : base + SLICE, 128 * tile : 128 * tile + 128] = total


def legendre_kernel(owner_ref, angle_ref, seed_ref, high_ref, low_ref, left_ref, right_ref):
    slot = lax.broadcasted_iota(jnp.int32, (8, 256), 0)
    order_at = jnp.where(slot < OWN, owner_ref[0] * OWN + slot, 2 * MODES)
    order = order_at.astype(f32)
    degree = lax.broadcasted_iota(jnp.int32, (8, 256), 1).astype(f32)
    square, below = degree * degree, (degree - 1.0) * (degree - 1.0)
    upper = jnp.sqrt(
        jnp.maximum(4.0 * square - 1.0, 1.0) / jnp.maximum(square - order * order, 1.0)
    )
    lower = jnp.sqrt(
        jnp.maximum(below - order * order, 0.0) / jnp.maximum(4.0 * below - 1.0, 1.0)
    )
    product = upper * lower
    cosine = jnp.broadcast_to(angle_ref[0:1, :], (8, 256))
    diagonal = jnp.exp(seed_ref[:, 0:1] + order * angle_ref[1:2, :])
    previous = jnp.zeros((8, 256), f32)
    earlier = previous
    for l in range(MODES):
        current = jnp.where(
            order_at == l,
            diagonal,
            (upper[:, l : l + 1] * cosine) * previous - product[:, l : l + 1] * earlier,
        )
        left_ref[8 * l : 8 * l + 8] = current[:, :128]
        right_ref[8 * l : 8 * l + 8] = current[:, 128:]
        previous, earlier = current, previous
    for k in range(OWN):
        for part, source in enumerate((left_ref, right_ref)):
            high, low = split(source[pl.ds(k, MODES, stride=8), :])
            high_ref[k, :, 128 * part : 128 * part + 128] = high
            low_ref[k, :, 128 * part : 128 * part + 128] = low

def spectral_kernel(in_ref, high_ref, low_ref, taps_ref, angle_ref, out_ref, u_ref, v_ref, f_ref):
    lane = lax.broadcasted_iota(jnp.int32, (1, 128), 1) % LAT

    def fill_edges(ref):
        for part in range(2):
            for group in range(2):
                for e in (0, 1):
                    block = pltpu.roll(ref[part, group, 2 + e], 127, 1)
                    ref[part, group, 10 + e] = jnp.where(lane == LAT - 1, 0.0, block)
                    block = pltpu.roll(ref[part, group, 8 + e], 1, 1)
                    ref[part, group, e] = jnp.where(lane == 0, 0.0, block)

    def stencil(ref, which, store):
        for group in range(2):
            for tile in range(5):
                rows = slice(8 * tile, 8 * tile + 8)
                taps = []
                for a in range(5):
                    base = (which * 5 + a) * SLICE + 8 * tile
                    taps.append(
                        [
                            taps_ref[base : base + 8, 128 * column : 128 * column + 128]
                            for column in FACTOR_TILES[group]
                        ]
                    )
                real = [ref[0, group, e, rows] for e in range(12)]
                imag = [ref[1, group, e, rows] for e in range(12)]
                for e in range(ROWS):
                    total_r, total_i = real[e + 2], imag[e + 2]
                    for a in range(5):
                        r_tap, s_tap, i_tap = taps[a]
                        total_r = total_r + (r_tap * real[e + a] - i_tap * imag[e + a])
                        total_i = total_i + (s_tap * imag[e + a] + i_tap * real[e + a])
                    store(group, rows, e, total_r, total_i)

    def rows_of(start, count):
        pieces = [in_ref[pl.ds(start + n, LAT, stride=LAT_CHUNK), :] for n in range(count)]
        if count < 4:
            pieces.append(jnp.zeros((LAT * (4 - count), 128), f32))
        return jnp.concatenate(pieces, axis=0).T

    for group in range(2):
        count = min(4, OWN - 4 * group)
        for tile in range(2):
            for part in range(2):
                block = rows_of(OWN * (2 * tile + part) + 4 * group, count)
                for e in range(ROWS):
                    u_ref[part, group, 2 + e, 16 * tile : 16 * tile + 16] = block[16 * e : 16 * e + 16]
        block = rows_of(4 * OWN + 4 * group, count)
        for e in range(ROWS):
            for part in range(2):
                start = 16 * e + 8 * part
                u_ref[part, group, 2 + e, 32:40] = block[start : start + 8]
    fill_edges(u_ref)

    def keep_first(group, rows, e, total_r, total_i):
        v_ref[0, group, 2 + e, rows] = total_r
        v_ref[1, group, 2 + e, rows] = total_i

    stencil(u_ref, 0, keep_first)

    weight = angle_ref[2:3, :]
    for part in range(2):
        for group in range(2):
            halves = [
                swap_blocks([v_ref[part, group, 2 + 4 * j + e] for e in range(4)], 32) for j in range(2)
            ]
            for n in range(4):
                if 4 * group + n < OWN:
                    f_ref[4 * group + n, SLICE * part : SLICE * part + SLICE] = (
                        jnp.concatenate([halves[0][n], halves[1][n]], axis=1) * weight
                    )
    gain, masked = (taps_ref[SLICE * n : SLICE * n + SLICE, :MODES] for n in (10, 11))
    for k in range(OWN):
        table = (high_ref[k], low_ref[k])
        spectrum = dot3(split(f_ref[k]), table, ((1,), (1,)))
        second = masked if k == 0 else gain
        f_ref[k] = dot3(split(spectrum * jnp.concatenate([gain, second], axis=0)), table)
    for part in range(2):
        for group in range(2):
            rows = slice(SLICE * part, SLICE * part + SLICE)
            for j in range(2):
                values = [
                    f_ref[4 * group + n, rows, 128 * j : 128 * j + 128]
                    if 4 * group + n < OWN
                    else jnp.zeros((SLICE, 128), f32)
                    for n in range(4)
                ]
                for e, value in enumerate(swap_blocks(values, 32)):
                    v_ref[part, group, 2 + 4 * j + e] = v_ref[part, group, 2 + 4 * j + e] + value
    fill_edges(v_ref)

    def keep_second(group, rows, e, total_r, total_i):
        u_ref[0, group, 2 + e, rows] = total_r
        u_ref[1, group, 2 + e, rows] = total_i

    stencil(v_ref, 1, keep_second)

    def give(start, count, pieces):
        block = jnp.concatenate(pieces, axis=0).T
        for n in range(count):
            out_ref[pl.ds(start + n, LAT, stride=LAT_CHUNK), :] = block[LAT * n : LAT * n + LAT]

    for group in range(2):
        count = min(4, OWN - 4 * group)
        for tile in range(2):
            for part in range(2):
                give(
                    OWN * (2 * tile + part) + 4 * group,
                    count,
                    [u_ref[part, group, 2 + e, 16 * tile : 16 * tile + 16] for e in range(ROWS)],
                )
        give(
            4 * OWN + 4 * group,
            count,
            [u_ref[part, group, 2 + e, 32:40] for e in range(ROWS) for part in range(2)],
        )


def inverse_kernel(in_ref, local_ref, high_ref, low_ref, out_ref):
    totals = []
    for part in range(2):
        columns = []
        for tile, start in enumerate((OWN * part, OWN * (2 + part), 4 * OWN)):
            pieces = [in_ref[pl.ds(start + k, LAT, stride=LAT_CHUNK), :] for k in range(OWN)]
            row = LAT * part if tile < 2 else 0
            pieces.append(local_ref[row : row + LAT, 128 * tile : 128 * tile + 128])
            columns.append(jnp.concatenate(pieces + [jnp.zeros((LAT, 128), f32)], axis=0))
        x = split(jnp.concatenate(columns, axis=1))
        totals.append(dot3((high_ref[part], low_ref[part]), x))
    both = totals[0][:, :256] + totals[1][:, :256]
    g0, g1 = totals[0][:, 256:], totals[1][:, 256:]
    first = lane_slot(8) % 2 == 0
    last = jnp.where(
        first,
        g0[:256] + pltpu.roll(g1[:256], 120, 1),
        pltpu.roll(g0[256:], 8, 1) + g1[256:],
    )
    for q in range(LON):
        base = LON_CHUNK * q
        for tile in range(2):
            for half in range(2):
                row = 256 * half + 16 * q
                start = base + 28 * tile + 14 * half
                out_ref[start : start + 14] = both[row : row + 14, 128 * tile : 128 * tile + 128]
        out_ref[base + 56 : base + 70] = last[16 * q : 16 * q + 14]


def mlp_kernel(in_ref, gain_ref, up_ref, down_ref, out_hbm, x_ref, y_ref, sent):
    first = lane_slot(8) % 2 == 0
    for j in range(5):
        blocks = []
        for b in range(8):
            pair, place = divmod(8 * j + b, 5)
            even, odd = 2 * pair * LON_CHUNK, (2 * pair + 1) * LON_CHUNK
            if place == 2:
                e, o = in_ref[even + 56 : even + 70], in_ref[odd + 56 : odd + 70]
                top = jnp.where(first, e, pltpu.roll(o, 8, 1))
                bottom = jnp.where(first, pltpu.roll(e, 120, 1), o)
                blocks.append(jnp.concatenate([top, bottom], axis=0))
            else:
                base = (even, even + 28, None, odd, odd + 28)[place]
                blocks.append(in_ref[base : base + 28])
        for i, value in enumerate(swap_blocks(blocks, 16)):
            x_ref[:, i, 128 * j : 128 * j + 128] = value
    x = x_ref[...].reshape(COLS * ROWS, CHANNELS)
    average = jnp.mean(x, axis=-1, keepdims=True)
    centred = x - average
    spread = jnp.mean(centred * centred, axis=-1, keepdims=True)
    normed = (centred * lax.rsqrt(spread + 1e-05) * gain_ref[...].reshape(1, CHANNELS)).astype(bf16)
    active = []
    for n in range(5):
        hidden = dot(normed, up_ref[:, 256 * n : 256 * n + 256])
        active.append(jax.nn.gelu(hidden, approximate=True).astype(bf16))
    active = jnp.concatenate(active, axis=1)
    stores = []
    for n, (start, width) in enumerate(((0, 256), (256, 256), (512, 128))):
        lanes = pl.ds(start, width)
        total = x[:, start : start + width] + dot(active, down_ref[:, start : start + width])
        y_ref[:, :, start : start + width] = total.reshape(COLS, ROWS, width)
        stores.append(pltpu.make_async_copy(y_ref.at[:, :, lanes], out_hbm.at[:, :, lanes], sent.at[n]))
        stores[n].start()
    for store in stores:
        store.wait()


def vmem(count):
    return [pl.BlockSpec(memory_space=pltpu.VMEM)] * count


def run(kernel, shape, *operands, scratch=(), cost=(0, 0), grant=24, far=0, out=pltpu.VMEM):
    return pl.pallas_call(
        kernel,
        out_shape=jax.ShapeDtypeStruct(shape, f32),
        in_specs=vmem(len(operands) - far) + [pl.BlockSpec(memory_space=pltpu.HBM)] * far,
        out_specs=pl.BlockSpec(memory_space=out),
        scratch_shapes=list(scratch),
        compiler_params=pltpu.CompilerParams(vmem_limit_bytes=grant << 20),
        cost_estimate=pl.CostEstimate(flops=cost[0], bytes_accessed=cost[1], transcendentals=0),
    )(*operands)


def legendre(*operands):
    table = jax.ShapeDtypeStruct((OWN, MODES, NLAT), bf16)
    return pl.pallas_call(
        legendre_kernel,
        out_shape=(table, table),
        in_specs=[pl.BlockSpec(memory_space=pltpu.SMEM)] + vmem(2),
        out_specs=vmem(2),
        scratch_shapes=[pltpu.VMEM((8 * MODES, 128), f32)] * 2,
        compiler_params=pltpu.CompilerParams(vmem_limit_bytes=16 << 20),
        cost_estimate=pl.CostEstimate(flops=10**7, bytes_accessed=10**7, transcendentals=0),
    )(*operands)


def wave_np():
    angle = 2.0 * np.pi * (MODES + np.arange(LAT)) / NLON
    waves = [np.cos(angle), np.cos(2.0 * angle), np.sin(angle), np.sin(2.0 * angle)]
    return np.repeat(np.stack(waves, axis=1), 128, axis=1).astype(np.float32)


def exchange(array, axis, count):
    rows = array.shape[0] // count
    shape = (count, rows, 128) if rows % 8 == 0 else (count, 1, rows * 128)
    moved = lax.all_to_all(array.reshape(shape), axis, split_axis=0, concat_axis=0, tiled=True)
    return moved.reshape(array.shape)


def per_device(latent, conv_first, conv_second, filter_gains, norm_gain, up_weight, down_weight):
    band = lax.axis_index("lat")
    sector = lax.axis_index("lon")
    odd = sector % 2 == 1
    forward, inverse = fourier_np()
    forward, inverse = split_np(forward), split_np(inverse)
    angles = jnp.asarray(latitude_np())

    packed = run(
        pack_kernel,
        (LON * LON_CHUNK, 128),
        latent.transpose(1, 0, 2),
        scratch=[
            pltpu.VMEM((COLS, ROWS, CHANNELS), f32),
            pltpu.SemaphoreType.DMA((5,)),
        ],
        far=1,
        grant=53,
    )
    circles = exchange(packed, "lon", LON)

    shapes = ((LAT * LAT_CHUNK, 128), (2 * LAT, 384))
    coeffs, local = pl.pallas_call(
        forward_kernel,
        out_shape=tuple(jax.ShapeDtypeStruct(shape, f32) for shape in shapes),
        in_specs=vmem(3),
        out_specs=vmem(2),
        compiler_params=pltpu.CompilerParams(vmem_limit_bytes=24 << 20),
    )(circles, *map(jnp.asarray, forward))
    orders = exchange(coeffs, "lat", LAT)
    local, conv_first, conv_second, band = lax.optimization_barrier(
        (local, conv_first, conv_second, band)
    )
    seeds = lax.dynamic_index_in_dim(jnp.asarray(seed_np()), band, 0, False)
    owner = band.astype(jnp.int32).reshape(1)
    high, low = legendre(owner, angles, seeds)
    phases = lax.dynamic_index_in_dim(jnp.asarray(phase_np()), band, 0, False)
    place = jnp.stack([band, odd, sector]).astype(jnp.int32)
    shapes = ((584, 640), (3 * LAT, 128), (3 * LAT, 128))
    taps, up, down = pl.pallas_call(
        taps_kernel,
        out_shape=tuple(jax.ShapeDtypeStruct(shape, f32) for shape in shapes),
        in_specs=[pl.BlockSpec(memory_space=pltpu.SMEM)] + vmem(6),
        out_specs=vmem(3),
        compiler_params=pltpu.CompilerParams(vmem_limit_bytes=16 << 20),
        cost_estimate=pl.CostEstimate(flops=10**7, bytes_accessed=10**7, transcendentals=0),
    )(place, conv_first, conv_second, phases, local, filter_gains.T, jnp.asarray(wave_np()))
    rising = [(n, n + 1) for n in range(LAT - 1)]
    below = lax.ppermute(up, "lat", rising)
    above = lax.ppermute(down, "lat", [(target, source) for source, target in rising])
    stay = pl.pallas_call(
        local_kernel,
        out_shape=jax.ShapeDtypeStruct((2 * LAT, 384), f32),
        in_specs=vmem(4),
        out_specs=vmem(1)[0],
        compiler_params=pltpu.CompilerParams(vmem_limit_bytes=16 << 20),
        cost_estimate=pl.CostEstimate(flops=10**7, bytes_accessed=10**6, transcendentals=0),
    )(local, below, above, taps)
    orders, taps, high, low = lax.optimization_barrier((orders, taps, high, low))
    state = pltpu.VMEM((2, 2, 12, SLICE, 128), f32)
    third = run(
        spectral_kernel,
        (LAT * LAT_CHUNK, 128),
        orders,
        high,
        low,
        taps,
        angles,
        scratch=[state, state, pltpu.VMEM((OWN, 2 * SLICE, NLAT), f32)],
    )
    returned = exchange(third, "lat", LAT)
    restored = run(inverse_kernel, (LON * LON_CHUNK, 128), returned, stay, *map(jnp.asarray, inverse))
    arrived = exchange(restored, "lon", LON)
    result = run(
        mlp_kernel,
        (COLS, ROWS, CHANNELS),
        arrived,
        norm_gain,
        up_weight,
        down_weight,
        scratch=[
            pltpu.VMEM((COLS, ROWS, CHANNELS), f32),
            pltpu.VMEM((COLS, ROWS, CHANNELS), f32),
            pltpu.SemaphoreType.DMA((3,)),
        ],
        out=pltpu.HBM,
    )
    return result.transpose(1, 0, 2)


def solution(mesh):
    return jax.shard_map(
        per_device,
        mesh=mesh,
        in_specs=(P("lat", "lon", None), P(), P(), P(None, "lon"), P(), P(), P()),
        out_specs=P("lat", "lon", None),
        check_vma=False,
    )
```

```python
import math

import jax
import jax.numpy as jnp
import numpy as np
from jax import lax
from jax.experimental import pallas as pl
from jax.experimental.pallas import tpu as pltpu
from jax.sharding import PartitionSpec as P

ROWS, COLS, CHANNELS, HIDDEN = 8, 28, 640, 1280
LAT, LON, SLICE = 32, 16, 40
NLAT, NLON, MODES = 256, 448, 192
OWN = MODES // LAT
KEPT = OWN + 1
LON_CHUNK = 70
LAT_CHUNK = 30
f32, bf16 = jnp.float32, jnp.bfloat16


def split_np(table):
    high = table.astype(np.float32).astype(jnp.bfloat16)
    low = (table - high.astype(np.float64)).astype(np.float32).astype(jnp.bfloat16)
    return high, low


def order_of(owner, slot):
    return owner * OWN + slot if slot < OWN else MODES + owner


def fourier_np():
    half, sector, step = np.meshgrid(np.arange(2), np.arange(LON), np.arange(16), indexing="ij")
    place = (sector * COLS + half * 14 + step).reshape(-1)
    valid = (step < 14).reshape(-1)
    forward = np.zeros((2, KEPT, LAT, 512))
    inverse = np.zeros((2, 512, 8, LAT))
    for slot in range(KEPT):
        for owner in range(LAT):
            order = order_of(owner, slot)
            angle = 2.0 * np.pi * ((order * place) % NLON) / NLON
            double = 1.0 if order == 0 else 2.0
            real, imag = np.cos(angle), -np.sin(angle)
            if order == 0:
                imag = np.cos(np.pi * (place % 2))
            forward[0, slot, owner] = real / NLON * valid
            forward[1, slot, owner] = imag / NLON * valid
            inverse[0, :, slot, owner] = real * double * valid
            inverse[1, :, slot, owner] = imag * double * valid
    return forward.reshape(2 * KEPT * LAT, 512), inverse.reshape(2, 512, 8 * LAT)


FACTOR_TILES = ((0, 1, 2), (3, 3, 4))


def phase_np():
    table = np.zeros((LAT, 8, 5, 4))
    for owner in range(LAT):
        for slot in range(OWN):
            order = order_of(owner, slot)
            real, second, imag = FACTOR_TILES[slot // 4]
            for b in range(-2, 3):
                angle = 2.0 * np.pi * ((order * b) % NLON) / NLON
                table[owner, b + 2, real, slot % 4] = np.cos(angle)
                if second != real:
                    table[owner, b + 2, second, slot % 4] = np.cos(np.pi * b) if order == 0 else np.cos(angle)
                table[owner, b + 2, imag, slot % 4] = np.sin(angle)
    return table.reshape(LAT, 8, 20).astype(np.float32)


def latitude_np():
    e, q = np.meshgrid(np.arange(ROWS), np.arange(LAT), indexing="ij")
    theta = np.pi * ((q * ROWS + e).reshape(-1) + 0.5) / NLAT
    weight = 2.0 * np.pi * np.pi * np.sin(theta) / NLAT
    rows = np.stack([np.cos(theta), np.log(np.sin(theta)), weight])
    return np.concatenate([rows, np.zeros((5, NLAT))]).astype(np.float32)


def seed_np():
    seeds = np.zeros((LAT, 8, 128), np.float32)
    for m in range(MODES):
        value = 0.5 * (
            math.log((2 * m + 1) / (4 * math.pi))
            + math.lgamma(2 * m + 1)
            - 2 * m * math.log(2)
            - 2 * math.lgamma(m + 1)
        )
        seeds[m // OWN, m % OWN] = value
    return seeds


def lane_slot(width):
    return lax.broadcasted_iota(jnp.int32, (1, 128), 1) // width


def swap_blocks(values, width):
    values = list(values)
    step = len(values) // 2
    while step:
        shift = step * width
        first = lane_slot(shift) % 2 == 0
        for a in range(len(values)):
            if not a & step:
                low, high = values[a], values[a | step]
                values[a] = jnp.where(first, low, pltpu.roll(high, shift, 1))
                values[a | step] = jnp.where(first, pltpu.roll(low, 128 - shift, 1), high)
        step //= 2
    return values


def split(value):
    high = value.astype(bf16)
    return high, (value - high.astype(f32)).astype(bf16)


def dot(a, b, dims=((1,), (0,))):
    return lax.dot_general(a, b, (dims, ((), ())), preferred_element_type=f32)


def dot3(a, b, dims=((1,), (0,))):
    rows = a[0].shape[0]
    both = dot(jnp.concatenate(a, axis=0), b[0], dims)
    return both[:rows] + (both[rows:] + dot(a[0], b[1], dims))


def pack_kernel(x_hbm, out_ref, x_ref, arrivals):
    first = lane_slot(8) % 2 == 0
    fetches = []
    for j in range(5):
        lanes = pl.ds(128 * j, 128)
        for part in range(4):
            place = (pl.ds(7 * part, 7), slice(None), lanes)
            fetches.append(pltpu.make_async_copy(x_hbm.at[place], x_ref.at[place], arrivals.at[4 * j + part]))
            fetches[-1].start()
    for j in range(5):
        for fetch in fetches[4 * j : 4 * j + 4]:
            fetch.wait()
        blocks = swap_blocks([x_ref[:, i, 128 * j : 128 * j + 128] for i in range(ROWS)], 16)
        for b in range(8):
            pair, place = divmod(8 * j + b, 5)
            even, odd = 2 * pair * LON_CHUNK, (2 * pair + 1) * LON_CHUNK
            block = blocks[b]
            if place == 2:
                top, bottom = block[:14], block[14:]
                out_ref[even + 56 : even + 70] = jnp.where(first, top, pltpu.roll(bottom, 8, 1))
                out_ref[odd + 56 : odd + 70] = jnp.where(first, pltpu.roll(top, 120, 1), bottom)
            else:
                base = (even, even + 28, None, odd, odd + 28)[place]
                out_ref[base : base + 28] = block


def forward_kernel(in_ref, high_ref, low_ref, out_ref, local_ref):
    totals = []
    for half in range(2):
        pieces = []
        for start in (14 * half, 28 + 14 * half, 56):
            blocks = [in_ref[LON_CHUNK * q + start : LON_CHUNK * q + start + 16] for q in range(LON - 1)]
            tail = LON_CHUNK * (LON - 1) + start
            blocks += [in_ref[tail : tail + 14], jnp.zeros((2, 128), f32)]
            pieces.append(jnp.concatenate(blocks, axis=0))
        x = split(jnp.concatenate(pieces, axis=1))
        lanes = slice(256 * half, 256 * half + 256)
        totals.append(dot3((high_ref[:, lanes], low_ref[:, lanes]), x))
    both = totals[0][:, :256] + totals[1][:, :256]
    g0, g1 = totals[0][:, 256:], totals[1][:, 256:]
    half_rows = KEPT * LAT
    first = lane_slot(8) % 2 == 0
    last = jnp.where(
        first,
        g0[:half_rows] + pltpu.roll(g1[:half_rows], 120, 1),
        pltpu.roll(g0[half_rows:], 8, 1) + g1[half_rows:],
    )
    for r in range(2):
        for k in range(OWN):
            part = both[LAT * (KEPT * r + k) : LAT * (KEPT * r + k) + LAT]
            row = OWN * r + k
            out_ref[pl.ds(row, LAT, stride=LAT_CHUNK), :] = part[:, :128]
            out_ref[pl.ds(2 * OWN + row, LAT, stride=LAT_CHUNK), :] = part[:, 128:]
    for k in range(OWN):
        out_ref[pl.ds(4 * OWN + k, LAT, stride=LAT_CHUNK), :] = last[LAT * k : LAT * k + LAT]
    for r in range(2):
        rows = slice(LAT * r, LAT * r + LAT)
        local_ref[rows, :256] = both[LAT * (KEPT * r + OWN) : LAT * (KEPT * r + OWN) + LAT]
    local_ref[0:LAT, 256:] = last[LAT * OWN : LAT * OWN + LAT]
    local_ref[LAT:, 256:] = jnp.zeros((LAT, 128), f32)


def local_kernel(own_ref, below_ref, above_ref, taps_ref, out_ref):
    lane = lax.broadcasted_iota(jnp.int32, (1, 128), 1)
    left = lane < 64
    masks = (taps_ref[576:577, :128], taps_ref[577:578, :128])

    def extend(own, below, above):
        turned = pltpu.roll(own, 64, 1)
        return jnp.where(left, below, turned), jnp.where(left, turned, above)

    def turn(value):
        return pltpu.roll(value, 64, 1)

    def shifted(tiles, a):
        if a == 0:
            return tiles
        amount = (-16 * a) % 128
        first, second = (pltpu.roll(tile, amount, 1) for tile in tiles)
        if a > 0:
            keep = lane < 128 - 16 * a
            return jnp.where(keep, first, second), jnp.where(keep, second, first)
        keep = lane >= -16 * a
        return jnp.where(keep, first, second), jnp.where(keep, second, first)

    def weights(which, a, tile):
        start = 480 + 32 * which + 5 * a
        rows = [taps_ref[start + b : start + b + 1, 128 * tile : 128 * tile + 128] for b in range(5)]
        cos1, cos2, sin1, sin2 = (taps_ref[544:576, 128 * n : 128 * n + 128] for n in range(4))
        real = rows[2] + (rows[3] + rows[1]) * cos1 + (rows[4] + rows[0]) * cos2
        imag = (rows[3] - rows[1]) * sin1 + (rows[4] - rows[0]) * sin2
        return real, imag

    for tile in range(2):
        parts = []
        for r in range(2):
            rows = slice(LAT * r, LAT * r + LAT)
            own = own_ref[rows, 128 * tile : 128 * tile + 128]
            below, above = below_ref[rows], above_ref[rows]
            if tile == 0:
                parts.append(extend(own, below, turn(above)))
            else:
                parts.append(extend(own, turn(below), above))
        for which in range(2):
            real, imag = [list(value) for value in parts]
            for a in range(-2, 3):
                w_r, w_i = weights(which, a + 2, tile)
                e_r, e_i = shifted(parts[0], a), shifted(parts[1], a)
                for n in range(2):
                    real[n] = real[n] + (w_r * e_r[n] - w_i * e_i[n])
                    imag[n] = imag[n] + (w_r * e_i[n] + w_i * e_r[n])
            parts = [tuple(v * m for v, m in zip(value, masks)) for value in (real, imag)]
        for r in range(2):
            result = jnp.where(left, turn(parts[r][0]), turn(parts[r][1]))
            out_ref[LAT * r : LAT * r + LAT, 128 * tile : 128 * tile + 128] = result
    second = lane_slot(8) % 2 == 1
    value = extend(own_ref[0:LAT, 256:], turn(below_ref[2 * LAT :]), turn(above_ref[2 * LAT :]))
    for which in range(2):
        total = list(value)
        swapped = [jnp.where(second, pltpu.roll(v, 8, 1), pltpu.roll(v, 120, 1)) for v in value]
        for a in range(-2, 3):
            w_r, w_i = weights(which, a + 2, 2)
            w_i = jnp.where(second, w_i, -w_i)
            e, f = shifted(value, a), shifted(swapped, a)
            for n in range(2):
                total[n] = total[n] + (w_r * e[n] + w_i * f[n])
        value = tuple(v * m for v, m in zip(total, masks))
    out_ref[0:LAT, 256:] = jnp.where(left, turn(value[0]), turn(value[1]))
    out_ref[LAT:, 256:] = jnp.zeros((LAT, 128), f32)


def channel_at(place_ref, local):
    turned = jnp.where(local >= 32, local - 32, local + 8)
    return place_ref[2] * SLICE + jnp.where(place_ref[1] == 1, turned, local)


def pick(a, b, dims):
    return lax.dot_general(a, b, (dims, ((), ())), precision=lax.Precision.HIGHEST, preferred_element_type=f32)


def taps_kernel(place_ref, first_ref, second_ref, phase_ref, local_ref, gain_ref, wave_ref, taps_ref, up_ref, down_ref):
    gain = gain_ref[...]
    gain = jnp.where(place_ref[1] == 1, jnp.concatenate([gain[8:], gain[:8]], axis=0), gain)
    base = 10 * SLICE
    taps_ref[base : base + SLICE, :MODES] = gain
    taps_ref[base + SLICE : base + 2 * SLICE, :MODES] = jnp.where(place_ref[0] == 0, 0.0, gain)
    left = lane_slot(64) == 0
    a, b = local_ref[:, :128], local_ref[:, 128:256]
    up_ref[: 2 * LAT] = jnp.where(left, pltpu.roll(a, 64, 1), b)
    down_ref[: 2 * LAT] = jnp.where(left, a, pltpu.roll(b, 64, 1))
    up_ref[2 * LAT :] = local_ref[:LAT, 256:]
    down_ref[2 * LAT :] = local_ref[:LAT, 256:]
    taps_ref[544:576, :512] = wave_ref[...]
    south = jnp.where(place_ref[0] == 0, 0.0, 1.0)
    north = jnp.where(place_ref[0] == LAT - 1, 0.0, 1.0)
    row = lax.broadcasted_iota(jnp.int32, (8, 128), 0)
    edges = jnp.where(row == 0, jnp.where(left, south, 1.0), jnp.where(left, 1.0, north))
    taps_ref[576:584, :128] = edges
    shape = (CHANNELS, 384)
    at = lax.broadcasted_iota(jnp.int32, shape, 1)
    tail = at % 8 + 32
    at = jnp.where(at >= 256, tail, at // 128 * 16 + at % 16)
    chosen = (lax.broadcasted_iota(jnp.int32, shape, 0) == channel_at(place_ref, at)).astype(f32)
    taps_ref[480:505, :384] = pick(first_ref[...], chosen, ((1,), (0,)))
    taps_ref[512:537, :384] = pick(second_ref[...], chosen, ((1,), (0,)))
    shape = (SLICE, CHANNELS)
    wanted = channel_at(place_ref, lax.broadcasted_iota(jnp.int32, shape, 0))
    chosen = (lax.broadcasted_iota(jnp.int32, shape, 1) == wanted).astype(f32)
    rows = [pick(chosen, ref[...], ((1,), (1,))) for ref in (first_ref, second_ref)]
    for tile in range(5):
        phase = phase_ref[:, 4 * tile : 4 * tile + 1]
        for n in range(1, 4):
            column = phase_ref[:, 4 * tile + n : 4 * tile + n + 1]
            phase = jnp.where(lane_slot(LAT) >= n, column, phase)
        for which in range(2):
            for a in range(5):
                total = rows[which][:, 5 * a : 5 * a + 1] * phase[0:1]
                for b in range(1, 5):
                    total = total + rows[which][:, 5 * a + b : 5 * a + b + 1] * phase[b : b + 1]
                base = (5 * which + a) * SLICE
                taps_ref[base : base + SLICE, 128 * tile : 128 * tile + 128] = total


def legendre_kernel(owner_ref, angle_ref, seed_ref, high_ref, low_ref, left_ref, right_ref):
    slot = lax.broadcasted_iota(jnp.int32, (8, 256), 0)
    order_at = jnp.where(slot < OWN, owner_ref[0] * OWN + slot, 2 * MODES)
    order = order_at.astype(f32)
    degree = lax.broadcasted_iota(jnp.int32, (8, 256), 1).astype(f32)
    square, below = degree * degree, (degree - 1.0) * (degree - 1.0)
    upper = jnp.sqrt(
        jnp.maximum(4.0 * square - 1.0, 1.0) / jnp.maximum(square - order * order, 1.0)
    )
    lower = jnp.sqrt(
        jnp.maximum(below - order * order, 0.0) / jnp.maximum(4.0 * below - 1.0, 1.0)
    )
    product = upper * lower
    cosine = jnp.broadcast_to(angle_ref[0:1, :], (8, 256))
    diagonal = jnp.exp(seed_ref[:, 0:1] + order * angle_ref[1:2, :])
    previous = jnp.zeros((8, 256), f32)
    earlier = previous
    for l in range(MODES):
        current = jnp.where(
            order_at == l,
            diagonal,
            (upper[:, l : l + 1] * cosine) * previous - product[:, l : l + 1] * earlier,
        )
        left_ref[8 * l : 8 * l + 8] = current[:, :128]
        right_ref[8 * l : 8 * l + 8] = current[:, 128:]
        previous, earlier = current, previous
    for k in range(OWN):
        for part, source in enumerate((left_ref, right_ref)):
            high, low = split(source[pl.ds(k, MODES, stride=8), :])
            high_ref[k, :, 128 * part : 128 * part + 128] = high
            low_ref[k, :, 128 * part : 128 * part + 128] = low

def spectral_kernel(in_ref, high_ref, low_ref, taps_ref, angle_ref, out_ref, u_ref, v_ref, f_ref):
    lane = lax.broadcasted_iota(jnp.int32, (1, 128), 1) % LAT

    def fill_edges(ref):
        for part in range(2):
            for group in range(2):
                for e in (0, 1):
                    block = pltpu.roll(ref[part, group, 2 + e], 127, 1)
                    ref[part, group, 10 + e] = jnp.where(lane == LAT - 1, 0.0, block)
                    block = pltpu.roll(ref[part, group, 8 + e], 1, 1)
                    ref[part, group, e] = jnp.where(lane == 0, 0.0, block)

    def stencil(ref, which, store):
        for group in range(2):
            for tile in range(5):
                rows = slice(8 * tile, 8 * tile + 8)
                taps = []
                for a in range(5):
                    base = (which * 5 + a) * SLICE + 8 * tile
                    taps.append(
                        [
                            taps_ref[base : base + 8, 128 * column : 128 * column + 128]
                            for column in FACTOR_TILES[group]
                        ]
                    )
                real = [ref[0, group, e, rows] for e in range(12)]
                imag = [ref[1, group, e, rows] for e in range(12)]
                for e in range(ROWS):
                    total_r, total_i = real[e + 2], imag[e + 2]
                    for a in range(5):
                        r_tap, s_tap, i_tap = taps[a]
                        total_r = total_r + (r_tap * real[e + a] - i_tap * imag[e + a])
                        total_i = total_i + (s_tap * imag[e + a] + i_tap * real[e + a])
                    store(group, rows, e, total_r, total_i)

    def rows_of(start, count):
        pieces = [in_ref[pl.ds(start + n, LAT, stride=LAT_CHUNK), :] for n in range(count)]
        if count < 4:
            pieces.append(jnp.zeros((LAT * (4 - count), 128), f32))
        return jnp.concatenate(pieces, axis=0).T

    for group in range(2):
        count = min(4, OWN - 4 * group)
        for tile in range(2):
            for part in range(2):
                block = rows_of(OWN * (2 * tile + part) + 4 * group, count)
                for e in range(ROWS):
                    u_ref[part, group, 2 + e, 16 * tile : 16 * tile + 16] = block[16 * e : 16 * e + 16]
        block = rows_of(4 * OWN + 4 * group, count)
        for e in range(ROWS):
            for part in range(2):
                start = 16 * e + 8 * part
                u_ref[part, group, 2 + e, 32:40] = block[start : start + 8]
    fill_edges(u_ref)

    def keep_first(group, rows, e, total_r, total_i):
        v_ref[0, group, 2 + e, rows] = total_r
        v_ref[1, group, 2 + e, rows] = total_i

    stencil(u_ref, 0, keep_first)

    weight = angle_ref[2:3, :]
    for part in range(2):
        for group in range(2):
            halves = [
                swap_blocks([v_ref[part, group, 2 + 4 * j + e] for e in range(4)], 32) for j in range(2)
            ]
            for n in range(4):
                if 4 * group + n < OWN:
                    f_ref[4 * group + n, SLICE * part : SLICE * part + SLICE] = (
                        jnp.concatenate([halves[0][n], halves[1][n]], axis=1) * weight
                    )
    gain, masked = (taps_ref[SLICE * n : SLICE * n + SLICE, :MODES] for n in (10, 11))
    for k in range(OWN):
        table = (high_ref[k], low_ref[k])
        spectrum = dot3(split(f_ref[k]), table, ((1,), (1,)))
        second = masked if k == 0 else gain
        f_ref[k] = dot3(split(spectrum * jnp.concatenate([gain, second], axis=0)), table)
    for part in range(2):
        for group in range(2):
            rows = slice(SLICE * part, SLICE * part + SLICE)
            for j in range(2):
                values = [
                    f_ref[4 * group + n, rows, 128 * j : 128 * j + 128]
                    if 4 * group + n < OWN
                    else jnp.zeros((SLICE, 128), f32)
                    for n in range(4)
                ]
                for e, value in enumerate(swap_blocks(values, 32)):
                    v_ref[part, group, 2 + 4 * j + e] = v_ref[part, group, 2 + 4 * j + e] + value
    fill_edges(v_ref)

    def keep_second(group, rows, e, total_r, total_i):
        u_ref[0, group, 2 + e, rows] = total_r
        u_ref[1, group, 2 + e, rows] = total_i

    stencil(v_ref, 1, keep_second)

    def give(start, count, pieces):
        block = jnp.concatenate(pieces, axis=0).T
        for n in range(count):
            out_ref[pl.ds(start + n, LAT, stride=LAT_CHUNK), :] = block[LAT * n : LAT * n + LAT]

    for group in range(2):
        count = min(4, OWN - 4 * group)
        for tile in range(2):
            for part in range(2):
                give(
                    OWN * (2 * tile + part) + 4 * group,
                    count,
                    [u_ref[part, group, 2 + e, 16 * tile : 16 * tile + 16] for e in range(ROWS)],
                )
        give(
            4 * OWN + 4 * group,
            count,
            [u_ref[part, group, 2 + e, 32:40] for e in range(ROWS) for part in range(2)],
        )


def inverse_kernel(in_ref, local_ref, high_ref, low_ref, out_ref):
    totals = []
    for part in range(2):
        columns = []
        for tile, start in enumerate((OWN * part, OWN * (2 + part), 4 * OWN)):
            pieces = [in_ref[pl.ds(start + k, LAT, stride=LAT_CHUNK), :] for k in range(OWN)]
            row = LAT * part if tile < 2 else 0
            pieces.append(local_ref[row : row + LAT, 128 * tile : 128 * tile + 128])
            columns.append(jnp.concatenate(pieces + [jnp.zeros((LAT, 128), f32)], axis=0))
        x = split(jnp.concatenate(columns, axis=1))
        totals.append(dot3((high_ref[part], low_ref[part]), x))
    both = totals[0][:, :256] + totals[1][:, :256]
    g0, g1 = totals[0][:, 256:], totals[1][:, 256:]
    first = lane_slot(8) % 2 == 0
    last = jnp.where(
        first,
        g0[:256] + pltpu.roll(g1[:256], 120, 1),
        pltpu.roll(g0[256:], 8, 1) + g1[256:],
    )
    for q in range(LON):
        base = LON_CHUNK * q
        for tile in range(2):
            for half in range(2):
                row = 256 * half + 16 * q
                start = base + 28 * tile + 14 * half
                out_ref[start : start + 14] = both[row : row + 14, 128 * tile : 128 * tile + 128]
        out_ref[base + 56 : base + 70] = last[16 * q : 16 * q + 14]


def mlp_kernel(in_ref, gain_ref, up_ref, down_ref, out_hbm, x_ref, y_ref, sent):
    first = lane_slot(8) % 2 == 0
    for j in range(5):
        blocks = []
        for b in range(8):
            pair, place = divmod(8 * j + b, 5)
            even, odd = 2 * pair * LON_CHUNK, (2 * pair + 1) * LON_CHUNK
            if place == 2:
                e, o = in_ref[even + 56 : even + 70], in_ref[odd + 56 : odd + 70]
                top = jnp.where(first, e, pltpu.roll(o, 8, 1))
                bottom = jnp.where(first, pltpu.roll(e, 120, 1), o)
                blocks.append(jnp.concatenate([top, bottom], axis=0))
            else:
                base = (even, even + 28, None, odd, odd + 28)[place]
                blocks.append(in_ref[base : base + 28])
        for i, value in enumerate(swap_blocks(blocks, 16)):
            x_ref[:, i, 128 * j : 128 * j + 128] = value
    x = x_ref[...].reshape(COLS * ROWS, CHANNELS)
    average = jnp.mean(x, axis=-1, keepdims=True)
    centred = x - average
    spread = jnp.mean(centred * centred, axis=-1, keepdims=True)
    normed = (centred * lax.rsqrt(spread + 1e-05) * gain_ref[...].reshape(1, CHANNELS)).astype(bf16)
    active = []
    for n in range(5):
        hidden = dot(normed, up_ref[:, 256 * n : 256 * n + 256])
        active.append(jax.nn.gelu(hidden, approximate=True).astype(bf16))
    active = jnp.concatenate(active, axis=1)
    stores = []
    for n, (start, width) in enumerate(((0, 256), (256, 256), (512, 128))):
        lanes = pl.ds(start, width)
        total = x[:, start : start + width] + dot(active, down_ref[:, start : start + width])
        y_ref[:, :, start : start + width] = total.reshape(COLS, ROWS, width)
        stores.append(pltpu.make_async_copy(y_ref.at[:, :, lanes], out_hbm.at[:, :, lanes], sent.at[n]))
        stores[n].start()
    for store in stores:
        store.wait()


def vmem(count):
    return [pl.BlockSpec(memory_space=pltpu.VMEM)] * count


def run(kernel, shape, *operands, scratch=(), cost=(0, 0), grant=24, far=0, out=pltpu.VMEM):
    return pl.pallas_call(
        kernel,
        out_shape=jax.ShapeDtypeStruct(shape, f32),
        in_specs=vmem(len(operands) - far) + [pl.BlockSpec(memory_space=pltpu.HBM)] * far,
        out_specs=pl.BlockSpec(memory_space=out),
        scratch_shapes=list(scratch),
        compiler_params=pltpu.CompilerParams(vmem_limit_bytes=grant << 20),
        cost_estimate=pl.CostEstimate(flops=cost[0], bytes_accessed=cost[1], transcendentals=0),
    )(*operands)


def legendre(*operands):
    table = jax.ShapeDtypeStruct((OWN, MODES, NLAT), bf16)
    return pl.pallas_call(
        legendre_kernel,
        out_shape=(table, table),
        in_specs=[pl.BlockSpec(memory_space=pltpu.SMEM)] + vmem(2),
        out_specs=vmem(2),
        scratch_shapes=[pltpu.VMEM((8 * MODES, 128), f32)] * 2,
        compiler_params=pltpu.CompilerParams(vmem_limit_bytes=16 << 20),
        cost_estimate=pl.CostEstimate(flops=10**7, bytes_accessed=10**7, transcendentals=0),
    )(*operands)


def wave_np():
    angle = 2.0 * np.pi * (MODES + np.arange(LAT)) / NLON
    waves = [np.cos(angle), np.cos(2.0 * angle), np.sin(angle), np.sin(2.0 * angle)]
    return np.repeat(np.stack(waves, axis=1), 128, axis=1).astype(np.float32)


def exchange(array, axis, count):
    rows = array.shape[0] // count
    shape = (count, rows, 128) if rows % 8 == 0 else (count, 1, rows * 128)
    moved = lax.all_to_all(array.reshape(shape), axis, split_axis=0, concat_axis=0, tiled=True)
    return moved.reshape(array.shape)


def per_device(latent, conv_first, conv_second, filter_gains, norm_gain, up_weight, down_weight):
    band = lax.axis_index("lat")
    sector = lax.axis_index("lon")
    odd = sector % 2 == 1
    forward, inverse = fourier_np()
    forward, inverse = split_np(forward), split_np(inverse)
    angles = jnp.asarray(latitude_np())

    packed = run(
        pack_kernel,
        (LON * LON_CHUNK, 128),
        latent.transpose(1, 0, 2),
        scratch=[
            pltpu.VMEM((COLS, ROWS, CHANNELS), f32),
            pltpu.SemaphoreType.DMA((20,)),
        ],
        far=1,
        grant=53,
    )
    circles = exchange(packed, "lon", LON)

    shapes = ((LAT * LAT_CHUNK, 128), (2 * LAT, 384))
    coeffs, local = pl.pallas_call(
        forward_kernel,
        out_shape=tuple(jax.ShapeDtypeStruct(shape, f32) for shape in shapes),
        in_specs=vmem(3),
        out_specs=vmem(2),
        compiler_params=pltpu.CompilerParams(vmem_limit_bytes=24 << 20),
    )(circles, *map(jnp.asarray, forward))
    orders = exchange(coeffs, "lat", LAT)
    local, conv_first, conv_second, band = lax.optimization_barrier(
        (local, conv_first, conv_second, band)
    )
    seeds = lax.dynamic_index_in_dim(jnp.asarray(seed_np()), band, 0, False)
    owner = band.astype(jnp.int32).reshape(1)
    high, low = legendre(owner, angles, seeds)
    phases = lax.dynamic_index_in_dim(jnp.asarray(phase_np()), band, 0, False)
    place = jnp.stack([band, odd, sector]).astype(jnp.int32)
    shapes = ((584, 640), (3 * LAT, 128), (3 * LAT, 128))
    taps, up, down = pl.pallas_call(
        taps_kernel,
        out_shape=tuple(jax.ShapeDtypeStruct(shape, f32) for shape in shapes),
        in_specs=[pl.BlockSpec(memory_space=pltpu.SMEM)] + vmem(6),
        out_specs=vmem(3),
        compiler_params=pltpu.CompilerParams(vmem_limit_bytes=16 << 20),
        cost_estimate=pl.CostEstimate(flops=10**7, bytes_accessed=10**7, transcendentals=0),
    )(place, conv_first, conv_second, phases, local, filter_gains.T, jnp.asarray(wave_np()))
    rising = [(n, n + 1) for n in range(LAT - 1)]
    below = lax.ppermute(up, "lat", rising)
    above = lax.ppermute(down, "lat", [(target, source) for source, target in rising])
    stay = pl.pallas_call(
        local_kernel,
        out_shape=jax.ShapeDtypeStruct((2 * LAT, 384), f32),
        in_specs=vmem(4),
        out_specs=vmem(1)[0],
        compiler_params=pltpu.CompilerParams(vmem_limit_bytes=16 << 20),
        cost_estimate=pl.CostEstimate(flops=10**7, bytes_accessed=10**6, transcendentals=0),
    )(local, below, above, taps)
    orders, taps, high, low = lax.optimization_barrier((orders, taps, high, low))
    state = pltpu.VMEM((2, 2, 12, SLICE, 128), f32)
    third = run(
        spectral_kernel,
        (LAT * LAT_CHUNK, 128),
        orders,
        high,
        low,
        taps,
        angles,
        scratch=[state, state, pltpu.VMEM((OWN, 2 * SLICE, NLAT), f32)],
    )
    returned = exchange(third, "lat", LAT)
    restored = run(inverse_kernel, (LON * LON_CHUNK, 128), returned, stay, *map(jnp.asarray, inverse))
    arrived = exchange(restored, "lon", LON)
    result = run(
        mlp_kernel,
        (COLS, ROWS, CHANNELS),
        arrived,
        norm_gain,
        up_weight,
        down_weight,
        scratch=[
            pltpu.VMEM((COLS, ROWS, CHANNELS), f32),
            pltpu.VMEM((COLS, ROWS, CHANNELS), f32),
            pltpu.SemaphoreType.DMA((3,)),
        ],
        out=pltpu.HBM,
    )
    return result.transpose(1, 0, 2)


def solution(mesh):
    return jax.shard_map(
        per_device,
        mesh=mesh,
        in_specs=(P("lat", "lon", None), P(), P(), P(None, "lon"), P(), P(), P()),
        out_specs=P("lat", "lon", None),
        check_vma=False,
    )
```
